32 devices in a mesh: dp: 2 (over y), fsdp: 16 (over z, x, core).
Axes of the slice: x: 2, y: 2, z: 4, core: 2. Of those that a mesh axis runs over, the one named last changes fastest.
Arguments:
- hidden_in: bfloat16 [512, 128, 768], P(('dp', 'fsdp')), may hold values from -6 to 6
- segment_ids: int32 [512, 128], P(('dp', 'fsdp')), may hold values from 0 to 3, never falling along the last dimension, each value on 1 to 64 neighbouring positions
- pooled_grad: float32 [512, 4, 768], P(('dp', 'fsdp')), may hold values from -192 to 192
- qkv_weight: bfloat16 [768, 2304], P('fsdp'), may hold values from -0.21875 to 0.21875
- qv_bias: bfloat16 [1536], P('fsdp'), may hold values from -3 to 3
- out_weight: bfloat16 [768, 768], P('fsdp'), may hold values from -1.25 to 1.25
- out_bias: bfloat16 [768], P('fsdp'), may hold values from -3 to 3
- first_gain: bfloat16 [768], P('fsdp'), may hold values from 0.5 to 1.5
- first_shift: bfloat16 [768], P('fsdp'), may hold values from -3 to 3
- up_weight: bfloat16 [768, 3072], P('fsdp'), may hold values from -0.21875 to 0.21875
- up_bias: bfloat16 [3072], P('fsdp'), may hold values from -3 to 3
- down_weight: bfloat16 [3072, 768], P('fsdp'), may hold values from -0.109375 to 0.109375
- down_bias: bfloat16 [768], P('fsdp'), may hold values from -3 to 3
- second_gain: bfloat16 [768], P('fsdp'), may hold values from 0.5 to 1.5
- second_shift: bfloat16 [768], P('fsdp'), may hold values from -3 to 3
Outputs:
- pooled: float32 [512, 4, 768], P(('dp', 'fsdp'))
- grad_input: float32 [512, 128, 768], P(('dp', 'fsdp'))
- grad_qkv_weight: float32 [768, 2304], P('fsdp')
- grad_qv_bias: float32 [1536], P('fsdp')
- grad_out_weight: float32 [768, 768], P('fsdp')
- grad_out_bias: float32 [768], P('fsdp')
- grad_first_gain: float32 [768], P('fsdp')
- grad_first_shift: float32 [768], P('fsdp')
- grad_up_weight: float32 [768, 3072], P('fsdp')
- grad_up_bias: float32 [3072], P('fsdp')
- grad_down_weight: float32 [3072, 768], P('fsdp')
- grad_down_bias: float32 [768], P('fsdp')
- grad_second_gain: float32 [768], P('fsdp')
- grad_second_shift: float32 [768], P('fsdp')
The draws below stay inside these ranges and needn't reach their ends.
Inputs may be any that keep to these rules, and one draw needn't show every extreme that they name: `segment_ids`: within each row of 128 positions the ids never fall, every id occurs, and the longest segment has exactly 64 positions.
All inputs are finite; a program needn't handle non-finite values.
Results may differ from the reference program's by a relative error of at most 0.0065.
Values may be sent and summed in bfloat16 or wider, within the bound.
No kernel may reach another device: no remote copies, remote signals or barrier semaphores. Data moves between devices by JAX's collectives and lax.ppermute only.
A program may use at most 256 MiB of HBM per device.

```python
import math
import jax
import jax.numpy as jnp
import numpy as np
from jax import lax

D = 768
HEAD = 64
FF = 3072
ROW = 128
SEGS = 4
SEG_MOST = 64
NROWS = 512


def block_levels(own_key, dims, pieces, smallest, top_value):
    def one(axis_at, shards_of):
        draws = jax.random.uniform(jax.random.fold_in(jax.random.fold_in(own_key, 6), axis_at), (shards_of,), jnp.float32, smallest / len(pieces), top_value / len(pieces))
        return jnp.repeat(jnp.exp(draws), dims[axis_at] // shards_of).reshape((-1,) + (1,) * (len(dims) - axis_at - 1))

    loudness = one(*pieces[0])
    for cut in pieces[1:]:
        loudness = loudness * one(*cut)
    return loudness


def profile(amount, total, limit, lean):
    weights = [(1 << 20) // math.isqrt(standing ** lean) + 1 for standing in range(2, amount + 1)]
    spare, holding = total - limit - (amount - 1), [1] * (amount - 1)
    while spare > 0:
        movable = [i for i in range(amount - 1) if holding[i] < limit]
        mass, budget = sum([weights[i] for i in movable]), spare
        for i in movable:
            more = min(limit - holding[i], max(1, budget * weights[i] // mass), spare)
            holding[i] = holding[i] + more
            spare = spare - more
    return np.array([limit] + holding)


def uneven_parts(rng, count, total, most, slope):
    if count == 2:
        one = jax.random.randint(rng, (), max(1, total - most), min(most, total - 1) + 1)
        return jnp.stack([one, total - one])
    sizes = jnp.asarray(profile(count, total, most, slope), jnp.int32)
    twos = (count - 1) // 2
    source_of, receiver = sizes[1:1 + 2 * twos:2], sizes[2:2 + 2 * twos:2]
    room = jnp.minimum(source_of - 1, most - receiver)
    moved = jax.random.randint(jax.random.fold_in(rng, 1), (twos,), 0, 1 << 20) % (room + 1)
    sizes = sizes.at[1:1 + 2 * twos:2].set(source_of - moved).at[2:2 + 2 * twos:2].set(receiver + moved)
    return sizes[jax.random.permutation(jax.random.fold_in(rng, 2), count)]


def noise(own_key, extent, spread, bound, cuts=(), held_as=jnp.bfloat16):
    result = spread * jax.random.normal(own_key, extent, jnp.float32)
    if cuts:
        result = result * block_levels(own_key, extent, cuts, -0.22, 0.18)
    return jnp.clip(result, -bound, bound).astype(held_as)


def setup_inputs(seed: int = 0) -> dict:
    arg_keys = jax.random.split(jax.random.key(seed), 16)
    return {
        "hidden_in": noise(arg_keys[0], (NROWS, ROW, D), 1.0, 6.0, ((0, 32),)),
        "segment_ids": jax.vmap(lambda own: jnp.searchsorted(jnp.cumsum(uneven_parts(own, SEGS, ROW, SEG_MOST, 0)), jnp.arange(ROW), side="right"))(jax.random.split(arg_keys[1], NROWS)).reshape((NROWS, ROW)).astype(jnp.int32),
        "pooled_grad": noise(arg_keys[2], (NROWS, SEGS, D), (ROW // SEGS), 192.0, ((0, 32),), jnp.float32),
        "qkv_weight": noise(arg_keys[3], (D, 3 * D), D ** -0.5, 0.21875, ((0, 16),)),
        "qv_bias": noise(arg_keys[4], (2 * D,), 0.5, 3.0, ((0, 16),)),
        "out_weight": noise(arg_keys[5], (D, D), (D * SEGS // ROW) ** -0.5, 1.25, ((0, 16),)),
        "out_bias": noise(arg_keys[6], (D,), 0.5, 3.0, ((0, 16),)),
        "first_gain": jnp.clip(1.0 + 0.1 * jax.random.normal(arg_keys[7], (D,), jnp.float32), 0.5, 1.5).astype(jnp.bfloat16),
        "first_shift": noise(arg_keys[8], (D,), 0.5, 3.0, ((0, 16),)),
        "up_weight": noise(arg_keys[9], (D, FF), D ** -0.5, 0.21875, ((0, 16),)),
        "up_bias": noise(arg_keys[10], (FF,), 0.5, 3.0, ((0, 16),)),
        "down_weight": noise(arg_keys[11], (FF, D), FF ** -0.5, 0.109375, ((0, 16),)),
        "down_bias": noise(arg_keys[12], (D,), 0.5, 3.0, ((0, 16),)),
        "second_gain": jnp.clip(1.0 + 0.1 * jax.random.normal(arg_keys[13], (D,), jnp.float32), 0.5, 1.5).astype(jnp.bfloat16),
        "second_shift": noise(arg_keys[14], (D,), 0.5, 3.0, ((0, 16),)),
    }


@jax.custom_vjp
def low(v):
    return lax.optimization_barrier(v.astype(jnp.bfloat16)).astype(jnp.float32)

@jax.custom_vjp
def low_back(v):
    return v

def low_keep(v):
    return (low(v), None)

def low_pass(kept, grad):
    return (grad,)

def back_keep(v):
    return (v, None)

def back_low(kept, grad):
    return (low(grad),)
low.defvjp(low_keep, low_pass)
low_back.defvjp(back_keep, back_low)
EPSILON = 1e-12
HIGHEST = lax.Precision.HIGHEST

def norm_rows(residual, norm_gain, norm_shift):
    average = lax.optimization_barrier(jnp.mean(residual, axis=-1, keepdims=True))
    centred = residual - average
    variance = lax.optimization_barrier(jnp.mean(centred * centred, axis=-1, keepdims=True))
    return centred * lax.rsqrt(variance + EPSILON) * norm_gain + norm_shift

def forward_block(weight_set, block_in, block_ids):
    qkv_weight, qv_bias, out_weight, out_bias, first_gain, first_shift, up_weight, up_bias, down_weight, down_bias, second_gain, second_shift = weight_set
    row_count, length, model_width = block_in.shape
    head_count = model_width // HEAD
    token_count = row_count * length
    flat_rows = block_in.reshape(token_count, model_width)
    zero_bias = jnp.zeros((model_width,), jnp.float32)
    joined_bias = jnp.concatenate([qv_bias[:model_width], zero_bias, qv_bias[model_width:]])
    qkv_rows = jnp.dot(flat_rows, qkv_weight, precision=HIGHEST) + joined_bias
    qkv_rows = low(low_back(qkv_rows)).reshape(row_count, length, 3, head_count, HEAD)
    queries = qkv_rows[:, :, 0]
    key_rows = qkv_rows[:, :, 1]
    value_rows = qkv_rows[:, :, 2]
    scores = jnp.einsum('bqhd,bkhd->bhqk', queries, key_rows, precision=HIGHEST) * (1.0 / HEAD ** 0.5)
    scores = low_back(scores)
    same_segment = block_ids[:, :, None] == block_ids[:, None, :]
    masked = jnp.where(same_segment[:, None], scores, -1e+30)
    attention = low(jax.nn.softmax(masked, axis=-1))
    context = jnp.einsum('bhqk,bkhd->bqhd', attention, value_rows, precision=HIGHEST)
    context = low(low_back(context)).reshape(token_count, model_width)
    attended = low_back(jnp.dot(context, out_weight, precision=HIGHEST) + out_bias)
    normed = norm_rows(flat_rows + attended, first_gain, first_shift)
    hidden_pre = low_back(jnp.dot(low(normed), up_weight, precision=HIGHEST) + up_bias)
    active = low(jax.nn.gelu(hidden_pre, approximate=False))
    branch = low_back(jnp.dot(active, down_weight, precision=HIGHEST) + down_bias)
    final_rows = norm_rows(normed + branch, second_gain, second_shift).reshape(row_count, length, model_width)
    member = (block_ids[:, :, None] == jnp.arange(SEGS, dtype=jnp.int32)[None, None, :]).astype(jnp.float32)
    population = lax.optimization_barrier(jnp.sum(member, axis=1))
    pooled = jnp.einsum('bts,btd->bsd', member, final_rows, precision=HIGHEST)
    return pooled / population[:, :, None]

def reference(hidden_in, segment_ids, pooled_grad, qkv_weight, qv_bias, out_weight, out_bias, first_gain, first_shift, up_weight, up_bias, down_weight, down_bias, second_gain, second_shift):
    weight_set = tuple((weight_array.astype(jnp.float32) for weight_array in (qkv_weight, qv_bias, out_weight, out_bias, first_gain, first_shift, up_weight, up_bias, down_weight, down_bias, second_gain, second_shift)))
    total_rows = hidden_in.shape[0]
    block_rows = 32 if total_rows % 32 == 0 else total_rows
    block_count = total_rows // block_rows
    inputs_all = hidden_in.astype(jnp.float32).reshape(block_count, block_rows, ROW, D)
    block_ids_all = segment_ids.reshape(block_count, block_rows, ROW)
    cotangent_all = pooled_grad.reshape(block_count, block_rows, SEGS, D)

    def visit_block(running, portion):
        block_in, block_ids, block_cot = portion

        def forward_of(weight_values, layer_in):
            return forward_block(weight_values, layer_in, block_ids)
        pooled, backward = jax.vjp(forward_of, weight_set, block_in)
        weight_grads, input_grad = backward(block_cot)
        summed = tuple((earlier + addend for earlier, addend in zip(running, weight_grads)))
        return (summed, (pooled, input_grad))
    zeros_start = tuple((jnp.zeros_like(weight_array) for weight_array in weight_set))
    totals, (pooled, input_grad) = lax.scan(visit_block, zeros_start, (inputs_all, block_ids_all, cotangent_all))
    pooled = pooled.reshape(total_rows, SEGS, D)
    input_grad = input_grad.reshape(total_rows, ROW, D)
    return (pooled, input_grad, totals[0], totals[1], totals[2], totals[3], totals[4], totals[5], totals[6], totals[7], totals[8], totals[9], totals[10], totals[11])
```

```python
import functools
import math

import jax
import jax.numpy as jnp
from jax import lax
from jax.experimental import pallas as pl
from jax.experimental.pallas import tpu as pltpu
from jax.sharding import PartitionSpec as P

HEAD = 64
PAIR = 2 * HEAD
EPSILON = 1e-12
F32 = jnp.float32
BF16 = jnp.bfloat16
VMEM_LIMIT = 60000 * 1024

ERFC_SLOPE = 0.33
ERFC_TERMS = (
    0.18635788923911423,
    0.18295457713165508,
    0.20123280917878972,
    0.04718951182123742,
    0.408562666534809,
    -0.35122255207376696,
    0.46028245445329624,
    -0.1353573694779288,
)


def product(left, right):
    return jnp.dot(left, right, preferred_element_type=F32)


def times_transpose(left, right):
    return lax.dot_general(left, right, (((1,), (1,)), ((), ())), preferred_element_type=F32)


def transpose_times(left, right):
    return lax.dot_general(left, right, (((0,), (0,)), ((), ())), preferred_element_type=F32)


def normal_parts(u):
    density = jnp.exp(-0.5 * u * u)
    t = 1.0 / (1.0 + (ERFC_SLOPE / math.sqrt(2.0)) * jnp.abs(u))
    poly = jnp.full_like(t, 0.5 * ERFC_TERMS[-1])
    for term in ERFC_TERMS[-2::-1]:
        poly = poly * t + 0.5 * term
    tail = poly * t * density
    cumulative = jnp.where(u >= 0.0, 1.0 - tail, tail)
    return cumulative, u * (density * (1.0 / math.sqrt(2.0 * math.pi)))


def normalise(rows):
    average = jnp.mean(rows, axis=-1, keepdims=True)
    centred = rows - average
    variance = jnp.mean(centred * centred, axis=-1, keepdims=True)
    rstd = lax.rsqrt(variance + EPSILON)
    return centred * rstd, rstd


def normalise_back(grad, gain, xhat, rstd):
    e = grad * gain
    mean_e = jnp.mean(e, axis=-1, keepdims=True)
    mean_ex = jnp.mean(e * xhat, axis=-1, keepdims=True)
    return rstd * (e - mean_e - xhat * mean_ex)


def fold(values):
    rows, width = values.shape
    return jnp.sum(values.reshape(rows // 8, 8, width), axis=0)


def lane_halves():
    lane = lax.broadcasted_iota(jnp.int32, (1, PAIR), 1)
    return (lane < HEAD).astype(BF16), (lane >= HEAD).astype(BF16)


def split_heads(block, low_half, high_half):
    return jnp.concatenate([block * low_half, block * high_half], axis=0)


def segment_grid(seg_ref, row, length):
    ids = seg_ref[pl.ds(row, 1), :].astype(F32)
    along_lanes = jnp.broadcast_to(ids, (length, length))
    return along_lanes, along_lanes.T


def attention_kernel(length, width, x_ref, seg_ref, w_ref, bias_ref, qkv_ref, ctx_ref):
    tokens = x_ref.shape[0]
    step = pl.program_id(0)
    x = x_ref[...]
    for part in range(3):
        cols = pl.ds(part * width, width)
        qkv_ref[:, cols] = (product(x, w_ref[:, cols]) + bias_ref[:, cols]).astype(BF16)
    low_half, high_half = lane_halves()
    ones_low = jnp.broadcast_to(low_half, (length, PAIR))
    ones_high = jnp.broadcast_to(high_half, (length, PAIR))
    scale = HEAD**-0.5
    for local in range(tokens // length):
        rows = pl.ds(local * length, length)
        along_lanes, along_rows = segment_grid(seg_ref, step * (tokens // length) + local, length)
        same = along_lanes == along_rows
        for pair in range(width // PAIR):
            q = qkv_ref[rows, pl.ds(pair * PAIR, PAIR)] * BF16(scale)
            k = qkv_ref[rows, pl.ds(width + pair * PAIR, PAIR)]
            v = qkv_ref[rows, pl.ds(2 * width + pair * PAIR, PAIR)]
            scores = times_transpose(q, split_heads(k, low_half, high_half))
            parts = []
            for half in range(2):
                masked = jnp.where(same, scores[:, half * length : (half + 1) * length], -1e30)
                peak = jnp.max(masked, axis=-1, keepdims=True)
                parts.append(jnp.exp(masked - peak).astype(BF16))
            values = jnp.concatenate(
                [
                    split_heads(v, low_half, high_half),
                    jnp.concatenate([ones_low, ones_high], axis=0),
                ],
                axis=1,
            )
            both = product(jnp.concatenate(parts, axis=1), values)
            ctx_ref[rows, pl.ds(pair * PAIR, PAIR)] = (both[:, :PAIR] / both[:, PAIR:]).astype(BF16)


def attention_forward(x, seg, w, bias, rows_per_step=2):
    row_count, length = seg.shape
    tokens, width = x.shape
    block = rows_per_step * length
    return pl.pallas_call(
        functools.partial(attention_kernel, length, width),
        grid=(row_count // rows_per_step,),
        in_specs=[
            pl.BlockSpec((block, width), lambda i: (i, 0)),
            pl.BlockSpec((row_count, length), lambda i: (0, 0)),
            pl.BlockSpec((width, 3 * width), lambda i: (0, 0), pipeline_mode=pl.Buffered(1)),
            pl.BlockSpec((1, 3 * width), lambda i: (0, 0)),
        ],
        out_specs=[
            pl.BlockSpec((block, 3 * width), lambda i: (i, 0)),
            pl.BlockSpec((block, width), lambda i: (i, 0)),
        ],
        out_shape=[
            jax.ShapeDtypeStruct((tokens, 3 * width), BF16),
            jax.ShapeDtypeStruct((tokens, width), BF16),
        ],
        compiler_params=pltpu.CompilerParams(vmem_limit_bytes=VMEM_LIMIT),
        cost_estimate=pl.CostEstimate(
            flops=2 * tokens * width * 3 * width + 8 * tokens * length * width,
            bytes_accessed=tokens * width * 10 + 6 * width * width,
            transcendentals=tokens * length * (width // HEAD),
        ),
        name="attention_forward",
    )(x, seg, w, bias)


def feedforward_kernel(
    length,
    chunk,
    x_ref,
    ctx_ref,
    seg_ref,
    pooled_grad_ref,
    out_w_ref,
    up_w_ref,
    down_w_ref,
    vec_ref,
    up_bias_ref,
    pooled_ref,
    active_ref,
    hidden_ref,
    normed_ref,
    branch_ref,
    first_ref,
    attended_ref,
    context_ref,
    small_ref,
    up_small_ref,
    slope_ref,
):
    step = pl.program_id(0)
    tokens, width = x_ref.shape
    hidden = up_w_ref.shape[1]
    segments = pooled_grad_ref.shape[1]
    out_bias, gain_one, shift_one = vec_ref[0:1, :], vec_ref[1:2, :], vec_ref[2:3, :]
    down_bias, gain_two, shift_two = vec_ref[3:4, :], vec_ref[4:5, :], vec_ref[5:6, :]

    @pl.when(step == 0)
    def _():
        small_ref[...] = jnp.zeros_like(small_ref)
        up_small_ref[...] = jnp.zeros_like(up_small_ref)

    first_sum = x_ref[...].astype(F32) + product(ctx_ref[...], out_w_ref[...]) + out_bias
    xhat_one, rstd_one = normalise(first_sum)
    normed_one = xhat_one * gain_one + shift_one
    normed_low = normed_one.astype(BF16)
    normed_ref[...] = normed_low
    second_sum = normed_one + down_bias
    for start in range(0, hidden, chunk):
        cols = pl.ds(start, chunk)
        pre = product(normed_low, up_w_ref[:, cols]) + up_bias_ref[:, cols]
        cumulative, tilt = normal_parts(pre)
        active = (pre * cumulative).astype(BF16)
        slope_ref[:, cols] = cumulative + tilt
        active_ref[:, cols] = active
        second_sum = second_sum + product(active, down_w_ref[cols, :])
    xhat_two, rstd_two = normalise(second_sum)
    final = xhat_two * gain_two + shift_two
    final_high = final.astype(BF16)
    final_low = (final - final_high.astype(F32)).astype(BF16)
    token_parts = []
    for local in range(tokens // length):
        rows = slice(local * length, (local + 1) * length)
        along_lanes, along_rows = segment_grid(seg_ref, step * (tokens // length) + local, length)
        index = lax.broadcasted_iota(jnp.int32, (8, length), 0).astype(F32)
        member = (along_lanes[:8, :] == index).astype(F32)
        population = jnp.sum(member, axis=1, keepdims=True)
        member_low = member.astype(BF16)
        sums = product(member_low, final_high[rows]) + product(member_low, final_low[rows])
        pooled_ref[local] = sums[:segments] / population[:segments]
        share = pooled_grad_ref[local] / population[:segments]
        wide = jnp.concatenate([along_rows] * (width // length), axis=1)
        token = jnp.broadcast_to(share[segments - 1 : segments], (length, width))
        for s in range(segments - 2, -1, -1):
            token = jnp.where(wide == float(s), share[s : s + 1], token)
        token_parts.append(token)
    token_grad = jnp.concatenate(token_parts, axis=0)
    second_grad = normalise_back(token_grad, gain_two, xhat_two, rstd_two)
    branch = second_grad.astype(BF16)
    branch_ref[...] = branch
    small_ref[24:32, :] += fold(branch.astype(F32))
    small_ref[32:40, :] += fold(token_grad * xhat_two)
    small_ref[40:48, :] += fold(token_grad)
    normed_grad = second_grad
    for start in range(0, hidden, chunk):
        cols = pl.ds(start, chunk)
        grad = (times_transpose(branch, down_w_ref[cols, :]) * slope_ref[:, cols]).astype(BF16)
        hidden_ref[:, cols] = grad
        up_small_ref[:, cols] += fold(grad.astype(F32))
        normed_grad = normed_grad + times_transpose(grad, up_w_ref[:, cols])
    first_grad = normalise_back(normed_grad, gain_one, xhat_one, rstd_one)
    first_ref[...] = first_grad
    attended = first_grad.astype(BF16)
    attended_ref[...] = attended
    context_ref[...] = times_transpose(attended, out_w_ref[...]).astype(BF16)
    small_ref[0:8, :] += fold(attended.astype(F32))
    small_ref[8:16, :] += fold(normed_grad * xhat_one)
    small_ref[16:24, :] += fold(normed_grad)


def feedforward(x, ctx, seg, pooled_grad, out_w, up_w, down_w, vectors, up_bias, rows_per_step=2, chunk=768):
    row_count, length = seg.shape
    tokens, width = x.shape
    hidden = up_w.shape[1]
    segments = pooled_grad.shape[1]
    block = rows_per_step * length

    def tiled(columns):
        return pl.BlockSpec((block, columns), lambda i: (i, 0))

    def whole(shape):
        return pl.BlockSpec(shape, lambda i: (0,) * len(shape), pipeline_mode=pl.Buffered(1))

    def kept(shape):
        return pl.BlockSpec(shape, lambda i: (0,) * len(shape))

    def rows(columns, dtype):
        return jax.ShapeDtypeStruct((tokens, columns), dtype)

    return pl.pallas_call(
        functools.partial(feedforward_kernel, length, chunk),
        grid=(row_count // rows_per_step,),
        in_specs=[
            tiled(width),
            tiled(width),
            whole((row_count, length)),
            pl.BlockSpec((rows_per_step, segments, width), lambda i: (i, 0, 0)),
            whole((width, width)),
            whole((width, hidden)),
            whole((hidden, width)),
            whole((8, width)),
            whole((1, hidden)),
        ],
        out_specs=[
            pl.BlockSpec((rows_per_step, segments, width), lambda i: (i, 0, 0)),
            tiled(hidden),
            tiled(hidden),
            tiled(width),
            tiled(width),
            tiled(width),
            tiled(width),
            tiled(width),
            kept((48, width)),
            kept((8, hidden)),
        ],
        out_shape=[
            jax.ShapeDtypeStruct((row_count, segments, width), F32),
            rows(hidden, BF16),
            rows(hidden, BF16),
            rows(width, BF16),
            rows(width, BF16),
            rows(width, F32),
            rows(width, BF16),
            rows(width, BF16),
            jax.ShapeDtypeStruct((48, width), F32),
            jax.ShapeDtypeStruct((8, hidden), F32),
        ],
        scratch_shapes=[pltpu.VMEM((block, hidden), F32)],
        compiler_params=pltpu.CompilerParams(vmem_limit_bytes=VMEM_LIMIT),
        cost_estimate=pl.CostEstimate(
            flops=tokens * width * (4 * width + 8 * hidden),
            bytes_accessed=tokens * (width * 18 + hidden * 4) + 4 * width * hidden,
            transcendentals=2 * tokens * hidden,
        ),
        name="feedforward",
    )(x, ctx, seg, pooled_grad, out_w, up_w, down_w, vectors, up_bias)


def attention_back_kernel(length, width, qkv_ref, grad_ref, seg_ref, out_ref, small_ref):
    tokens = grad_ref.shape[0]
    step = pl.program_id(0)

    @pl.when(step == 0)
    def _():
        small_ref[...] = jnp.zeros_like(small_ref)

    low_half, high_half = lane_halves()
    scale = HEAD**-0.5
    for local in range(tokens // length):
        rows = pl.ds(local * length, length)
        along_lanes, along_rows = segment_grid(seg_ref, step * (tokens // length) + local, length)
        same = along_lanes == along_rows
        same = jnp.concatenate([same, same], axis=1)
        for pair in range(width // PAIR):
            at = (pl.ds(pair * PAIR, PAIR), pl.ds(width + pair * PAIR, PAIR), pl.ds(2 * width + pair * PAIR, PAIR))
            q = split_heads(qkv_ref[rows, at[0]] * BF16(scale), low_half, high_half)
            k = qkv_ref[rows, at[1]]
            v = qkv_ref[rows, at[2]]
            ctx_grad = split_heads(grad_ref[rows, at[0]], low_half, high_half)
            scores = jnp.where(same, times_transpose(k, q), -1e30)
            weights = jnp.exp(scores - jnp.max(scores, axis=0, keepdims=True))
            weights = weights * (1.0 / jnp.sum(weights, axis=0, keepdims=True))
            probs_grad = times_transpose(v, ctx_grad)
            inner = jnp.sum(weights * probs_grad, axis=0, keepdims=True)
            scores_grad = (weights * (probs_grad - inner)).astype(BF16)
            values_grad = product(weights.astype(BF16), ctx_grad).astype(BF16)
            keys_grad = product(scores_grad, q).astype(BF16)
            turned = jnp.concatenate([scores_grad[:, :length].T, scores_grad[:, length:].T], axis=1)
            queries_grad = product(turned, split_heads(k * BF16(scale), low_half, high_half)).astype(BF16)
            out_ref[rows, at[0]] = queries_grad
            out_ref[rows, at[1]] = keys_grad
            out_ref[rows, at[2]] = values_grad
            small_ref[:, at[0]] += fold(queries_grad.astype(F32))
            small_ref[:, at[1]] += fold(values_grad.astype(F32))


def attention_backward(qkv, ctx_grad, seg, rows_per_step=2):
    row_count, length = seg.shape
    tokens, width = ctx_grad.shape
    block = rows_per_step * length
    return pl.pallas_call(
        functools.partial(attention_back_kernel, length, width),
        grid=(row_count // rows_per_step,),
        in_specs=[
            pl.BlockSpec((block, 3 * width), lambda i: (i, 0)),
            pl.BlockSpec((block, width), lambda i: (i, 0)),
            pl.BlockSpec((row_count, length), lambda i: (0, 0)),
        ],
        out_specs=[
            pl.BlockSpec((block, 3 * width), lambda i: (i, 0)),
            pl.BlockSpec((8, 2 * width), lambda i: (0, 0)),
        ],
        out_shape=[
            jax.ShapeDtypeStruct((tokens, 3 * width), BF16),
            jax.ShapeDtypeStruct((8, 2 * width), F32),
        ],
        compiler_params=pltpu.CompilerParams(vmem_limit_bytes=VMEM_LIMIT),
        cost_estimate=pl.CostEstimate(
            flops=20 * tokens * length * width,
            bytes_accessed=tokens * width * 14,
            transcendentals=tokens * length * (width // HEAD),
        ),
        name="attention_backward",
    )(qkv, ctx_grad, seg)


def body(
    hidden_in,
    segment_ids,
    pooled_grad,
    qkv_weight,
    qv_bias,
    out_weight,
    out_bias,
    first_gain,
    first_shift,
    up_weight,
    up_bias,
    down_weight,
    down_bias,
    second_gain,
    second_shift,
):
    row_count, length, width = hidden_in.shape
    x = hidden_in.reshape(row_count * length, width)

    def gather(shard):
        return lax.all_gather(shard, "fsdp", axis=0, tiled=True)

    small = jnp.concatenate(
        [qv_bias, out_bias, first_gain, first_shift, up_bias, down_bias, second_gain, second_shift]
    ).astype(BF16)
    small = lax.all_gather(small, "fsdp", axis=0, tiled=False).astype(F32)
    unit = out_bias.shape[0]
    ends = [0]
    for part in (qv_bias, out_bias, first_gain, first_shift, up_bias, down_bias, second_gain, second_shift):
        ends.append(ends[-1] + part.shape[0])
    qv, ob, g1, s1, ub, db, g2, s2 = (small[:, a:b].reshape(1, -1) for a, b in zip(ends[:-1], ends[1:]))
    zeros = jnp.zeros((1, width), F32)
    vectors = jnp.concatenate([ob, g1, s1, db, g2, s2, zeros, zeros], axis=0)
    qkv_bias = jnp.concatenate([qv[:, :width], zeros, qv[:, width:]], axis=1)
    qkv_matrix = gather(qkv_weight)
    out_matrix = gather(out_weight)
    up_matrix = gather(up_weight)
    down_matrix = gather(down_weight)
    qkv, ctx = attention_forward(x, segment_ids, qkv_matrix, qkv_bias)
    pooled, active, hidden_grad, normed, branch, first_grad, attended, ctx_grad, sums, up_sums = feedforward(
        x, ctx, segment_ids, pooled_grad, out_matrix, up_matrix, down_matrix, vectors, ub
    )

    def scatter(grad):
        return lax.psum_scatter(grad.astype(BF16), "fsdp", scatter_dimension=0, tiled=True)

    grad_down = scatter(transpose_times(active, branch))
    grad_up = scatter(transpose_times(normed, hidden_grad))
    grad_out = scatter(transpose_times(ctx, attended))
    qkv_grad, qv_sums = attention_backward(qkv, ctx_grad, segment_ids)
    grad_qkv = scatter(transpose_times(x, qkv_grad))
    grad_input = first_grad + times_transpose(qkv_grad, qkv_matrix)
    grad_qkv, grad_out, grad_up, grad_down = lax.psum(
        tuple(g.astype(F32) for g in (grad_qkv, grad_out, grad_up, grad_down)), "dp"
    )
    sums = jnp.sum(sums.reshape(6, 8, width), axis=1)
    vector_sums = jnp.concatenate(
        [jnp.sum(qv_sums, axis=0), sums.reshape(-1), jnp.sum(up_sums, axis=0)]
    )
    vector_sums = lax.psum(vector_sums, ("dp", "fsdp"))
    me = lax.axis_index("fsdp")

    def mine(start, size):
        return lax.dynamic_slice(vector_sums, (start + me * size,), (size,))

    at = 2 * width
    return (
        pooled,
        grad_input.reshape(row_count, length, width),
        grad_qkv,
        mine(0, 2 * unit),
        grad_out,
        mine(at, unit),
        mine(at + width, unit),
        mine(at + 2 * width, unit),
        grad_up,
        mine(at + 6 * width, up_bias.shape[0]),
        grad_down,
        mine(at + 3 * width, unit),
        mine(at + 4 * width, unit),
        mine(at + 5 * width, unit),
    )


def solution(mesh):
    rows = ("dp", "fsdp")
    in_specs = (P(rows, None, None), P(rows, None), P(rows, None, None)) + (
        P("fsdp", None),
        P("fsdp"),
        P("fsdp", None),
        P("fsdp"),
        P("fsdp"),
        P("fsdp"),
        P("fsdp", None),
        P("fsdp"),
        P("fsdp", None),
        P("fsdp"),
        P("fsdp"),
        P("fsdp"),
    )
    out_specs = (
        P(rows, None, None),
        P(rows, None, None),
        P("fsdp", None),
        P("fsdp"),
        P("fsdp", None),
        P("fsdp"),
        P("fsdp"),
        P("fsdp"),
        P("fsdp", None),
        P("fsdp"),
        P("fsdp", None),
        P("fsdp"),
        P("fsdp"),
        P("fsdp"),
    )
    return jax.shard_map(body, mesh=mesh, in_specs=in_specs, out_specs=out_specs, check_vma=False)
```

```python
import functools
import math

import jax
import jax.numpy as jnp
from jax import lax
from jax.experimental import pallas as pl
from jax.experimental.pallas import tpu as pltpu
from jax.sharding import PartitionSpec as P

HEAD = 64
PAIR = 2 * HEAD
EPSILON = 1e-12
F32 = jnp.float32
BF16 = jnp.bfloat16
VMEM_LIMIT = 60000 * 1024

ERFC_SLOPE = 0.33
ERFC_TERMS = (
    0.18635788923911423,
    0.18295457713165508,
    0.20123280917878972,
    0.04718951182123742,
    0.408562666534809,
    -0.35122255207376696,
    0.46028245445329624,
    -0.1353573694779288,
)


def product(left, right):
    return jnp.dot(left, right, preferred_element_type=F32)


def times_transpose(left, right):
    return lax.dot_general(left, right, (((1,), (1,)), ((), ())), preferred_element_type=F32)


def transpose_times(left, right):
    return lax.dot_general(left, right, (((0,), (0,)), ((), ())), preferred_element_type=F32)


def normal_parts(u):
    density = jnp.exp(-0.5 * u * u)
    t = 1.0 / (1.0 + (ERFC_SLOPE / math.sqrt(2.0)) * jnp.abs(u))
    poly = jnp.full_like(t, 0.5 * ERFC_TERMS[-1])
    for term in ERFC_TERMS[-2::-1]:
        poly = poly * t + 0.5 * term
    tail = poly * t * density
    cumulative = jnp.where(u >= 0.0, 1.0 - tail, tail)
    return cumulative, u * (density * (1.0 / math.sqrt(2.0 * math.pi)))


def normalise(rows):
    average = jnp.mean(rows, axis=-1, keepdims=True)
    centred = rows - average
    variance = jnp.mean(centred * centred, axis=-1, keepdims=True)
    rstd = lax.rsqrt(variance + EPSILON)
    return centred * rstd, rstd


def normalise_back(grad, gain, xhat, rstd):
    e = grad * gain
    mean_e = jnp.mean(e, axis=-1, keepdims=True)
    mean_ex = jnp.mean(e * xhat, axis=-1, keepdims=True)
    return rstd * (e - mean_e - xhat * mean_ex)


def fold(values):
    rows, width = values.shape
    return jnp.sum(values.reshape(rows // 8, 8, width), axis=0)


def lane_halves():
    lane = lax.broadcasted_iota(jnp.int32, (1, PAIR), 1)
    return (lane < HEAD).astype(BF16), (lane >= HEAD).astype(BF16)


def split_heads(block, low_half, high_half):
    return jnp.concatenate([block * low_half, block * high_half], axis=0)


def segment_grid(seg_ref, row, length):
    ids = seg_ref[pl.ds(row, 1), :].astype(F32)
    along_lanes = jnp.broadcast_to(ids, (length, length))
    return along_lanes, along_lanes.T


BLOCK = 384
SMALL = 16


def place_of(place_ref):
    return place_ref[0], place_ref[1], place_ref[2], place_ref[3]


def shard_slots(place_ref):
    y, z, x, core = place_of(place_ref)
    for other in range(2):
        for plane in range(4):
            for turn in range(4):
                if plane < 3:
                    buffer, at = plane, turn
                else:
                    buffer, at = 3 + turn // 2, turn % 2
                owner = ((z - turn) & 3) * 4 + (x ^ (plane & 1)) * 2 + (core ^ other)
                yield 5 * other + buffer, at, owner, y ^ (plane >> 1), plane < 2


def run_copies(copies, sems):
    started = []
    for number, (source, target) in enumerate(copies):
        copy = pltpu.make_async_copy(source, target, sems.at[number])
        copy.start()
        started.append(copy)
    for copy in started:
        copy.wait()


def aligned(index, unit):
    return pl.multiple_of(index * unit, unit)


def attention_rows(length, width, x_ref, seg_ref, w_ref, bias_ref, qkv_ref, ctx_ref):
    tokens = x_ref.shape[0]
    step = pl.program_id(0)
    x = x_ref[...]
    for part in range(3):
        cols = pl.ds(part * width, width)
        qkv_ref[:, cols] = (product(x, w_ref[:, cols]) + bias_ref[0:1, cols]).astype(BF16)
    low_half, high_half = lane_halves()
    ones_low = jnp.broadcast_to(low_half, (length, PAIR))
    ones_high = jnp.broadcast_to(high_half, (length, PAIR))
    scale = HEAD**-0.5
    for local in range(tokens // length):
        rows = pl.ds(local * length, length)
        along_lanes, along_rows = segment_grid(seg_ref, step * (tokens // length) + local, length)
        same = along_lanes == along_rows
        for pair in range(width // PAIR):
            q = qkv_ref[rows, pl.ds(pair * PAIR, PAIR)] * BF16(scale)
            k = qkv_ref[rows, pl.ds(width + pair * PAIR, PAIR)]
            v = qkv_ref[rows, pl.ds(2 * width + pair * PAIR, PAIR)]
            scores = times_transpose(q, split_heads(k, low_half, high_half))
            parts = []
            for half in range(2):
                masked = jnp.where(same, scores[:, half * length : (half + 1) * length], -1e30)
                peak = jnp.max(masked, axis=-1, keepdims=True)
                parts.append(jnp.exp(masked - peak).astype(BF16))
            values = jnp.concatenate(
                [
                    split_heads(v, low_half, high_half),
                    jnp.concatenate([ones_low, ones_high], axis=0),
                ],
                axis=1,
            )
            both = product(jnp.concatenate(parts, axis=1), values)
            ctx_ref[rows, pl.ds(pair * PAIR, PAIR)] = (both[:, :PAIR] / both[:, PAIR:]).astype(BF16)


def attention_gathered_kernel(length, width, place_ref, x_ref, seg_ref, *rest):
    buffers, (qkv_ref, ctx_ref, w_ref, small_ref, bias_ref, sems) = rest[:10], rest[10:]
    unit = width // 16

    @pl.when(pl.program_id(0) == 0)
    def _():
        copies = []
        for buffer, at, owner, half, first in shard_slots(place_ref):
            source = buffers[buffer].at[at]
            for block in range(3):
                target = w_ref.at[
                    pl.ds(aligned(owner, unit), unit), pl.ds(aligned(half * 3 + block, BLOCK), BLOCK)
                ]
                copies.append((source.at[pl.ds(block * unit, unit)], target))
            if first:
                copies.append((source.at[pl.ds(3 * unit, SMALL)], small_ref.at[owner]))
        run_copies(copies, sems)
        piece = 2 * unit
        lane = lax.broadcasted_iota(jnp.int32, (8, width), 1)
        for part, first in ((0, 0), (2, 8)):
            total = jnp.zeros((8, width), F32)
            for s in range(8):
                row = small_ref[first + s].astype(F32)[:8]
                row = jnp.where(lane < piece, jnp.concatenate([row, row], axis=1), 0.0)
                total = total + (pltpu.roll(row, s * piece, 1) if s else row)
            bias_ref[:, pl.ds(part * width, width)] = total
        bias_ref[:, pl.ds(width, width)] = jnp.zeros((8, width), F32)

    attention_rows(length, width, x_ref, seg_ref, w_ref, bias_ref, qkv_ref, ctx_ref)


def attention_whole_kernel(length, width, x_ref, seg_ref, w_ref, bias_ref, qkv_ref, ctx_ref):
    attention_rows(length, width, x_ref, seg_ref, w_ref, bias_ref, qkv_ref, ctx_ref)


def attention_forward(x, seg, weights, place=None, rows_per_step=2):
    row_count, length = seg.shape
    tokens, width = x.shape
    block = rows_per_step * length
    in_specs = [
        pl.BlockSpec((block, width), lambda i, *_: (i, 0)),
        pl.BlockSpec((row_count, length), lambda i, *_: (0, 0)),
    ]
    out_specs = [
        pl.BlockSpec((block, 3 * width), lambda i, *_: (i, 0)),
        pl.BlockSpec((block, width), lambda i, *_: (i, 0)),
    ]
    out_shape = [
        jax.ShapeDtypeStruct((tokens, 3 * width), BF16),
        jax.ShapeDtypeStruct((tokens, width), BF16),
    ]
    settings = dict(
        compiler_params=pltpu.CompilerParams(vmem_limit_bytes=VMEM_LIMIT),
        cost_estimate=pl.CostEstimate(
            flops=2 * tokens * width * 3 * width + 8 * tokens * length * width,
            bytes_accessed=tokens * width * 10 + 6 * width * width,
            transcendentals=tokens * length * (width // HEAD),
        ),
        name="attention_forward",
    )
    grid = (row_count // rows_per_step,)
    matrix_spec = pl.BlockSpec((width, 3 * width), lambda i, *_: (0, 0), pipeline_mode=pl.Buffered(1))
    if place is None:
        in_specs += [matrix_spec, pl.BlockSpec((1, 3 * width), lambda i: (0, 0))]
        return pl.pallas_call(
            functools.partial(attention_whole_kernel, length, width),
            grid=grid,
            in_specs=in_specs,
            out_specs=out_specs,
            out_shape=out_shape,
            **settings,
        )(x, seg, *weights)
    spec = pltpu.PrefetchScalarGridSpec(
        num_scalar_prefetch=1,
        grid=grid,
        in_specs=in_specs + [pl.BlockSpec(memory_space=pl.ANY)] * 10,
        out_specs=out_specs + [pl.BlockSpec((width, 3 * width), lambda i, *_: (0, 0))],
        scratch_shapes=[
            pltpu.VMEM((16, SMALL, BLOCK), BF16),
            pltpu.VMEM((8, 3 * width), F32),
            pltpu.SemaphoreType.DMA((112,)),
        ],
    )
    return pl.pallas_call(
        functools.partial(attention_gathered_kernel, length, width),
        grid_spec=spec,
        out_shape=out_shape + [jax.ShapeDtypeStruct((width, 3 * width), BF16)],
        **settings,
    )(place, x, seg, *weights)


def feedforward_rows(
    length,
    chunk,
    x_ref,
    ctx_ref,
    seg_ref,
    pooled_grad_ref,
    out_w_ref,
    up_w_ref,
    down_w_ref,
    vec_ref,
    up_bias_ref,
    pooled_ref,
    active_ref,
    hidden_ref,
    normed_ref,
    branch_ref,
    first_ref,
    attended_ref,
    context_ref,
    small_ref,
    up_small_ref,
    slope_ref,
):
    step = pl.program_id(0)
    tokens, width = x_ref.shape
    hidden = up_w_ref.shape[1]
    segments = pooled_grad_ref.shape[1]
    out_bias, gain_one, shift_one = vec_ref[0:1, :], vec_ref[1:2, :], vec_ref[2:3, :]
    down_bias, gain_two, shift_two = vec_ref[3:4, :], vec_ref[4:5, :], vec_ref[5:6, :]

    @pl.when(step == 0)
    def _():
        small_ref[...] = jnp.zeros_like(small_ref)
        up_small_ref[...] = jnp.zeros_like(up_small_ref)

    first_sum = x_ref[...].astype(F32) + product(ctx_ref[...], out_w_ref[...]) + out_bias
    xhat_one, rstd_one = normalise(first_sum)
    normed_one = xhat_one * gain_one + shift_one
    normed_low = normed_one.astype(BF16)
    normed_ref[...] = normed_low
    second_sum = normed_one + down_bias
    for start in range(0, hidden, chunk):
        cols = pl.ds(start, chunk)
        pre = product(normed_low, up_w_ref[:, cols]) + up_bias_ref[:, cols]
        cumulative, tilt = normal_parts(pre)
        active = (pre * cumulative).astype(BF16)
        slope_ref[:, cols] = cumulative + tilt
        active_ref[:, cols] = active
        second_sum = second_sum + product(active, down_w_ref[cols, :])
    xhat_two, rstd_two = normalise(second_sum)
    final = xhat_two * gain_two + shift_two
    final_high = final.astype(BF16)
    final_low = (final - final_high.astype(F32)).astype(BF16)
    token_parts = []
    for local in range(tokens // length):
        rows = slice(local * length, (local + 1) * length)
        along_lanes, along_rows = segment_grid(seg_ref, step * (tokens // length) + local, length)
        index = lax.broadcasted_iota(jnp.int32, (8, length), 0).astype(F32)
        member = (along_lanes[:8, :] == index).astype(F32)
        population = jnp.sum(member, axis=1, keepdims=True)
        member_low = member.astype(BF16)
        sums = product(member_low, final_high[rows]) + product(member_low, final_low[rows])
        pooled_ref[local] = sums[:segments] / population[:segments]
        share = pooled_grad_ref[local] / population[:segments]
        wide = jnp.concatenate([along_rows] * (width // length), axis=1)
        token = jnp.broadcast_to(share[segments - 1 : segments], (length, width))
        for s in range(segments - 2, -1, -1):
            token = jnp.where(wide == float(s), share[s : s + 1], token)
        token_parts.append(token)
    token_grad = jnp.concatenate(token_parts, axis=0)
    second_grad = normalise_back(token_grad, gain_two, xhat_two, rstd_two)
    branch = second_grad.astype(BF16)
    branch_ref[...] = branch
    small_ref[24:32, :] += fold(branch.astype(F32))
    small_ref[32:40, :] += fold(token_grad * xhat_two)
    small_ref[40:48, :] += fold(token_grad)
    normed_grad = second_grad
    for start in range(0, hidden, chunk):
        cols = pl.ds(start, chunk)
        grad = (times_transpose(branch, down_w_ref[cols, :]) * slope_ref[:, cols]).astype(BF16)
        hidden_ref[:, cols] = grad
        up_small_ref[:, cols] += fold(grad.astype(F32))
        normed_grad = normed_grad + times_transpose(grad, up_w_ref[:, cols])
    first_grad = normalise_back(normed_grad, gain_one, xhat_one, rstd_one)
    first_ref[...] = first_grad
    attended = first_grad.astype(BF16)
    attended_ref[...] = attended
    context_ref[...] = times_transpose(attended, out_w_ref[...]).astype(BF16)
    small_ref[0:8, :] += fold(attended.astype(F32))
    small_ref[8:16, :] += fold(normed_grad * xhat_one)
    small_ref[16:24, :] += fold(normed_grad)


def feedforward_gathered_kernel(length, chunk, place_ref, x_ref, ctx_ref, seg_ref, pooled_grad_ref, *rest):
    buffers, outs = rest[:10], rest[10:20]
    slope_ref, out_w_ref, up_w_ref, down_w_ref, vec_ref, up_bias_ref, gathered_ref, sems = rest[20:]
    width, hidden = up_w_ref.shape
    unit = width // 16
    ratio = hidden // width

    @pl.when(pl.program_id(0) == 0)
    def _():
        copies = []
        for buffer, at, owner, half, first in shard_slots(place_ref):
            source = buffers[buffer].at[at]
            rows = pl.ds(aligned(owner, unit), unit)
            for block in range(ratio):
                cols = pl.ds(aligned(half * ratio + block, BLOCK), BLOCK)
                copies.append((source.at[pl.ds(block * unit, unit)], up_w_ref.at[rows, cols]))
            cols = pl.ds(aligned(half, BLOCK), BLOCK)
            down_rows = pl.ds(aligned(owner, ratio * unit), ratio * unit)
            copies.append((source.at[pl.ds(ratio * unit, ratio * unit)], down_w_ref.at[down_rows, cols]))
            copies.append((source.at[pl.ds(2 * ratio * unit, unit)], out_w_ref.at[rows, cols]))
            if first:
                at_small = (2 * ratio + 1) * unit
                copies.append((source.at[pl.ds(at_small, SMALL)], gathered_ref.at[owner]))
        run_copies(copies, sems)
        lane = lax.broadcasted_iota(jnp.int32, (8, width), 1)
        total = jnp.zeros((8, width), F32)
        for s in range(16):
            row = gathered_ref[s].astype(F32)[:8]
            row = jnp.where(lane < unit, jnp.concatenate([row, row], axis=1), 0.0)
            total = total + (pltpu.roll(row, s * unit, 1) if s else row)
        vec_ref[...] = total
        lane = lax.broadcasted_iota(jnp.int32, (8, BLOCK), 1)
        for s in range(0, 16, 2):
            low = gathered_ref[s].astype(F32)[:8]
            high = gathered_ref[s + 1].astype(F32)[:8]
            high = pltpu.roll(high, BLOCK // 2, 1)
            both = jnp.where(lane < BLOCK // 2, low, high)
            up_bias_ref[:, pl.ds((s // 2) * BLOCK, BLOCK)] = both[6:7, :]

    feedforward_rows(
        length, chunk, x_ref, ctx_ref, seg_ref, pooled_grad_ref,
        out_w_ref, up_w_ref, down_w_ref, vec_ref, up_bias_ref, *outs, slope_ref,
    )


def feedforward(x, ctx, seg, pooled_grad, weights, hidden, place=None, rows_per_step=2, chunk=768):
    row_count, length = seg.shape
    tokens, width = x.shape
    segments = pooled_grad.shape[1]
    block = rows_per_step * length

    def tiled(columns):
        return pl.BlockSpec((block, columns), lambda i, *_: (i, 0))

    def whole(shape):
        return pl.BlockSpec(shape, lambda i, *_: (0,) * len(shape), pipeline_mode=pl.Buffered(1))

    def kept(shape):
        return pl.BlockSpec(shape, lambda i, *_: (0,) * len(shape))

    def rows(columns, dtype):
        return jax.ShapeDtypeStruct((tokens, columns), dtype)

    grid = (row_count // rows_per_step,)
    in_specs = [
        tiled(width),
        tiled(width),
        whole((row_count, length)),
        pl.BlockSpec((rows_per_step, segments, width), lambda i, *_: (i, 0, 0)),
    ]
    out_specs = [
        pl.BlockSpec((rows_per_step, segments, width), lambda i, *_: (i, 0, 0)),
        tiled(hidden),
        tiled(hidden),
        tiled(width),
        tiled(width),
        tiled(width),
        tiled(width),
        tiled(width),
        kept((48, width)),
        kept((8, hidden)),
    ]
    out_shape = [
        jax.ShapeDtypeStruct((row_count, segments, width), F32),
        rows(hidden, BF16),
        rows(hidden, BF16),
        rows(width, BF16),
        rows(width, BF16),
        rows(width, F32),
        rows(width, BF16),
        rows(width, BF16),
        jax.ShapeDtypeStruct((48, width), F32),
        jax.ShapeDtypeStruct((8, hidden), F32),
    ]
    settings = dict(
        compiler_params=pltpu.CompilerParams(vmem_limit_bytes=VMEM_LIMIT),
        cost_estimate=pl.CostEstimate(
            flops=tokens * width * (4 * width + 8 * hidden),
            bytes_accessed=tokens * (width * 18 + hidden * 4) + 4 * width * hidden,
            transcendentals=2 * tokens * hidden,
        ),
        name="feedforward",
    )
    slope = pltpu.VMEM((block, hidden), F32)
    if place is None:
        in_specs += [
            whole((width, width)),
            whole((width, hidden)),
            whole((hidden, width)),
            whole((8, width)),
            whole((1, hidden)),
        ]
        return pl.pallas_call(
            functools.partial(feedforward_rows, length, chunk),
            grid=grid,
            in_specs=in_specs,
            out_specs=out_specs,
            out_shape=out_shape,
            scratch_shapes=[slope],
            **settings,
        )(x, ctx, seg, pooled_grad, *weights)
    spec = pltpu.PrefetchScalarGridSpec(
        num_scalar_prefetch=1,
        grid=grid,
        in_specs=in_specs + [pl.BlockSpec(memory_space=pl.ANY)] * 10,
        out_specs=out_specs,
        scratch_shapes=[
            slope,
            pltpu.VMEM((width, width), BF16),
            pltpu.VMEM((width, hidden), BF16),
            pltpu.VMEM((hidden, width), BF16),
            pltpu.VMEM((8, width), F32),
            pltpu.VMEM((1, hidden), F32),
            pltpu.VMEM((16, SMALL, BLOCK), BF16),
            pltpu.SemaphoreType.DMA((32 * (hidden // width + 2) + 16,)),
        ],
    )
    return pl.pallas_call(
        functools.partial(feedforward_gathered_kernel, length, chunk),
        grid_spec=spec,
        out_shape=out_shape,
        **settings,
    )(place, x, ctx, seg, pooled_grad, *weights)


def attention_back_kernel(length, width, qkv_ref, grad_ref, seg_ref, out_ref, small_ref):
    tokens = grad_ref.shape[0]
    step = pl.program_id(0)

    @pl.when(step == 0)
    def _():
        small_ref[...] = jnp.zeros_like(small_ref)

    low_half, high_half = lane_halves()
    scale = HEAD**-0.5
    for local in range(tokens // length):
        rows = pl.ds(local * length, length)
        along_lanes, along_rows = segment_grid(seg_ref, step * (tokens // length) + local, length)
        same = along_lanes == along_rows
        same = jnp.concatenate([same, same], axis=1)
        for pair in range(width // PAIR):
            at = (pl.ds(pair * PAIR, PAIR), pl.ds(width + pair * PAIR, PAIR), pl.ds(2 * width + pair * PAIR, PAIR))
            q = split_heads(qkv_ref[rows, at[0]] * BF16(scale), low_half, high_half)
            k = qkv_ref[rows, at[1]]
            v = qkv_ref[rows, at[2]]
            ctx_grad = split_heads(grad_ref[rows, at[0]], low_half, high_half)
            scores = jnp.where(same, times_transpose(k, q), -1e30)
            weights = jnp.exp(scores - jnp.max(scores, axis=0, keepdims=True))
            weights = weights * (1.0 / jnp.sum(weights, axis=0, keepdims=True))
            probs_grad = times_transpose(v, ctx_grad)
            inner = jnp.sum(weights * probs_grad, axis=0, keepdims=True)
            scores_grad = (weights * (probs_grad - inner)).astype(BF16)
            values_grad = product(weights.astype(BF16), ctx_grad).astype(BF16)
            keys_grad = product(scores_grad, q).astype(BF16)
            turned = jnp.concatenate([scores_grad[:, :length].T, scores_grad[:, length:].T], axis=1)
            queries_grad = product(turned, split_heads(k * BF16(scale), low_half, high_half)).astype(BF16)
            out_ref[rows, at[0]] = queries_grad
            out_ref[rows, at[1]] = keys_grad
            out_ref[rows, at[2]] = values_grad
            small_ref[:, at[0]] += fold(queries_grad.astype(F32))
            small_ref[:, at[1]] += fold(values_grad.astype(F32))


def attention_backward(qkv, ctx_grad, seg, rows_per_step=2):
    row_count, length = seg.shape
    tokens, width = ctx_grad.shape
    block = rows_per_step * length
    return pl.pallas_call(
        functools.partial(attention_back_kernel, length, width),
        grid=(row_count // rows_per_step,),
        in_specs=[
            pl.BlockSpec((block, 3 * width), lambda i: (i, 0)),
            pl.BlockSpec((block, width), lambda i: (i, 0)),
            pl.BlockSpec((row_count, length), lambda i: (0, 0)),
        ],
        out_specs=[
            pl.BlockSpec((block, 3 * width), lambda i: (i, 0)),
            pl.BlockSpec((8, 2 * width), lambda i: (0, 0)),
        ],
        out_shape=[
            jax.ShapeDtypeStruct((tokens, 3 * width), BF16),
            jax.ShapeDtypeStruct((8, 2 * width), F32),
        ],
        compiler_params=pltpu.CompilerParams(vmem_limit_bytes=VMEM_LIMIT),
        cost_estimate=pl.CostEstimate(
            flops=20 * tokens * length * width,
            bytes_accessed=tokens * width * 14,
            transcendentals=tokens * length * (width // HEAD),
        ),
        name="attention_backward",
    )(qkv, ctx_grad, seg)


def cut_columns(half_index, shard, out_ref, row_at, blocks):
    rows = shard.shape[0]
    for half in range(2):

        @pl.when(half_index == half)
        def _():
            for block in range(blocks):
                cols = pl.ds((half * blocks + block) * BLOCK, BLOCK)
                out_ref[pl.ds(row_at + block * rows, rows), :] = shard[:, cols]


def pack_attention_kernel(place_ref, qkv_ref, small_ref, out_ref):
    unit = qkv_ref.shape[0]
    cut_columns(place_ref[0], qkv_ref, out_ref, 0, 3)
    out_ref[pl.ds(3 * unit, SMALL), :] = small_ref[...]


def pack_feedforward_kernel(place_ref, up_ref, down_ref, out_w_ref, small_ref, out_ref):
    unit = up_ref.shape[0]
    ratio = down_ref.shape[0] // unit
    cut_columns(place_ref[0], up_ref, out_ref, 0, ratio)
    cut_columns(place_ref[0], down_ref, out_ref, ratio * unit, 1)
    cut_columns(place_ref[0], out_w_ref, out_ref, 2 * ratio * unit, 1)
    out_ref[pl.ds((2 * ratio + 1) * unit, SMALL), :] = small_ref[...]


def pack(kernel, name, place, rows, *shards):
    spec = pltpu.PrefetchScalarGridSpec(
        num_scalar_prefetch=1,
        grid=(1,),
        in_specs=[pl.BlockSpec(s.shape, lambda i, *_: (0, 0)) for s in shards],
        out_specs=pl.BlockSpec((rows, BLOCK), lambda i, *_: (0, 0)),
    )
    return pl.pallas_call(
        kernel, grid_spec=spec, out_shape=jax.ShapeDtypeStruct((rows, BLOCK), BF16), name=name
    )(place, *shards)


def store_shards(place_ref, keep_ref, send_ref, plane_z, half, row_at, rows, values):
    y, z, x, core = place_of(place_ref)
    turn = (z - plane_z) & 3
    first = core == 0
    for plane_x in range(2):
        even = values(plane_z * 4 + plane_x * 2)
        odd = values(plane_z * 4 + plane_x * 2 + 1)
        at = (half ^ y, plane_x ^ x, turn, pl.ds(row_at, rows))
        keep_ref[at] = jnp.where(first, even, odd)
        send_ref[at] = jnp.where(first, odd, even)


def down_gradient_kernel(place_ref, active_ref, branch_ref, keep_ref, send_ref):
    grad = transpose_times(active_ref[...], branch_ref[...]).astype(BF16)
    rows = grad.shape[0] // 4
    for half in range(2):

        def values(s):
            return grad[(s % 4) * rows : (s % 4 + 1) * rows, half * BLOCK : (half + 1) * BLOCK]

        y, z, x, core = place_of(place_ref)
        turn = (z - pl.program_id(0)) & 3
        first = core == 0
        for plane_x in range(2):
            even, odd = values(plane_x * 2), values(plane_x * 2 + 1)
            at = (half ^ y, plane_x ^ x, turn)
            keep_ref[at] = jnp.where(first, even, odd)
            send_ref[at] = jnp.where(first, odd, even)


def store_columns(place_ref, keep_ref, send_ref, grad, first_block, blocks):
    unit = grad.shape[0] // 16
    for part in range(2):
        number = first_block + part
        half = number // blocks
        row_at = (number - half * blocks) * unit
        if not isinstance(row_at, int):
            row_at = pl.multiple_of(row_at, unit)

        def values(s):
            return grad[s * unit : (s + 1) * unit, part * BLOCK : (part + 1) * BLOCK]

        for plane_z in range(4):
            store_shards(place_ref, keep_ref, send_ref, plane_z, half, row_at, unit, values)


def store_small(place_ref, keep_ref, send_ref, row_at, values):
    for half in range(2):
        for plane_z in range(4):
            store_shards(place_ref, keep_ref, send_ref, plane_z, half, row_at, SMALL, values)


def up_gradient_kernel(
    place_ref, normed_ref, hidden_ref, ctx_ref, attended_ref, sums_ref, up_sums_ref, keep_ref, send_ref, turned_ref
):
    step = pl.program_id(0)
    last = pl.num_programs(0) - 1
    width = normed_ref.shape[1]
    unit = width // 16
    blocks = last

    @pl.when(step == 0)
    def _():
        turned_ref[...] = normed_ref[...].T

    @pl.when(step < last)
    def _():
        grad = product(turned_ref[...], hidden_ref[...]).astype(BF16)
        store_columns(place_ref, keep_ref, send_ref, grad, 2 * step, blocks)

    @pl.when(step == last)
    def _():
        grad = transpose_times(ctx_ref[...], attended_ref[...]).astype(BF16)
        steps = up_sums_ref.shape[1] // width
        for part in range(2):

            def values(s):
                return grad[s * unit : (s + 1) * unit, part * BLOCK : (part + 1) * BLOCK]

            for plane_z in range(4):
                store_shards(place_ref, keep_ref, send_ref, plane_z, part, steps * unit, unit, values)
        row = lax.broadcasted_iota(jnp.int32, (SMALL, width), 0)
        vectors = jnp.zeros((SMALL, width), F32)
        for number in range(6):
            total = jnp.sum(sums_ref[pl.ds(8 * number, 8), :], axis=0, keepdims=True)
            vectors = jnp.where(row == number, total, vectors)
        up_total = jnp.sum(up_sums_ref[...], axis=0, keepdims=True)
        row = row[:, :BLOCK]

        def small(s):
            rolled = pltpu.roll(vectors, width - s * unit, 1) if s else vectors
            up = jnp.broadcast_to(up_total[:, (s // 2) * BLOCK : (s // 2 + 1) * BLOCK], (SMALL, BLOCK))
            up = pltpu.roll(up, BLOCK // 2, 1) if s % 2 else up
            return jnp.where(row == 6, up, rolled[:, :BLOCK]).astype(BF16)

        store_small(place_ref, keep_ref, send_ref, (steps + 1) * unit, small)


def qkv_gradient_kernel(place_ref, x_ref, grad_ref, sums_ref, keep_ref, send_ref, turned_ref):
    step = pl.program_id(0)
    width = x_ref.shape[1]
    unit = width // 16

    @pl.when(step == 0)
    def _():
        turned_ref[...] = x_ref[...].T
        total = jnp.sum(sums_ref[...], axis=0, keepdims=True)

        def small(s):
            part = total[:, (s // 8) * width : (s // 8 + 1) * width]
            part = jnp.broadcast_to(part, (SMALL, width))
            shift = (s % 8) * 2 * unit
            part = pltpu.roll(part, width - shift, 1) if shift else part
            return part[:, :BLOCK].astype(BF16)

        store_small(place_ref, keep_ref, send_ref, 3 * unit, small)

    grad = product(turned_ref[...], grad_ref[...]).astype(BF16)
    store_columns(place_ref, keep_ref, send_ref, grad, 2 * step, 3)


def weight_gradient(kernel, name, place, rows, steps, arrays, specs, flops, turned=None):
    shape = (2, 2, 4, rows, BLOCK)
    whole = pl.BlockSpec(shape, lambda i, *_: (0,) * 5)
    spec = pltpu.PrefetchScalarGridSpec(
        num_scalar_prefetch=1,
        grid=(steps,),
        in_specs=specs,
        out_specs=[whole, whole],
        scratch_shapes=[] if turned is None else [pltpu.VMEM(turned, BF16)],
    )
    return pl.pallas_call(
        kernel,
        grid_spec=spec,
        out_shape=[jax.ShapeDtypeStruct(shape, BF16)] * 2,
        compiler_params=pltpu.CompilerParams(vmem_limit_bytes=VMEM_LIMIT),
        cost_estimate=pl.CostEstimate(
            flops=flops, bytes_accessed=sum(2 * a.size for a in arrays), transcendentals=0
        ),
        name=name,
    )(place, *arrays)


def resident(shape):
    return pl.BlockSpec(shape, lambda i, *_: (0,) * len(shape), pipeline_mode=pl.Buffered(1))


def input_gradient_kernel(first_ref, grad_ref, w_ref, out_ref):
    out_ref[...] = first_ref[...] + times_transpose(grad_ref[...], w_ref[...])


def input_gradient(first_grad, qkv_grad, matrix, rows=512):
    tokens, width = first_grad.shape
    return pl.pallas_call(
        input_gradient_kernel,
        grid=(tokens // rows,),
        in_specs=[
            pl.BlockSpec((rows, width), lambda i: (i, 0)),
            pl.BlockSpec((rows, 3 * width), lambda i: (i, 0)),
            resident(matrix.shape),
        ],
        out_specs=pl.BlockSpec((rows, width), lambda i: (i, 0)),
        out_shape=jax.ShapeDtypeStruct((tokens, width), F32),
        compiler_params=pltpu.CompilerParams(vmem_limit_bytes=VMEM_LIMIT),
        cost_estimate=pl.CostEstimate(
            flops=6 * tokens * width * width, bytes_accessed=14 * tokens * width, transcendentals=0
        ),
        name="input_gradient",
    )(first_grad, qkv_grad, matrix)


AXES = ("dp", "fsdp")
DEVICES = 32


def across(value, mask):
    return lax.ppermute(value, AXES, [(i, i ^ mask) for i in range(DEVICES)])


def along_z(value, distance):
    def target(i):
        return i - i % 16 + (i % 16 + 4 * distance) % 16

    return lax.ppermute(value, AXES, [(i, target(i)) for i in range(DEVICES)])


CORE, X, Y = 1, 2, 16


def gather_shards(own):
    turned = [along_z(own, d) for d in (1, 2, 3)]
    here = jnp.stack([own] + turned)
    from_x = across(here, X)
    from_y = across(here, Y)
    diagonal_low = across(from_x[:2], Y)
    diagonal_high = across(from_y[2:], X)
    mine = (here, from_x, from_y, diagonal_low, diagonal_high)
    return mine + tuple(across(piece, CORE) for piece in mine)


def reduce_shards(keep, send):
    def wide(value):
        return value.astype(F32)

    got = across(send, CORE)

    def pair(at):
        return wide(keep[at]) + wide(got[at])

    low, high = slice(0, 2), slice(2, 4)
    every = slice(None)
    low_x = across(pair((every, 1, low)).astype(BF16), X)
    high_y = across(pair((1, every, high)).astype(BF16), Y)
    low_y = across((pair((1, 0, low)) + wide(low_x[1])).astype(BF16), Y)
    high_x = across((pair((0, 1, high)) + wide(high_y[1])).astype(BF16), X)
    low_sum = pair((0, 0, low)) + wide(low_x[0]) + wide(low_y)
    high_sum = pair((0, 0, high)) + wide(high_y[0]) + wide(high_x)
    total = low_sum[0]
    for turn in (1, 2, 3):
        part = low_sum[1] if turn == 1 else high_sum[turn - 2]
        total = total + wide(along_z(part.astype(BF16), 4 - turn))
    return total


def both_halves(mine, y):
    theirs = across(mine.astype(BF16), Y).astype(F32)
    swap = y == 0
    return jnp.where(swap, mine, theirs), jnp.where(swap, theirs, mine)


def join_columns(halves, unit, blocks):
    parts = []
    for half in halves:
        cols = half.reshape(blocks, unit, BLOCK)
        parts += [cols[b] for b in range(blocks)]
    return jnp.concatenate(parts, axis=1)


def rows_of(vectors, rows):
    padded = [jnp.pad(v, (0, BLOCK - v.shape[0])) for v in vectors]
    padded += [jnp.zeros((BLOCK,), BF16)] * (rows - len(padded))
    return jnp.stack(padded)


def body_by_permutes(
    hidden_in,
    segment_ids,
    pooled_grad,
    qkv_weight,
    qv_bias,
    out_weight,
    out_bias,
    first_gain,
    first_shift,
    up_weight,
    up_bias,
    down_weight,
    down_bias,
    second_gain,
    second_shift,
):
    row_count, length, width = hidden_in.shape
    tokens = row_count * length
    x = hidden_in.reshape(tokens, width)
    unit = qkv_weight.shape[0]
    hidden = up_weight.shape[1]
    ratio = hidden // width
    y, shard = lax.axis_index("dp"), lax.axis_index("fsdp")
    place = jnp.stack([y, shard // 4, shard // 2 % 2, shard % 2]).astype(jnp.int32)

    attention_rows_count = 3 * unit + SMALL
    feedforward_rows_count = (2 * ratio + 1) * unit + SMALL
    own_attention = pack(
        pack_attention_kernel,
        "pack_attention",
        place,
        attention_rows_count,
        qkv_weight,
        rows_of([qv_bias], SMALL),
    )
    own_feedforward = pack(
        pack_feedforward_kernel,
        "pack_feedforward",
        place,
        feedforward_rows_count,
        up_weight,
        down_weight,
        out_weight,
        rows_of([out_bias, first_gain, first_shift, down_bias, second_gain, second_shift, up_bias], SMALL),
    )
    attention_pieces = gather_shards(own_attention)
    feedforward_pieces = gather_shards(own_feedforward)
    qkv, ctx, qkv_matrix = attention_forward(x, segment_ids, attention_pieces, place)
    pooled, active, hidden_grad, normed, branch, first_grad, attended, ctx_grad, sums, up_sums = feedforward(
        x, ctx, segment_ids, pooled_grad, feedforward_pieces, hidden, place
    )
    down_keep, down_send = weight_gradient(
        down_gradient_kernel,
        "down_gradient",
        place,
        ratio * unit,
        4,
        (active, branch),
        [pl.BlockSpec((tokens, hidden // 4), lambda i, *_: (0, i)), resident((tokens, width))],
        2 * tokens * hidden * width,
    )
    down_total = reduce_shards(down_keep, down_send)
    up_keep, up_send = weight_gradient(
        up_gradient_kernel,
        "up_gradient",
        place,
        (ratio + 1) * unit + SMALL,
        ratio + 1,
        (normed, hidden_grad, ctx, attended, sums, up_sums),
        [
            resident((tokens, width)),
            pl.BlockSpec((tokens, width), lambda i, *_: (0, jnp.minimum(i, ratio - 1))),
            resident((tokens, width)),
            resident((tokens, width)),
            resident(sums.shape),
            resident(up_sums.shape),
        ],
        2 * tokens * width * (hidden + width),
        (width, tokens),
    )
    up_total = reduce_shards(up_keep, up_send)
    qkv_grad, qv_sums = attention_backward(qkv, ctx_grad, segment_ids)
    qkv_keep, qkv_send = weight_gradient(
        qkv_gradient_kernel,
        "qkv_gradient",
        place,
        3 * unit + SMALL,
        3,
        (x, qkv_grad, qv_sums),
        [
            resident((tokens, width)),
            pl.BlockSpec((tokens, width), lambda i, *_: (0, i)),
            resident(qv_sums.shape),
        ],
        6 * tokens * width * width,
        (width, tokens),
    )
    qkv_total = reduce_shards(qkv_keep, qkv_send)
    grad_input = input_gradient(first_grad, qkv_grad, qkv_matrix)

    grad_down = jnp.concatenate(both_halves(down_total, y), axis=1)
    up_part, up_small = up_total[: (ratio + 1) * unit], up_total[(ratio + 1) * unit :]
    up_low, up_high = both_halves(up_part, y)
    grad_up = join_columns((up_low[: ratio * unit], up_high[: ratio * unit]), unit, ratio)
    grad_out = join_columns((up_low[ratio * unit :], up_high[ratio * unit :]), unit, 1)
    qkv_part, qkv_small = qkv_total[: 3 * unit], qkv_total[3 * unit :]
    grad_qkv = join_columns(both_halves(qkv_part, y), unit, 3)
    return (
        pooled,
        grad_input.reshape(row_count, length, width),
        grad_qkv,
        qkv_small[0, : 2 * unit],
        grad_out,
        up_small[0, :unit],
        up_small[1, :unit],
        up_small[2, :unit],
        grad_up,
        up_small[6, : ratio * unit],
        grad_down,
        up_small[3, :unit],
        up_small[4, :unit],
        up_small[5, :unit],
    )


def body_by_collectives(
    hidden_in,
    segment_ids,
    pooled_grad,
    qkv_weight,
    qv_bias,
    out_weight,
    out_bias,
    first_gain,
    first_shift,
    up_weight,
    up_bias,
    down_weight,
    down_bias,
    second_gain,
    second_shift,
):
    row_count, length, width = hidden_in.shape
    x = hidden_in.reshape(row_count * length, width)

    def gather(shard):
        return lax.all_gather(shard, "fsdp", axis=0, tiled=True)

    small = jnp.concatenate(
        [qv_bias, out_bias, first_gain, first_shift, up_bias, down_bias, second_gain, second_shift]
    ).astype(BF16)
    small = lax.all_gather(small, "fsdp", axis=0, tiled=False).astype(F32)
    unit = out_bias.shape[0]
    ends = [0]
    for part in (qv_bias, out_bias, first_gain, first_shift, up_bias, down_bias, second_gain, second_shift):
        ends.append(ends[-1] + part.shape[0])
    qv, ob, g1, s1, ub, db, g2, s2 = (small[:, a:b].reshape(1, -1) for a, b in zip(ends[:-1], ends[1:]))
    zeros = jnp.zeros((1, width), F32)
    vectors = jnp.concatenate([ob, g1, s1, db, g2, s2, zeros, zeros], axis=0)
    qkv_bias = jnp.concatenate([qv[:, :width], zeros, qv[:, width:]], axis=1)
    qkv_matrix = gather(qkv_weight)
    out_matrix = gather(out_weight)
    up_matrix = gather(up_weight)
    down_matrix = gather(down_weight)
    qkv, ctx = attention_forward(x, segment_ids, (qkv_matrix, qkv_bias))
    pooled, active, hidden_grad, normed, branch, first_grad, attended, ctx_grad, sums, up_sums = feedforward(
        x, ctx, segment_ids, pooled_grad, (out_matrix, up_matrix, down_matrix, vectors, ub), up_matrix.shape[1]
    )

    def scatter(grad):
        return lax.psum_scatter(grad.astype(BF16), "fsdp", scatter_dimension=0, tiled=True)

    grad_down = scatter(transpose_times(active, branch))
    grad_up = scatter(transpose_times(normed, hidden_grad))
    grad_out = scatter(transpose_times(ctx, attended))
    qkv_grad, qv_sums = attention_backward(qkv, ctx_grad, segment_ids)
    grad_qkv = scatter(transpose_times(x, qkv_grad))
    grad_input = first_grad + times_transpose(qkv_grad, qkv_matrix)
    grad_qkv, grad_out, grad_up, grad_down = lax.psum(
        tuple(g.astype(F32) for g in (grad_qkv, grad_out, grad_up, grad_down)), "dp"
    )
    sums = jnp.sum(sums.reshape(6, 8, width), axis=1)
    vector_sums = jnp.concatenate(
        [jnp.sum(qv_sums, axis=0), sums.reshape(-1), jnp.sum(up_sums, axis=0)]
    )
    vector_sums = lax.psum(vector_sums, ("dp", "fsdp"))
    me = lax.axis_index("fsdp")

    def mine(start, size):
        return lax.dynamic_slice(vector_sums, (start + me * size,), (size,))

    at = 2 * width
    return (
        pooled,
        grad_input.reshape(row_count, length, width),
        grad_qkv,
        mine(0, 2 * unit),
        grad_out,
        mine(at, unit),
        mine(at + width, unit),
        mine(at + 2 * width, unit),
        grad_up,
        mine(at + 6 * width, up_bias.shape[0]),
        grad_down,
        mine(at + 3 * width, unit),
        mine(at + 4 * width, unit),
        mine(at + 5 * width, unit),
    )


def solution(mesh):
    rows = ("dp", "fsdp")
    in_specs = (P(rows, None, None), P(rows, None), P(rows, None, None)) + (
        P("fsdp", None),
        P("fsdp"),
        P("fsdp", None),
        P("fsdp"),
        P("fsdp"),
        P("fsdp"),
        P("fsdp", None),
        P("fsdp"),
        P("fsdp", None),
        P("fsdp"),
        P("fsdp"),
        P("fsdp"),
    )
    out_specs = (
        P(rows, None, None),
        P(rows, None, None),
        P("fsdp", None),
        P("fsdp"),
        P("fsdp", None),
        P("fsdp"),
        P("fsdp"),
        P("fsdp"),
        P("fsdp", None),
        P("fsdp"),
        P("fsdp", None),
        P("fsdp"),
        P("fsdp"),
        P("fsdp"),
    )
    body = body_by_permutes if dict(mesh.shape) == {"dp": 2, "fsdp": 16} else body_by_collectives
    return jax.shard_map(body, mesh=mesh, in_specs=in_specs, out_specs=out_specs, check_vma=False)
```

```python
import functools
import math

import jax
import jax.numpy as jnp
from jax import lax
from jax.experimental import pallas as pl
from jax.experimental.pallas import tpu as pltpu
from jax.sharding import PartitionSpec as P

HEAD = 64
PAIR = 2 * HEAD
EPSILON = 1e-12
F32 = jnp.float32
BF16 = jnp.bfloat16
VMEM_LIMIT = 60000 * 1024


def product(left, right):
    return jnp.dot(left, right, preferred_element_type=F32)


def times_transpose(left, right):
    return lax.dot_general(left, right, (((1,), (1,)), ((), ())), preferred_element_type=F32)


def transpose_times(left, right):
    return lax.dot_general(left, right, (((0,), (0,)), ((), ())), preferred_element_type=F32)


def normal_parts(u):
    cumulative = 0.5 + 0.5 * lax.erf(u * math.sqrt(0.5))
    return cumulative, u * (jnp.exp(-0.5 * u * u) * (1.0 / math.sqrt(2.0 * math.pi)))


def normalise(rows):
    average = jnp.mean(rows, axis=-1, keepdims=True)
    centred = rows - average
    variance = jnp.mean(centred * centred, axis=-1, keepdims=True)
    rstd = lax.rsqrt(variance + EPSILON)
    return centred * rstd, rstd


def normalise_back(grad, gain, xhat, rstd):
    e = grad * gain
    mean_e = jnp.mean(e, axis=-1, keepdims=True)
    mean_ex = jnp.mean(e * xhat, axis=-1, keepdims=True)
    return rstd * (e - mean_e - xhat * mean_ex)


def fold(values):
    rows, width = values.shape
    return jnp.sum(values.reshape(rows // 8, 8, width), axis=0)


def lane_halves():
    lane = lax.broadcasted_iota(jnp.int32, (1, PAIR), 1)
    return (lane < HEAD).astype(BF16), (lane >= HEAD).astype(BF16)


def split_heads(block, low_half, high_half):
    return jnp.concatenate([block * low_half, block * high_half], axis=0)


def segment_grid(seg_ref, row, length):
    ids = seg_ref[pl.ds(row, 1), :].astype(F32)
    along_lanes = jnp.broadcast_to(ids, (length, length))
    return along_lanes, along_lanes.T


BLOCK = 384
SMALL = 16


def place_of(place_ref):
    return place_ref[0], place_ref[1], place_ref[2], place_ref[3]


def shard_slots(place_ref, whole_planes):
    y, z, x, core = place_of(place_ref)
    for other in range(2):
        for plane in range(4):
            for turn in range(4):
                if plane < whole_planes:
                    buffer, at = plane, turn
                else:
                    buffer, at = 2 * plane - whole_planes + turn // 2, turn % 2
                owner = ((z - turn) & 3) * 4 + (x ^ (plane & 1)) * 2 + (core ^ other)
                yield (8 - whole_planes) * other + buffer, at, owner, y ^ (plane >> 1), plane < 2


def run_copies(copies, sems):
    started = []
    for number, (source, target) in enumerate(copies):
        copy = pltpu.make_async_copy(source, target, sems.at[number])
        copy.start()
        started.append(copy)
    for copy in started:
        copy.wait()


def aligned(index, unit):
    return pl.multiple_of(index * unit, unit)


def attention_rows(length, width, first, x_ref, seg_ref, w_ref, bias_ref, qkv_ref, ctx_ref):
    tokens = x_ref.shape[0]
    step = pl.program_id(0) + first
    x = x_ref[...]
    for part in range(3):
        cols = pl.ds(part * width, width)
        qkv_ref[:, cols] = (product(x, w_ref[:, cols]) + bias_ref[0:1, cols]).astype(BF16)
    low_half, high_half = lane_halves()
    ones_low = jnp.broadcast_to(low_half, (length, PAIR))
    ones_high = jnp.broadcast_to(high_half, (length, PAIR))
    scale = HEAD**-0.5
    for local in range(tokens // length):
        rows = pl.ds(local * length, length)
        along_lanes, along_rows = segment_grid(seg_ref, step * (tokens // length) + local, length)
        same = along_lanes == along_rows
        for pair in range(width // PAIR):
            q = qkv_ref[rows, pl.ds(pair * PAIR, PAIR)] * BF16(scale)
            k = qkv_ref[rows, pl.ds(width + pair * PAIR, PAIR)]
            v = qkv_ref[rows, pl.ds(2 * width + pair * PAIR, PAIR)]
            scores = times_transpose(q, split_heads(k, low_half, high_half))
            parts = []
            for half in range(2):
                masked = jnp.where(same, scores[:, half * length : (half + 1) * length], -1e30)
                peak = jnp.max(masked, axis=-1, keepdims=True)
                parts.append(jnp.exp(masked - peak).astype(BF16))
            values = jnp.concatenate(
                [
                    split_heads(v, low_half, high_half),
                    jnp.concatenate([ones_low, ones_high], axis=0),
                ],
                axis=1,
            )
            both = product(jnp.concatenate(parts, axis=1), values)
            ctx_ref[rows, pl.ds(pair * PAIR, PAIR)] = (both[:, :PAIR] / both[:, PAIR:]).astype(BF16)


def attention_gathered_kernel(length, width, place_ref, x_ref, seg_ref, *rest):
    buffers, (qkv_ref, ctx_ref, w_ref, bias_ref, small_ref, sems) = rest[:10], rest[10:]
    unit = width // 16

    @pl.when(pl.program_id(0) == 0)
    def _():
        copies = []
        for buffer, at, owner, half, first in shard_slots(place_ref, 3):
            source = buffers[buffer].at[at]
            for block in range(3):
                target = w_ref.at[
                    pl.ds(aligned(owner, unit), unit), pl.ds(aligned(half * 3 + block, BLOCK), BLOCK)
                ]
                copies.append((source.at[pl.ds(block * unit, unit)], target))
            if first:
                copies.append((source.at[pl.ds(3 * unit, SMALL)], small_ref.at[owner]))
        run_copies(copies, sems)
        piece = 2 * unit
        lane = lax.broadcasted_iota(jnp.int32, (8, width), 1)
        for part, first in ((0, 0), (2, 8)):
            total = jnp.zeros((8, width), F32)
            for s in range(8):
                row = small_ref[first + s].astype(F32)[:8]
                row = jnp.where(lane < piece, jnp.concatenate([row, row], axis=1), 0.0)
                total = total + (pltpu.roll(row, s * piece, 1) if s else row)
            bias_ref[:, pl.ds(part * width, width)] = total
        bias_ref[:, pl.ds(width, width)] = jnp.zeros((8, width), F32)

    attention_rows(length, width, 0, x_ref, seg_ref, w_ref, bias_ref, qkv_ref, ctx_ref)


def attention_whole_kernel(length, width, first, x_ref, seg_ref, w_ref, bias_ref, *outs):
    attention_rows(length, width, first, x_ref, seg_ref, w_ref, bias_ref, *outs[-2:])


def attention_forward(x, seg, weights, place=None, part=(0, 1), earlier=(), rows_per_step=2):
    row_count, length = seg.shape
    tokens, width = x.shape
    block = rows_per_step * length
    steps = row_count // rows_per_step // part[1]
    first = part[0] * steps
    in_specs = [
        pl.BlockSpec((block, width), lambda i, *_: (i + first, 0)),
        pl.BlockSpec((row_count, length), lambda i, *_: (0, 0)),
    ]
    out_specs = [
        pl.BlockSpec((block, 3 * width), lambda i, *_: (i + first, 0)),
        pl.BlockSpec((block, width), lambda i, *_: (i + first, 0)),
    ]
    out_shape = [
        jax.ShapeDtypeStruct((tokens, 3 * width), BF16),
        jax.ShapeDtypeStruct((tokens, width), BF16),
    ]
    settings = dict(
        compiler_params=pltpu.CompilerParams(vmem_limit_bytes=VMEM_LIMIT),
        cost_estimate=pl.CostEstimate(
            flops=(2 * tokens * width * 3 * width + 8 * tokens * length * width) // part[1],
            bytes_accessed=tokens * width * 10 // part[1] + 6 * width * width,
            transcendentals=tokens * length * (width // HEAD) // part[1],
        ),
        name="attention_forward",
    )
    if place is None:
        in_specs += [
            pl.BlockSpec((width, 3 * width), lambda i: (0, 0), pipeline_mode=pl.Buffered(1)),
            pl.BlockSpec(weights[1].shape, lambda i: (0, 0)),
        ]
        in_specs += [pl.BlockSpec(memory_space=pl.ANY)] * len(earlier)
        return pl.pallas_call(
            functools.partial(attention_whole_kernel, length, width, first),
            grid=(steps,),
            in_specs=in_specs,
            out_specs=out_specs,
            out_shape=out_shape,
            input_output_aliases={4 + n: n for n in range(len(earlier))},
            **settings,
        )(x, seg, *weights, *earlier)
    spec = pltpu.PrefetchScalarGridSpec(
        num_scalar_prefetch=1,
        grid=(steps,),
        in_specs=in_specs + [pl.BlockSpec(memory_space=pl.ANY)] * 10,
        out_specs=out_specs
        + [
            pl.BlockSpec((width, 3 * width), lambda i, *_: (0, 0)),
            pl.BlockSpec((8, 3 * width), lambda i, *_: (0, 0)),
        ],
        scratch_shapes=[
            pltpu.VMEM((16, SMALL, BLOCK), BF16),
            pltpu.SemaphoreType.DMA((112,)),
        ],
    )
    return pl.pallas_call(
        functools.partial(attention_gathered_kernel, length, width),
        grid_spec=spec,
        out_shape=out_shape
        + [
            jax.ShapeDtypeStruct((width, 3 * width), BF16),
            jax.ShapeDtypeStruct((8, 3 * width), F32),
        ],
        **settings,
    )(place, x, seg, *weights)


def feedforward_rows(
    length,
    chunk,
    x_ref,
    ctx_ref,
    seg_ref,
    pooled_grad_ref,
    out_w_ref,
    up_w_ref,
    down_w_ref,
    vec_ref,
    up_bias_ref,
    pooled_ref,
    active_ref,
    hidden_ref,
    normed_ref,
    branch_ref,
    first_ref,
    attended_ref,
    context_ref,
    small_ref,
    up_small_ref,
    slope_ref,
):
    step = pl.program_id(0)
    tokens, width = x_ref.shape
    hidden = up_w_ref.shape[1]
    segments = pooled_grad_ref.shape[1]
    out_bias, gain_one, shift_one = vec_ref[0:1, :], vec_ref[1:2, :], vec_ref[2:3, :]
    down_bias, gain_two, shift_two = vec_ref[3:4, :], vec_ref[4:5, :], vec_ref[5:6, :]

    @pl.when(step == 0)
    def _():
        small_ref[...] = jnp.zeros_like(small_ref)
        up_small_ref[...] = jnp.zeros_like(up_small_ref)

    first_sum = x_ref[...].astype(F32) + product(ctx_ref[...], out_w_ref[...]) + out_bias
    xhat_one, rstd_one = normalise(first_sum)
    normed_one = xhat_one * gain_one + shift_one
    normed_low = normed_one.astype(BF16)
    normed_ref[...] = normed_low
    second_sum = normed_one + down_bias
    for start in range(0, hidden, chunk):
        cols = pl.ds(start, chunk)
        pre = product(normed_low, up_w_ref[:, cols]) + up_bias_ref[:, cols]
        cumulative, tilt = normal_parts(pre)
        active = (pre * cumulative).astype(BF16)
        slope_ref[:, cols] = cumulative + tilt
        active_ref[:, cols] = active
        second_sum = second_sum + product(active, down_w_ref[cols, :])
    xhat_two, rstd_two = normalise(second_sum)
    final = xhat_two * gain_two + shift_two
    final_high = final.astype(BF16)
    final_low = (final - final_high.astype(F32)).astype(BF16)
    token_parts = []
    for local in range(tokens // length):
        rows = slice(local * length, (local + 1) * length)
        along_lanes, along_rows = segment_grid(seg_ref, step * (tokens // length) + local, length)
        index = lax.broadcasted_iota(jnp.int32, (8, length), 0).astype(F32)
        member = (along_lanes[:8, :] == index).astype(F32)
        population = jnp.sum(member, axis=1, keepdims=True)
        member_low = member.astype(BF16)
        sums = product(member_low, final_high[rows]) + product(member_low, final_low[rows])
        pooled_ref[local] = sums[:segments] / population[:segments]
        share = pooled_grad_ref[local] / population[:segments]
        wide = jnp.concatenate([along_rows] * (width // length), axis=1)
        token = jnp.broadcast_to(share[segments - 1 : segments], (length, width))
        for s in range(segments - 2, -1, -1):
            token = jnp.where(wide == float(s), share[s : s + 1], token)
        token_parts.append(token)
    token_grad = jnp.concatenate(token_parts, axis=0)
    second_grad = normalise_back(token_grad, gain_two, xhat_two, rstd_two)
    branch = second_grad.astype(BF16)
    branch_ref[...] = branch
    small_ref[24:32, :] += fold(branch.astype(F32))
    small_ref[32:40, :] += fold(token_grad * xhat_two)
    small_ref[40:48, :] += fold(token_grad)
    normed_grad = second_grad
    for start in range(0, hidden, chunk):
        cols = pl.ds(start, chunk)
        grad = (times_transpose(branch, down_w_ref[cols, :]) * slope_ref[:, cols]).astype(BF16)
        hidden_ref[:, cols] = grad
        up_small_ref[:, cols] += fold(grad.astype(F32))
        normed_grad = normed_grad + times_transpose(grad, up_w_ref[:, cols])
    first_grad = normalise_back(normed_grad, gain_one, xhat_one, rstd_one)
    first_ref[...] = first_grad
    attended = first_grad.astype(BF16)
    attended_ref[...] = attended
    context_ref[...] = times_transpose(attended, out_w_ref[...]).astype(BF16)
    small_ref[0:8, :] += fold(attended.astype(F32))
    small_ref[8:16, :] += fold(normed_grad * xhat_one)
    small_ref[16:24, :] += fold(normed_grad)


def feedforward_gathered_kernel(length, chunk, place_ref, x_ref, ctx_ref, seg_ref, pooled_grad_ref, *rest):
    buffers, outs = rest[:16], rest[16:26]
    slope_ref, out_w_ref, up_w_ref, down_w_ref, vec_ref, up_bias_ref, gathered_ref, sems = rest[26:]
    width, hidden = up_w_ref.shape
    unit = width // 16
    ratio = hidden // width

    @pl.when(pl.program_id(0) == 0)
    def _():
        copies = []
        for buffer, at, owner, half, first in shard_slots(place_ref, 0):
            source = buffers[buffer].at[at]
            rows = pl.ds(aligned(owner, unit), unit)
            for block in range(ratio):
                cols = pl.ds(aligned(half * ratio + block, BLOCK), BLOCK)
                copies.append((source.at[pl.ds(block * unit, unit)], up_w_ref.at[rows, cols]))
            cols = pl.ds(aligned(half, BLOCK), BLOCK)
            down_rows = pl.ds(aligned(owner, ratio * unit), ratio * unit)
            copies.append((source.at[pl.ds(ratio * unit, ratio * unit)], down_w_ref.at[down_rows, cols]))
            copies.append((source.at[pl.ds(2 * ratio * unit, unit)], out_w_ref.at[rows, cols]))
            if first:
                at_small = (2 * ratio + 1) * unit
                copies.append((source.at[pl.ds(at_small, SMALL)], gathered_ref.at[owner]))
        run_copies(copies, sems)
        lane = lax.broadcasted_iota(jnp.int32, (8, width), 1)
        total = jnp.zeros((8, width), F32)
        for s in range(16):
            row = gathered_ref[s].astype(F32)[:8]
            row = jnp.where(lane < unit, jnp.concatenate([row, row], axis=1), 0.0)
            total = total + (pltpu.roll(row, s * unit, 1) if s else row)
        vec_ref[...] = total
        lane = lax.broadcasted_iota(jnp.int32, (8, BLOCK), 1)
        for s in range(0, 16, 2):
            low = gathered_ref[s].astype(F32)[:8]
            high = gathered_ref[s + 1].astype(F32)[:8]
            high = pltpu.roll(high, BLOCK // 2, 1)
            both = jnp.where(lane < BLOCK // 2, low, high)
            up_bias_ref[:, pl.ds((s // 2) * BLOCK, BLOCK)] = both[6:7, :]

    feedforward_rows(
        length, chunk, x_ref, ctx_ref, seg_ref, pooled_grad_ref,
        out_w_ref, up_w_ref, down_w_ref, vec_ref, up_bias_ref, *outs, slope_ref,
    )


def feedforward(x, ctx, seg, pooled_grad, weights, hidden, place=None, rows_per_step=4, chunk=768):
    row_count, length = seg.shape
    tokens, width = x.shape
    segments = pooled_grad.shape[1]
    block = rows_per_step * length

    def tiled(columns):
        return pl.BlockSpec((block, columns), lambda i, *_: (i, 0))

    def whole(shape):
        return pl.BlockSpec(shape, lambda i, *_: (0,) * len(shape), pipeline_mode=pl.Buffered(1))

    def kept(shape):
        return pl.BlockSpec(shape, lambda i, *_: (0,) * len(shape))

    def rows(columns, dtype):
        return jax.ShapeDtypeStruct((tokens, columns), dtype)

    grid = (row_count // rows_per_step,)
    in_specs = [
        tiled(width),
        tiled(width),
        whole((row_count, length)),
        pl.BlockSpec((rows_per_step, segments, width), lambda i, *_: (i, 0, 0)),
    ]
    out_specs = [
        pl.BlockSpec((rows_per_step, segments, width), lambda i, *_: (i, 0, 0)),
        tiled(hidden),
        tiled(hidden),
        tiled(width),
        tiled(width),
        tiled(width),
        tiled(width),
        tiled(width),
        kept((48, width)),
        kept((8, hidden)),
    ]
    out_shape = [
        jax.ShapeDtypeStruct((row_count, segments, width), F32),
        rows(hidden, BF16),
        rows(hidden, BF16),
        rows(width, BF16),
        rows(width, BF16),
        rows(width, F32),
        rows(width, BF16),
        rows(width, BF16),
        jax.ShapeDtypeStruct((48, width), F32),
        jax.ShapeDtypeStruct((8, hidden), F32),
    ]
    settings = dict(
        compiler_params=pltpu.CompilerParams(vmem_limit_bytes=VMEM_LIMIT),
        cost_estimate=pl.CostEstimate(
            flops=tokens * width * (4 * width + 8 * hidden),
            bytes_accessed=tokens * (width * 18 + hidden * 4) + 4 * width * hidden,
            transcendentals=2 * tokens * hidden,
        ),
        name="feedforward",
    )
    slope = pltpu.VMEM((block, hidden), F32)
    if place is None:
        in_specs += [
            whole((width, width)),
            whole((width, hidden)),
            whole((hidden, width)),
            whole((8, width)),
            whole((1, hidden)),
        ]
        return pl.pallas_call(
            functools.partial(feedforward_rows, length, chunk),
            grid=grid,
            in_specs=in_specs,
            out_specs=out_specs,
            out_shape=out_shape,
            scratch_shapes=[slope],
            **settings,
        )(x, ctx, seg, pooled_grad, *weights)
    spec = pltpu.PrefetchScalarGridSpec(
        num_scalar_prefetch=1,
        grid=grid,
        in_specs=in_specs + [pl.BlockSpec(memory_space=pl.ANY)] * 16,
        out_specs=out_specs,
        scratch_shapes=[
            slope,
            pltpu.VMEM((width, width), BF16),
            pltpu.VMEM((width, hidden), BF16),
            pltpu.VMEM((hidden, width), BF16),
            pltpu.VMEM((8, width), F32),
            pltpu.VMEM((1, hidden), F32),
            pltpu.VMEM((16, SMALL, BLOCK), BF16),
            pltpu.SemaphoreType.DMA((32 * (hidden // width + 2) + 16,)),
        ],
    )
    return pl.pallas_call(
        functools.partial(feedforward_gathered_kernel, length, chunk),
        grid_spec=spec,
        out_shape=out_shape,
        **settings,
    )(place, x, ctx, seg, pooled_grad, *weights)


def attention_back_kernel(length, width, first, qkv_ref, grad_ref, seg_ref, *rest):
    out_ref, small_ref = rest[-2:]
    tokens = grad_ref.shape[0]
    step = pl.program_id(0) + first

    @pl.when(pl.program_id(0) == 0)
    def _():
        small_ref[...] = rest[1][...] if first else jnp.zeros_like(small_ref)

    low_half, high_half = lane_halves()
    scale = HEAD**-0.5
    for local in range(tokens // length):
        rows = pl.ds(local * length, length)
        along_lanes, along_rows = segment_grid(seg_ref, step * (tokens // length) + local, length)
        same = along_lanes == along_rows
        same = jnp.concatenate([same, same], axis=1)
        for pair in range(width // PAIR):
            at = (pl.ds(pair * PAIR, PAIR), pl.ds(width + pair * PAIR, PAIR), pl.ds(2 * width + pair * PAIR, PAIR))
            q = split_heads(qkv_ref[rows, at[0]] * BF16(scale), low_half, high_half)
            k = qkv_ref[rows, at[1]]
            v = qkv_ref[rows, at[2]]
            ctx_grad = split_heads(grad_ref[rows, at[0]], low_half, high_half)
            scores = jnp.where(same, times_transpose(k, q), -1e30)
            weights = jnp.exp(scores - jnp.max(scores, axis=0, keepdims=True))
            weights = weights * (1.0 / jnp.sum(weights, axis=0, keepdims=True))
            probs_grad = times_transpose(v, ctx_grad)
            inner = jnp.sum(weights * probs_grad, axis=0, keepdims=True)
            scores_grad = (weights * (probs_grad - inner)).astype(BF16)
            values_grad = product(weights.astype(BF16), ctx_grad).astype(BF16)
            keys_grad = product(scores_grad, q).astype(BF16)
            turned = jnp.concatenate([scores_grad[:, :length].T, scores_grad[:, length:].T], axis=1)
            queries_grad = product(turned, split_heads(k * BF16(scale), low_half, high_half)).astype(BF16)
            out_ref[rows, at[0]] = queries_grad
            out_ref[rows, at[1]] = keys_grad
            out_ref[rows, at[2]] = values_grad
            small_ref[:, at[0]] += fold(queries_grad.astype(F32))
            small_ref[:, at[1]] += fold(values_grad.astype(F32))


def attention_backward(qkv, ctx_grad, seg, part=(0, 1), earlier=(), rows_per_step=2):
    row_count, length = seg.shape
    tokens, width = ctx_grad.shape
    block = rows_per_step * length
    steps = row_count // rows_per_step // part[1]
    first = part[0] * steps
    sums_spec = pl.BlockSpec((8, 2 * width), lambda i: (0, 0))
    return pl.pallas_call(
        functools.partial(attention_back_kernel, length, width, first),
        grid=(steps,),
        in_specs=[
            pl.BlockSpec((block, 3 * width), lambda i: (i + first, 0)),
            pl.BlockSpec((block, width), lambda i: (i + first, 0)),
            pl.BlockSpec((row_count, length), lambda i: (0, 0)),
        ]
        + [pl.BlockSpec(memory_space=pl.ANY), sums_spec][: len(earlier)],
        out_specs=[pl.BlockSpec((block, 3 * width), lambda i: (i + first, 0)), sums_spec],
        out_shape=[
            jax.ShapeDtypeStruct((tokens, 3 * width), BF16),
            jax.ShapeDtypeStruct((8, 2 * width), F32),
        ],
        input_output_aliases={3: 0} if earlier else {},
        compiler_params=pltpu.CompilerParams(vmem_limit_bytes=VMEM_LIMIT),
        cost_estimate=pl.CostEstimate(
            flops=20 * tokens * length * width // part[1],
            bytes_accessed=tokens * width * 14 // part[1],
            transcendentals=tokens * length * (width // HEAD) // part[1],
        ),
        name="attention_backward",
    )(qkv, ctx_grad, seg, *earlier)


def cut_columns(half_index, shard, out_ref, row_at, blocks):
    rows = shard.shape[0]
    for half in range(2):

        @pl.when(half_index == half)
        def _():
            for block in range(blocks):
                cols = pl.ds((half * blocks + block) * BLOCK, BLOCK)
                out_ref[pl.ds(row_at + block * rows, rows), :] = shard[:, cols]


def pack_attention_kernel(place_ref, qkv_ref, small_ref, out_ref):
    unit = qkv_ref.shape[0]
    cut_columns(place_ref[0], qkv_ref, out_ref, 0, 3)
    out_ref[pl.ds(3 * unit, SMALL), :] = small_ref[...]


def pack_feedforward_kernel(place_ref, up_ref, down_ref, out_w_ref, small_ref, out_ref):
    unit = up_ref.shape[0]
    ratio = down_ref.shape[0] // unit
    cut_columns(place_ref[0], up_ref, out_ref, 0, ratio)
    cut_columns(place_ref[0], down_ref, out_ref, ratio * unit, 1)
    cut_columns(place_ref[0], out_w_ref, out_ref, 2 * ratio * unit, 1)
    out_ref[pl.ds((2 * ratio + 1) * unit, SMALL), :] = small_ref[...]


def pack(kernel, name, place, rows, *shards):
    spec = pltpu.PrefetchScalarGridSpec(
        num_scalar_prefetch=1,
        grid=(1,),
        in_specs=[pl.BlockSpec(s.shape, lambda i, *_: (0, 0)) for s in shards],
        out_specs=pl.BlockSpec((rows, BLOCK), lambda i, *_: (0, 0)),
    )
    return pl.pallas_call(
        kernel, grid_spec=spec, out_shape=jax.ShapeDtypeStruct((rows, BLOCK), BF16), name=name
    )(place, *shards)


def store_shards(place_ref, keep_ref, send_ref, plane_z, half, row_at, rows, values):
    y, z, x, core = place_of(place_ref)
    turn = (z - plane_z) & 3
    first = core == 0
    for plane_x in range(2):
        even = values(plane_z * 4 + plane_x * 2)
        odd = values(plane_z * 4 + plane_x * 2 + 1)
        at = (half ^ y, plane_x ^ x, turn, pl.ds(row_at, rows))
        keep_ref[at] = jnp.where(first, even, odd)
        send_ref[at] = jnp.where(first, odd, even)


def down_gradient_kernel(place_ref, active_ref, branch_ref, keep_ref, send_ref):
    grad = transpose_times(active_ref[...], branch_ref[...]).astype(BF16)
    rows = grad.shape[0] // 4
    for half in range(2):

        def values(s):
            return grad[(s % 4) * rows : (s % 4 + 1) * rows, half * BLOCK : (half + 1) * BLOCK]

        y, z, x, core = place_of(place_ref)
        turn = (z - pl.program_id(0)) & 3
        first = core == 0
        for plane_x in range(2):
            even, odd = values(plane_x * 2), values(plane_x * 2 + 1)
            at = (half ^ y, plane_x ^ x, turn)
            keep_ref[at] = jnp.where(first, even, odd)
            send_ref[at] = jnp.where(first, odd, even)


def store_columns(place_ref, keep_ref, send_ref, grad, first_block, blocks):
    unit = grad.shape[0] // 16
    for part in range(2):
        number = first_block + part
        half = number // blocks
        row_at = (number - half * blocks) * unit
        if not isinstance(row_at, int):
            row_at = pl.multiple_of(row_at, unit)

        def values(s):
            return grad[s * unit : (s + 1) * unit, part * BLOCK : (part + 1) * BLOCK]

        for plane_z in range(4):
            store_shards(place_ref, keep_ref, send_ref, plane_z, half, row_at, unit, values)


def store_small(place_ref, keep_ref, send_ref, row_at, values):
    for half in range(2):
        for plane_z in range(4):
            store_shards(place_ref, keep_ref, send_ref, plane_z, half, row_at, SMALL, values)


def up_gradient_kernel(
    place_ref, normed_ref, hidden_ref, ctx_ref, attended_ref, sums_ref, up_sums_ref, keep_ref, send_ref, turned_ref
):
    step = pl.program_id(0)
    last = pl.num_programs(0) - 1
    width = normed_ref.shape[1]
    unit = width // 16
    blocks = last

    @pl.when(step == 0)
    def _():
        turned_ref[...] = normed_ref[...].T

    @pl.when(step < last)
    def _():
        grad = product(turned_ref[...], hidden_ref[...]).astype(BF16)
        store_columns(place_ref, keep_ref, send_ref, grad, 2 * step, blocks)

    @pl.when(step == last)
    def _():
        grad = transpose_times(ctx_ref[...], attended_ref[...]).astype(BF16)
        steps = up_sums_ref.shape[1] // width
        for part in range(2):

            def values(s):
                return grad[s * unit : (s + 1) * unit, part * BLOCK : (part + 1) * BLOCK]

            for plane_z in range(4):
                store_shards(place_ref, keep_ref, send_ref, plane_z, part, steps * unit, unit, values)
        row = lax.broadcasted_iota(jnp.int32, (SMALL, width), 0)
        vectors = jnp.zeros((SMALL, width), F32)
        for number in range(6):
            total = jnp.sum(sums_ref[pl.ds(8 * number, 8), :], axis=0, keepdims=True)
            vectors = jnp.where(row == number, total, vectors)
        up_total = jnp.sum(up_sums_ref[...], axis=0, keepdims=True)
        row = row[:, :BLOCK]

        def small(s):
            rolled = pltpu.roll(vectors, width - s * unit, 1) if s else vectors
            up = jnp.broadcast_to(up_total[:, (s // 2) * BLOCK : (s // 2 + 1) * BLOCK], (SMALL, BLOCK))
            up = pltpu.roll(up, BLOCK // 2, 1) if s % 2 else up
            return jnp.where(row == 6, up, rolled[:, :BLOCK]).astype(BF16)

        store_small(place_ref, keep_ref, send_ref, (steps + 1) * unit, small)


def qkv_gradient_kernel(place_ref, x_ref, grad_ref, sums_ref, keep_ref, send_ref, turned_ref):
    step = pl.program_id(0)
    width = x_ref.shape[1]
    unit = width // 16

    @pl.when(step == 0)
    def _():
        turned_ref[...] = x_ref[...].T
        total = jnp.sum(sums_ref[...], axis=0, keepdims=True)

        def small(s):
            part = total[:, (s // 8) * width : (s // 8 + 1) * width]
            part = jnp.broadcast_to(part, (SMALL, width))
            shift = (s % 8) * 2 * unit
            part = pltpu.roll(part, width - shift, 1) if shift else part
            return part[:, :BLOCK].astype(BF16)

        store_small(place_ref, keep_ref, send_ref, 3 * unit, small)

    grad = product(turned_ref[...], grad_ref[...]).astype(BF16)
    store_columns(place_ref, keep_ref, send_ref, grad, 2 * step, 3)


def weight_gradient(kernel, name, place, rows, steps, arrays, specs, flops, turned=None):
    shape = (2, 2, 4, rows, BLOCK)
    whole = pl.BlockSpec(shape, lambda i, *_: (0,) * 5)
    spec = pltpu.PrefetchScalarGridSpec(
        num_scalar_prefetch=1,
        grid=(steps,),
        in_specs=specs,
        out_specs=[whole, whole],
        scratch_shapes=[] if turned is None else [pltpu.VMEM(turned, BF16)],
    )
    return pl.pallas_call(
        kernel,
        grid_spec=spec,
        out_shape=[jax.ShapeDtypeStruct(shape, BF16)] * 2,
        compiler_params=pltpu.CompilerParams(vmem_limit_bytes=VMEM_LIMIT),
        cost_estimate=pl.CostEstimate(
            flops=flops, bytes_accessed=sum(2 * a.size for a in arrays), transcendentals=0
        ),
        name=name,
    )(place, *arrays)


def resident(shape):
    return pl.BlockSpec(shape, lambda i, *_: (0,) * len(shape), pipeline_mode=pl.Buffered(1))


def input_gradient_kernel(first_ref, grad_ref, w_ref, *outs):
    outs[-1][...] = first_ref[...] + times_transpose(grad_ref[...], w_ref[...])


def input_gradient(first_grad, qkv_grad, matrix, part=(0, 1, 1), earlier=(), rows=512):
    tokens, width = first_grad.shape
    first = tokens // rows * part[0] // part[2]
    steps = tokens // rows * part[1] // part[2] - first
    return pl.pallas_call(
        input_gradient_kernel,
        grid=(steps,),
        in_specs=[
            pl.BlockSpec((rows, width), lambda i: (i + first, 0)),
            pl.BlockSpec((rows, 3 * width), lambda i: (i + first, 0)),
            resident(matrix.shape),
        ]
        + [pl.BlockSpec(memory_space=pl.ANY)] * len(earlier),
        out_specs=pl.BlockSpec((rows, width), lambda i: (i + first, 0)),
        out_shape=jax.ShapeDtypeStruct((tokens, width), F32),
        input_output_aliases={3: 0} if earlier else {},
        compiler_params=pltpu.CompilerParams(vmem_limit_bytes=VMEM_LIMIT),
        cost_estimate=pl.CostEstimate(
            flops=6 * steps * rows * width * width,
            bytes_accessed=14 * steps * rows * width,
            transcendentals=0,
        ),
        name="input_gradient",
    )(first_grad, qkv_grad, matrix, *earlier)


AXES = ("dp", "fsdp")
DEVICES = 32


def across(value, mask):
    return lax.ppermute(value, AXES, [(i, i ^ mask) for i in range(DEVICES)])


def along_z(value, distance):
    def target(i):
        return i - i % 16 + (i % 16 + 4 * distance) % 16

    return lax.ppermute(value, AXES, [(i, target(i)) for i in range(DEVICES)])


CORE, X, Y = 1, 2, 16


def together(*values):
    return lax.optimization_barrier(values)


def shifts(own):
    return tuple(along_z(own, d) for d in (1, 2, 3))


class Reduction:
    def __init__(self, keep, got):
        self.keep, self.got = keep, got

    def pair(self, *at):
        return self.keep[at].astype(F32) + self.got[at].astype(F32)

    def first(self):
        low_x = self.pair(slice(None), 1, slice(0, 2)).astype(BF16)
        high_y = self.pair(1, slice(None), slice(2, 4)).astype(BF16)
        return low_x, high_y

    @staticmethod
    def send_first(values):
        return across(values[0], X), across(values[1], Y)

    def second(self, received):
        low_x, high_y = self.received = received
        low_y = (self.pair(1, 0, slice(0, 2)) + low_x[1].astype(F32)).astype(BF16)
        high_x = (self.pair(0, 1, slice(2, 4)) + high_y[1].astype(F32)).astype(BF16)
        return low_y, high_x

    @staticmethod
    def send_second(values):
        return across(values[0], Y), across(values[1], X)

    def third(self, received):
        low = self.pair(0, 0, slice(0, 2)) + self.received[0][0].astype(F32) + received[0].astype(F32)
        high = self.pair(0, 0, slice(2, 4)) + self.received[1][0].astype(F32) + received[1].astype(F32)
        self.total = low[0]
        return low[1].astype(BF16), high[0].astype(BF16), high[1].astype(BF16)

    @staticmethod
    def send_third(values):
        return tuple(along_z(value, 3 - n) for n, value in enumerate(values))

    def finish(self, received):
        total = self.total
        for part in received:
            total = total + part.astype(F32)
        return total


def both_halves(mine, theirs, y):
    theirs = theirs.astype(F32)
    swap = y == 0
    return jnp.where(swap, mine, theirs), jnp.where(swap, theirs, mine)


def join_columns(halves, unit, blocks):
    parts = []
    for half in halves:
        cols = half.reshape(blocks, unit, BLOCK)
        parts += [cols[b] for b in range(blocks)]
    return jnp.concatenate(parts, axis=1)


def rows_of(vectors, rows):
    padded = [jnp.pad(v, (0, BLOCK - v.shape[0])) for v in vectors]
    padded += [jnp.zeros((BLOCK,), BF16)] * (rows - len(padded))
    return jnp.stack(padded)


def body_by_permutes(
    hidden_in,
    segment_ids,
    pooled_grad,
    qkv_weight,
    qv_bias,
    out_weight,
    out_bias,
    first_gain,
    first_shift,
    up_weight,
    up_bias,
    down_weight,
    down_bias,
    second_gain,
    second_shift,
):
    row_count, length, width = hidden_in.shape
    tokens = row_count * length
    x = hidden_in.reshape(tokens, width)
    unit = qkv_weight.shape[0]
    hidden = up_weight.shape[1]
    ratio = hidden // width
    y, shard = lax.axis_index("dp"), lax.axis_index("fsdp")
    place = jnp.stack([y, shard // 4, shard // 2 % 2, shard % 2]).astype(jnp.int32)

    own_attention = pack(
        pack_attention_kernel,
        "pack_attention",
        place,
        3 * unit + SMALL,
        qkv_weight,
        jnp.pad(qv_bias[None], ((0, SMALL - 1), (0, BLOCK - 2 * unit))),
    )
    vectors = [out_bias, first_gain, first_shift, down_bias, second_gain, second_shift, up_bias]
    own_attention, *vectors = together(own_attention, *vectors)
    own_feedforward = pack(
        pack_feedforward_kernel,
        "pack_feedforward",
        place,
        (2 * ratio + 1) * unit + SMALL,
        up_weight,
        down_weight,
        out_weight,
        rows_of(vectors, SMALL),
    )
    turned = shifts(own_attention)
    own_attention, own_feedforward, *turned = together(own_attention, own_feedforward, *turned)
    here_a = jnp.stack([own_attention, *turned])
    x_a, y_a = across(here_a, X), across(here_a, Y)
    here_a_core = across(here_a, CORE)
    turn_f = along_z(own_feedforward, 1)
    x_a, y_a, own_feedforward, turn_f = together(x_a, y_a, own_feedforward, turn_f)
    low_a, high_a = across(x_a[:2], Y), across(y_a[2:], X)
    x_a_core, y_a_core = across(x_a, CORE), across(y_a, CORE)
    here_low = jnp.stack([own_feedforward, turn_f])
    low_a, high_a, here_low, own_feedforward = together(low_a, high_a, here_low, own_feedforward)
    turn_two, turn_three = along_z(own_feedforward, 2), along_z(own_feedforward, 3)
    attention_pieces = (here_a, x_a, y_a, low_a, high_a)
    attention_pieces += (here_a_core, x_a_core, y_a_core, across(low_a, CORE), across(high_a, CORE))
    here_low, turn_three, *attention_pieces = together(here_low, turn_three, *attention_pieces)
    x_low, y_low = across(here_low, X), across(here_low, Y)
    here_low_core = across(here_low, CORE)
    qkv, ctx, qkv_matrix, qkv_bias = attention_forward(x, segment_ids, attention_pieces, place, (0, 2))
    x_low, y_low, turn_two, qkv, ctx = together(x_low, y_low, turn_two, qkv, ctx)
    here_high, qkv, ctx = together(jnp.stack([turn_two, turn_three]), qkv, ctx)
    x_high, y_high = across(here_high, X), across(here_high, Y)
    x_low_core, y_low_core, here_high_core = across(x_low, CORE), across(y_low, CORE), across(here_high, CORE)
    qkv, ctx = attention_forward(x, segment_ids, (qkv_matrix, qkv_bias), None, (1, 2), (qkv, ctx))
    x_high, y_high, qkv, ctx = together(x_high, y_high, qkv, ctx)
    both_low, both_high = across(x_low, Y), across(y_high, X)
    x_high_core, y_high_core = across(x_high, CORE), across(y_high, CORE)
    feedforward_pieces = (here_low, here_high, x_low, x_high, y_low, y_high, both_low, both_high)
    feedforward_pieces += (here_low_core, here_high_core, x_low_core, x_high_core, y_low_core, y_high_core)
    feedforward_pieces += (across(both_low, CORE), across(both_high, CORE))
    pooled, active, hidden_grad, normed, branch, first_grad, attended, ctx_grad, sums, up_sums = feedforward(
        x, ctx, segment_ids, pooled_grad, feedforward_pieces, hidden, place
    )

    up_keep, up_send = weight_gradient(
        up_gradient_kernel,
        "up_gradient",
        place,
        (ratio + 1) * unit + SMALL,
        ratio + 1,
        (normed, hidden_grad, ctx, attended, sums, up_sums),
        [
            resident((tokens, width)),
            pl.BlockSpec((tokens, width), lambda i, *_: (0, jnp.minimum(i, ratio - 1))),
            resident((tokens, width)),
            resident((tokens, width)),
            resident(sums.shape),
            resident(up_sums.shape),
        ],
        2 * tokens * width * (hidden + width),
        (width, tokens),
    )
    up_keep, up_send, active = together(up_keep, up_send, active)
    up_got = across(up_send, CORE)
    down_keep, down_send = weight_gradient(
        down_gradient_kernel,
        "down_gradient",
        place,
        ratio * unit,
        4,
        (active, branch),
        [pl.BlockSpec((tokens, hidden // 4), lambda i, *_: (0, i)), resident((tokens, width))],
        2 * tokens * hidden * width,
    )
    up_got, down_keep, down_send = together(up_got, down_keep, down_send)
    up = Reduction(up_keep, up_got)
    *up_first, down_send, ctx_grad = together(*up.first(), down_send, ctx_grad)
    up_first = up.send_first(up_first)
    down_got = across(down_send, CORE)
    qkv_grad, qv_sums = attention_backward(qkv, ctx_grad, segment_ids, (0, 2))
    *up_first, down_got, qkv_grad, qv_sums = together(*up_first, down_got, qkv_grad, qv_sums)
    down = Reduction(down_keep, down_got)
    *up_second, low_d, high_d, qv_sums = together(*up.second(up_first), *down.first(), qv_sums)
    up_second = up.send_second(up_second)
    down_first = down.send_first((low_d, high_d))
    qkv_grad, qv_sums = attention_backward(qkv, ctx_grad, segment_ids, (1, 2), (qkv_grad, qv_sums))
    *up_second, low_d, high_d, qkv_grad, qv_sums = together(*up_second, *down_first, qkv_grad, qv_sums)
    u1, u2, u3, low_d, high_d, qv_sums = together(*up.third(up_second), *down.second((low_d, high_d)), qv_sums)
    up_third = up.send_third((u1, u2, u3))
    down_second = down.send_second((low_d, high_d))
    qkv_keep, qkv_send = weight_gradient(
        qkv_gradient_kernel,
        "qkv_gradient",
        place,
        3 * unit + SMALL,
        3,
        (x, qkv_grad, qv_sums),
        [
            resident((tokens, width)),
            pl.BlockSpec((tokens, width), lambda i, *_: (0, i)),
            resident(qv_sums.shape),
        ],
        6 * tokens * width * width,
        (width, tokens),
    )
    *up_third, low_d, high_d, qkv_keep, qkv_send = together(*up_third, *down_second, qkv_keep, qkv_send)
    up_total = up.finish(up_third)
    up_part, up_small = up_total[: (ratio + 1) * unit], up_total[(ratio + 1) * unit :]
    up_half, qkv_send, qkv_grad = together(up_part.astype(BF16), qkv_send, qkv_grad)
    qkv_got = across(qkv_send, CORE)
    up_theirs = across(up_half, Y)
    grad_input = input_gradient(first_grad, qkv_grad, qkv_matrix, (0, 1, 4))
    qkv_got, up_theirs, grad_input = together(qkv_got, up_theirs, grad_input)
    up_low, up_high = both_halves(up_part, up_theirs, y)
    grad_up = join_columns((up_low[: ratio * unit], up_high[: ratio * unit]), unit, ratio)
    grad_out = join_columns((up_low[ratio * unit :], up_high[ratio * unit :]), unit, 1)
    qkv_sum = Reduction(qkv_keep, qkv_got)
    low_q, high_q, d1, d2, d3, grad_up, grad_out, grad_input = together(
        *qkv_sum.first(), *down.third((low_d, high_d)), grad_up, grad_out, grad_input
    )
    qkv_first = qkv_sum.send_first((low_q, high_q))
    down_third = down.send_third((d1, d2, d3))
    grad_input = input_gradient(first_grad, qkv_grad, qkv_matrix, (1, 3, 4), (grad_input,))
    *qkv_first, grad_input = together(*qkv_first, grad_input)
    *qkv_second, grad_input = together(*qkv_sum.second(qkv_first), grad_input)
    qkv_second = qkv_sum.send_second(qkv_second)
    grad_input = input_gradient(first_grad, qkv_grad, qkv_matrix, (3, 4, 4), (grad_input,))
    low_q, high_q, *down_third, grad_input = together(*qkv_second, *down_third, grad_input)
    qkv_second = low_q, high_q
    qkv_third = together(*qkv_sum.third(qkv_second))
    down_total = down.finish(down_third)
    qkv_third = qkv_sum.send_third(qkv_third)
    down_theirs = across(down_total.astype(BF16), Y)
    grad_down = jnp.concatenate(both_halves(down_total, down_theirs, y), axis=1)
    *qkv_third, grad_down = together(*qkv_third, grad_down)
    qkv_total = qkv_sum.finish(qkv_third)
    qkv_part, qkv_small = qkv_total[: 3 * unit], qkv_total[3 * unit :]
    qkv_theirs = across(qkv_part.astype(BF16), Y)
    grad_qkv = join_columns(both_halves(qkv_part, qkv_theirs, y), unit, 3)
    return (
        pooled,
        grad_input.reshape(row_count, length, width),
        grad_qkv,
        qkv_small[0, : 2 * unit],
        grad_out,
        up_small[0, :unit],
        up_small[1, :unit],
        up_small[2, :unit],
        grad_up,
        up_small[6, : ratio * unit],
        grad_down,
        up_small[3, :unit],
        up_small[4, :unit],
        up_small[5, :unit],
    )


def body_by_collectives(
    hidden_in,
    segment_ids,
    pooled_grad,
    qkv_weight,
    qv_bias,
    out_weight,
    out_bias,
    first_gain,
    first_shift,
    up_weight,
    up_bias,
    down_weight,
    down_bias,
    second_gain,
    second_shift,
):
    row_count, length, width = hidden_in.shape
    x = hidden_in.reshape(row_count * length, width)

    def gather(shard):
        return lax.all_gather(shard, "fsdp", axis=0, tiled=True)

    small = jnp.concatenate(
        [qv_bias, out_bias, first_gain, first_shift, up_bias, down_bias, second_gain, second_shift]
    ).astype(BF16)
    small = lax.all_gather(small, "fsdp", axis=0, tiled=False).astype(F32)
    unit = out_bias.shape[0]
    ends = [0]
    for part in (qv_bias, out_bias, first_gain, first_shift, up_bias, down_bias, second_gain, second_shift):
        ends.append(ends[-1] + part.shape[0])
    qv, ob, g1, s1, ub, db, g2, s2 = (small[:, a:b].reshape(1, -1) for a, b in zip(ends[:-1], ends[1:]))
    zeros = jnp.zeros((1, width), F32)
    vectors = jnp.concatenate([ob, g1, s1, db, g2, s2, zeros, zeros], axis=0)
    qkv_bias = jnp.concatenate([qv[:, :width], zeros, qv[:, width:]], axis=1)
    qkv_matrix = gather(qkv_weight)
    out_matrix = gather(out_weight)
    up_matrix = gather(up_weight)
    down_matrix = gather(down_weight)
    qkv, ctx = attention_forward(x, segment_ids, (qkv_matrix, qkv_bias))
    pooled, active, hidden_grad, normed, branch, first_grad, attended, ctx_grad, sums, up_sums = feedforward(
        x, ctx, segment_ids, pooled_grad, (out_matrix, up_matrix, down_matrix, vectors, ub), up_matrix.shape[1]
    )

    def scatter(grad):
        return lax.psum_scatter(grad.astype(BF16), "fsdp", scatter_dimension=0, tiled=True)

    grad_down = scatter(transpose_times(active, branch))
    grad_up = scatter(transpose_times(normed, hidden_grad))
    grad_out = scatter(transpose_times(ctx, attended))
    qkv_grad, qv_sums = attention_backward(qkv, ctx_grad, segment_ids)
    grad_qkv = scatter(transpose_times(x, qkv_grad))
    grad_input = first_grad + times_transpose(qkv_grad, qkv_matrix)
    grad_qkv, grad_out, grad_up, grad_down = lax.psum(
        tuple(g.astype(F32) for g in (grad_qkv, grad_out, grad_up, grad_down)), "dp"
    )
    sums = jnp.sum(sums.reshape(6, 8, width), axis=1)
    vector_sums = jnp.concatenate(
        [jnp.sum(qv_sums, axis=0), sums.reshape(-1), jnp.sum(up_sums, axis=0)]
    )
    vector_sums = lax.psum(vector_sums, ("dp", "fsdp"))
    me = lax.axis_index("fsdp")

    def mine(start, size):
        return lax.dynamic_slice(vector_sums, (start + me * size,), (size,))

    at = 2 * width
    return (
        pooled,
        grad_input.reshape(row_count, length, width),
        grad_qkv,
        mine(0, 2 * unit),
        grad_out,
        mine(at, unit),
        mine(at + width, unit),
        mine(at + 2 * width, unit),
        grad_up,
        mine(at + 6 * width, up_bias.shape[0]),
        grad_down,
        mine(at + 3 * width, unit),
        mine(at + 4 * width, unit),
        mine(at + 5 * width, unit),
    )


def solution(mesh):
    rows = ("dp", "fsdp")
    in_specs = (P(rows, None, None), P(rows, None), P(rows, None, None)) + (
        P("fsdp", None),
        P("fsdp"),
        P("fsdp", None),
        P("fsdp"),
        P("fsdp"),
        P("fsdp"),
        P("fsdp", None),
        P("fsdp"),
        P("fsdp", None),
        P("fsdp"),
        P("fsdp"),
        P("fsdp"),
    )
    out_specs = (
        P(rows, None, None),
        P(rows, None, None),
        P("fsdp", None),
        P("fsdp"),
        P("fsdp", None),
        P("fsdp"),
        P("fsdp"),
        P("fsdp"),
        P("fsdp", None),
        P("fsdp"),
        P("fsdp", None),
        P("fsdp"),
        P("fsdp"),
        P("fsdp"),
    )
    body = body_by_permutes if dict(mesh.shape) == {"dp": 2, "fsdp": 16} else body_by_collectives
    return jax.shard_map(body, mesh=mesh, in_specs=in_specs, out_specs=out_specs, check_vma=False)
```

```python
import functools
import math

import jax
import jax.numpy as jnp
from jax import lax
from jax.experimental import pallas as pl
from jax.experimental.pallas import tpu as pltpu
from jax.sharding import PartitionSpec as P

HEAD = 64
PAIR = 2 * HEAD
EPSILON = 1e-12
F32 = jnp.float32
BF16 = jnp.bfloat16
VMEM_LIMIT = 60000 * 1024
FF_ROWS = 2


def product(left, right):
    return jnp.dot(left, right, preferred_element_type=F32)


def times_transpose(left, right):
    return lax.dot_general(left, right, (((1,), (1,)), ((), ())), preferred_element_type=F32)


def transpose_times(left, right):
    return lax.dot_general(left, right, (((0,), (0,)), ((), ())), preferred_element_type=F32)


def normal_parts(u):
    cumulative = 0.5 + 0.5 * lax.erf(u * math.sqrt(0.5))
    return cumulative, u * (jnp.exp(-0.5 * u * u) * (1.0 / math.sqrt(2.0 * math.pi)))


def normalise(rows):
    average = jnp.mean(rows, axis=-1, keepdims=True)
    centred = rows - average
    variance = jnp.mean(centred * centred, axis=-1, keepdims=True)
    rstd = lax.rsqrt(variance + EPSILON)
    return centred * rstd, rstd


def normalise_back(grad, gain, xhat, rstd):
    e = grad * gain
    mean_e = jnp.mean(e, axis=-1, keepdims=True)
    mean_ex = jnp.mean(e * xhat, axis=-1, keepdims=True)
    return rstd * (e - mean_e - xhat * mean_ex)


def fold(values):
    rows, width = values.shape
    return jnp.sum(values.reshape(rows // 8, 8, width), axis=0)


def interleave(work, first, second, third):
    begun, done = {}, {}
    for number in range(len(work) + 2):
        if number < len(work):
            begun[number] = first(*work[number])
        if 0 <= number - 1 < len(work):
            done[number - 1] = second(*work[number - 1], begun.pop(number - 1))
        if number >= 2:
            third(*work[number - 2], done.pop(number - 2))


def lane_halves():
    lane = lax.broadcasted_iota(jnp.int32, (1, PAIR), 1)
    return (lane < HEAD).astype(BF16), (lane >= HEAD).astype(BF16)


def split_heads(block, low_half, high_half):
    return jnp.concatenate([block * low_half, block * high_half], axis=0)


def segment_grid(seg_ref, row, length):
    ids = seg_ref[pl.ds(row, 1), :].astype(F32)
    along_lanes = jnp.broadcast_to(ids, (length, length))
    return along_lanes, along_lanes.T


BLOCK = 384
SMALL = 16


def place_of(place_ref):
    return place_ref[0], place_ref[1], place_ref[2], place_ref[3]


def shard_slots(place_ref, whole_planes):
    y, z, x, core = place_of(place_ref)
    for other in range(2):
        for plane in range(4):
            for turn in range(4):
                if plane < whole_planes:
                    buffer, at = plane, turn
                else:
                    buffer, at = 2 * plane - whole_planes + turn // 2, turn % 2
                owner = ((z - turn) & 3) * 4 + (x ^ (plane & 1)) * 2 + (core ^ other)
                yield (8 - whole_planes) * other + buffer, at, owner, y ^ (plane >> 1), plane < 2


def run_copies(copies, sems):
    started = []
    for number, (source, target) in enumerate(copies):
        copy = pltpu.make_async_copy(source, target, sems.at[number])
        copy.start()
        started.append(copy)
    for copy in started:
        copy.wait()


def aligned(index, unit):
    return pl.multiple_of(index * unit, unit)


def attention_rows(length, width, first, x_ref, seg_ref, w_ref, bias_ref, qkv_ref, ctx_ref):
    tokens = x_ref.shape[0]
    step = pl.program_id(0) + first
    x = x_ref[...]
    for part in range(3):
        cols = pl.ds(part * width, width)
        qkv_ref[:, cols] = (product(x, w_ref[:, cols]) + bias_ref[0:1, cols]).astype(BF16)
    low_half, high_half = lane_halves()
    ones = jnp.concatenate(
        [jnp.broadcast_to(low_half, (length, PAIR)), jnp.broadcast_to(high_half, (length, PAIR))], axis=0
    )
    scale = HEAD**-0.5
    masks = []
    for local in range(tokens // length):
        along_lanes, along_rows = segment_grid(seg_ref, step * (tokens // length) + local, length)
        masks.append(along_lanes == along_rows)

    def score(local, pair):
        rows = pl.ds(local * length, length)
        q = qkv_ref[rows, pl.ds(pair * PAIR, PAIR)] * BF16(scale)
        k = qkv_ref[rows, pl.ds(width + pair * PAIR, PAIR)]
        return times_transpose(q, split_heads(k, low_half, high_half))

    def weigh(local, pair, scores):
        parts = []
        for half in range(2):
            masked = jnp.where(masks[local], scores[:, half * length : (half + 1) * length], -1e30)
            parts.append(jnp.exp(masked - jnp.max(masked, axis=-1, keepdims=True)).astype(BF16))
        return jnp.concatenate(parts, axis=1)

    def mix(local, pair, weights):
        rows = pl.ds(local * length, length)
        v = qkv_ref[rows, pl.ds(2 * width + pair * PAIR, PAIR)]
        values = jnp.concatenate([split_heads(v, low_half, high_half), ones], axis=1)
        both = product(weights, values)
        ctx_ref[rows, pl.ds(pair * PAIR, PAIR)] = (both[:, :PAIR] / both[:, PAIR:]).astype(BF16)

    interleave([(local, pair) for local in range(tokens // length) for pair in range(width // PAIR)], score, weigh, mix)


def attention_gathered_kernel(length, width, place_ref, x_ref, seg_ref, *rest):
    buffers, (qkv_ref, ctx_ref, w_ref, bias_ref, small_ref, sems) = rest[:10], rest[10:]
    unit = width // 16

    @pl.when(pl.program_id(0) == 0)
    def _():
        copies = []
        for buffer, at, owner, half, first in shard_slots(place_ref, 3):
            source = buffers[buffer].at[at]
            for block in range(3):
                target = w_ref.at[
                    pl.ds(aligned(owner, unit), unit), pl.ds(aligned(half * 3 + block, BLOCK), BLOCK)
                ]
                copies.append((source.at[pl.ds(block * unit, unit)], target))
            if first:
                copies.append((source.at[pl.ds(3 * unit, SMALL)], small_ref.at[owner]))
        run_copies(copies, sems)
        piece = 2 * unit
        lane = lax.broadcasted_iota(jnp.int32, (8, width), 1)
        for part, first in ((0, 0), (2, 8)):
            total = jnp.zeros((8, width), F32)
            for s in range(8):
                row = small_ref[first + s].astype(F32)[:8]
                row = jnp.where(lane < piece, jnp.concatenate([row, row], axis=1), 0.0)
                total = total + (pltpu.roll(row, s * piece, 1) if s else row)
            bias_ref[:, pl.ds(part * width, width)] = total
        bias_ref[:, pl.ds(width, width)] = jnp.zeros((8, width), F32)

    attention_rows(length, width, 0, x_ref, seg_ref, w_ref, bias_ref, qkv_ref, ctx_ref)


def attention_whole_kernel(length, width, first, x_ref, seg_ref, w_ref, bias_ref, *outs):
    attention_rows(length, width, first, x_ref, seg_ref, w_ref, bias_ref, *outs[-2:])


def attention_forward(x, seg, weights, place=None, part=(0, 1), earlier=(), rows_per_step=2):
    row_count, length = seg.shape
    tokens, width = x.shape
    block = rows_per_step * length
    steps = row_count // rows_per_step // part[1]
    first = part[0] * steps
    in_specs = [
        pl.BlockSpec((block, width), lambda i, *_: (i + first, 0)),
        pl.BlockSpec((row_count, length), lambda i, *_: (0, 0)),
    ]
    out_specs = [
        pl.BlockSpec((block, 3 * width), lambda i, *_: (i + first, 0)),
        pl.BlockSpec((block, width), lambda i, *_: (i + first, 0)),
    ]
    out_shape = [
        jax.ShapeDtypeStruct((tokens, 3 * width), BF16),
        jax.ShapeDtypeStruct((tokens, width), BF16),
    ]
    settings = dict(
        compiler_params=pltpu.CompilerParams(vmem_limit_bytes=VMEM_LIMIT),
        cost_estimate=pl.CostEstimate(
            flops=(2 * tokens * width * 3 * width + 8 * tokens * length * width) // part[1],
            bytes_accessed=tokens * width * 10 // part[1] + 6 * width * width,
            transcendentals=tokens * length * (width // HEAD) // part[1],
        ),
        name="attention_forward",
    )
    if place is None:
        in_specs += [
            pl.BlockSpec((width, 3 * width), lambda i: (0, 0), pipeline_mode=pl.Buffered(1)),
            pl.BlockSpec(weights[1].shape, lambda i: (0, 0)),
        ]
        in_specs += [pl.BlockSpec(memory_space=pl.ANY)] * len(earlier)
        return pl.pallas_call(
            functools.partial(attention_whole_kernel, length, width, first),
            grid=(steps,),
            in_specs=in_specs,
            out_specs=out_specs,
            out_shape=out_shape,
            input_output_aliases={4 + n: n for n in range(len(earlier))},
            **settings,
        )(x, seg, *weights, *earlier)
    spec = pltpu.PrefetchScalarGridSpec(
        num_scalar_prefetch=1,
        grid=(steps,),
        in_specs=in_specs + [pl.BlockSpec(memory_space=pl.ANY)] * 10,
        out_specs=out_specs
        + [
            pl.BlockSpec((width, 3 * width), lambda i, *_: (0, 0)),
            pl.BlockSpec((8, 3 * width), lambda i, *_: (0, 0)),
        ],
        scratch_shapes=[
            pltpu.VMEM((16, SMALL, BLOCK), BF16),
            pltpu.SemaphoreType.DMA((112,)),
        ],
    )
    return pl.pallas_call(
        functools.partial(attention_gathered_kernel, length, width),
        grid_spec=spec,
        out_shape=out_shape
        + [
            jax.ShapeDtypeStruct((width, 3 * width), BF16),
            jax.ShapeDtypeStruct((8, 3 * width), F32),
        ],
        **settings,
    )(place, x, seg, *weights)


def feedforward_rows(
    length,
    chunk,
    x_ref,
    ctx_ref,
    seg_ref,
    pooled_grad_ref,
    out_w_ref,
    up_w_ref,
    down_w_ref,
    vec_ref,
    up_bias_ref,
    pooled_ref,
    active_ref,
    hidden_ref,
    normed_ref,
    branch_ref,
    first_ref,
    attended_ref,
    context_ref,
    small_ref,
    up_small_ref,
    slope_ref,
):
    step = pl.program_id(0)
    tokens, width = x_ref.shape
    hidden = up_w_ref.shape[1]
    segments = pooled_grad_ref.shape[1]
    out_bias, gain_one, shift_one = vec_ref[0:1, :], vec_ref[1:2, :], vec_ref[2:3, :]
    down_bias, gain_two, shift_two = vec_ref[3:4, :], vec_ref[4:5, :], vec_ref[5:6, :]

    @pl.when(step == 0)
    def _():
        small_ref[...] = jnp.zeros_like(small_ref)
        up_small_ref[...] = jnp.zeros_like(up_small_ref)

    first_sum = x_ref[...].astype(F32) + product(ctx_ref[...], out_w_ref[...]) + out_bias
    xhat_one, rstd_one = normalise(first_sum)
    normed_one = xhat_one * gain_one + shift_one
    normed_low = normed_one.astype(BF16)
    normed_ref[...] = normed_low
    second_sum = normed_one + down_bias
    for start in range(0, hidden, chunk):
        cols = pl.ds(start, chunk)
        pre = product(normed_low, up_w_ref[:, cols]) + up_bias_ref[:, cols]
        cumulative, tilt = normal_parts(pre)
        active = (pre * cumulative).astype(BF16)
        slope_ref[:, cols] = cumulative + tilt
        active_ref[:, cols] = active
        second_sum = second_sum + product(active, down_w_ref[cols, :])
    xhat_two, rstd_two = normalise(second_sum)
    final = xhat_two * gain_two + shift_two
    final_high = final.astype(BF16)
    final_low = (final - final_high.astype(F32)).astype(BF16)
    token_parts = []
    for local in range(tokens // length):
        rows = slice(local * length, (local + 1) * length)
        along_lanes, along_rows = segment_grid(seg_ref, step * (tokens // length) + local, length)
        index = lax.broadcasted_iota(jnp.int32, (8, length), 0).astype(F32)
        member = (along_lanes[:8, :] == index).astype(F32)
        population = jnp.sum(member, axis=1, keepdims=True)
        member_low = member.astype(BF16)
        sums = product(member_low, final_high[rows]) + product(member_low, final_low[rows])
        pooled_ref[local] = sums[:segments] / population[:segments]
        share = pooled_grad_ref[local] / population[:segments]
        wide = jnp.concatenate([along_rows] * (width // length), axis=1)
        token = jnp.broadcast_to(share[segments - 1 : segments], (length, width))
        for s in range(segments - 2, -1, -1):
            token = jnp.where(wide == float(s), share[s : s + 1], token)
        token_parts.append(token)
    token_grad = jnp.concatenate(token_parts, axis=0)
    second_grad = normalise_back(token_grad, gain_two, xhat_two, rstd_two)
    branch = second_grad.astype(BF16)
    branch_ref[...] = branch
    small_ref[24:32, :] += fold(branch.astype(F32))
    small_ref[32:40, :] += fold(token_grad * xhat_two)
    small_ref[40:48, :] += fold(token_grad)
    normed_grad = second_grad
    for start in range(0, hidden, chunk):
        cols = pl.ds(start, chunk)
        grad = (times_transpose(branch, down_w_ref[cols, :]) * slope_ref[:, cols]).astype(BF16)
        hidden_ref[:, cols] = grad
        up_small_ref[:, cols] += fold(grad.astype(F32))
        normed_grad = normed_grad + times_transpose(grad, up_w_ref[:, cols])
    first_grad = normalise_back(normed_grad, gain_one, xhat_one, rstd_one)
    first_ref[...] = first_grad
    attended = first_grad.astype(BF16)
    attended_ref[...] = attended
    context_ref[...] = times_transpose(attended, out_w_ref[...]).astype(BF16)
    small_ref[0:8, :] += fold(attended.astype(F32))
    small_ref[8:16, :] += fold(normed_grad * xhat_one)
    small_ref[16:24, :] += fold(normed_grad)


def feedforward_gathered_kernel(length, chunk, place_ref, x_ref, ctx_ref, seg_ref, pooled_grad_ref, *rest):
    buffers, outs = rest[:16], rest[16:26]
    slope_ref, out_w_ref, up_w_ref, down_w_ref, vec_ref, up_bias_ref, gathered_ref, sems = rest[26:]
    width, hidden = up_w_ref.shape
    unit = width // 16
    ratio = hidden // width

    @pl.when(pl.program_id(0) == 0)
    def _():
        copies = []
        for buffer, at, owner, half, first in shard_slots(place_ref, 0):
            source = buffers[buffer].at[at]
            rows = pl.ds(aligned(owner, unit), unit)
            for block in range(ratio):
                cols = pl.ds(aligned(half * ratio + block, BLOCK), BLOCK)
                copies.append((source.at[pl.ds(block * unit, unit)], up_w_ref.at[rows, cols]))
            cols = pl.ds(aligned(half, BLOCK), BLOCK)
            down_rows = pl.ds(aligned(owner, ratio * unit), ratio * unit)
            copies.append((source.at[pl.ds(ratio * unit, ratio * unit)], down_w_ref.at[down_rows, cols]))
            copies.append((source.at[pl.ds(2 * ratio * unit, unit)], out_w_ref.at[rows, cols]))
            if first:
                at_small = (2 * ratio + 1) * unit
                copies.append((source.at[pl.ds(at_small, SMALL)], gathered_ref.at[owner]))
        run_copies(copies, sems)
        lane = lax.broadcasted_iota(jnp.int32, (8, width), 1)
        total = jnp.zeros((8, width), F32)
        for s in range(16):
            row = gathered_ref[s].astype(F32)[:8]
            row = jnp.where(lane < unit, jnp.concatenate([row, row], axis=1), 0.0)
            total = total + (pltpu.roll(row, s * unit, 1) if s else row)
        vec_ref[...] = total
        lane = lax.broadcasted_iota(jnp.int32, (8, BLOCK), 1)
        for s in range(0, 16, 2):
            low = gathered_ref[s].astype(F32)[:8]
            high = gathered_ref[s + 1].astype(F32)[:8]
            high = pltpu.roll(high, BLOCK // 2, 1)
            both = jnp.where(lane < BLOCK // 2, low, high)
            up_bias_ref[:, pl.ds((s // 2) * BLOCK, BLOCK)] = both[6:7, :]

    feedforward_rows(
        length, chunk, x_ref, ctx_ref, seg_ref, pooled_grad_ref,
        out_w_ref, up_w_ref, down_w_ref, vec_ref, up_bias_ref, *outs, slope_ref,
    )


def feedforward(x, ctx, seg, pooled_grad, weights, hidden, place=None, rows_per_step=FF_ROWS, chunk=768):
    row_count, length = seg.shape
    tokens, width = x.shape
    segments = pooled_grad.shape[1]
    block = rows_per_step * length

    def tiled(columns):
        return pl.BlockSpec((block, columns), lambda i, *_: (i, 0))

    def whole(shape):
        return pl.BlockSpec(shape, lambda i, *_: (0,) * len(shape), pipeline_mode=pl.Buffered(1))

    def kept(shape):
        return pl.BlockSpec(shape, lambda i, *_: (0,) * len(shape))

    def rows(columns, dtype):
        return jax.ShapeDtypeStruct((tokens, columns), dtype)

    grid = (row_count // rows_per_step,)
    in_specs = [
        tiled(width),
        tiled(width),
        whole((row_count, length)),
        pl.BlockSpec((rows_per_step, segments, width), lambda i, *_: (i, 0, 0)),
    ]
    out_specs = [
        pl.BlockSpec((rows_per_step, segments, width), lambda i, *_: (i, 0, 0)),
        tiled(hidden),
        tiled(hidden),
        tiled(width),
        tiled(width),
        tiled(width),
        tiled(width),
        tiled(width),
        kept((48, width)),
        kept((8, hidden)),
    ]
    out_shape = [
        jax.ShapeDtypeStruct((row_count, segments, width), F32),
        rows(hidden, BF16),
        rows(hidden, BF16),
        rows(width, BF16),
        rows(width, BF16),
        rows(width, F32),
        rows(width, BF16),
        rows(width, BF16),
        jax.ShapeDtypeStruct((48, width), F32),
        jax.ShapeDtypeStruct((8, hidden), F32),
    ]
    settings = dict(
        compiler_params=pltpu.CompilerParams(vmem_limit_bytes=VMEM_LIMIT),
        cost_estimate=pl.CostEstimate(
            flops=tokens * width * (4 * width + 8 * hidden),
            bytes_accessed=tokens * (width * 18 + hidden * 4) + 4 * width * hidden,
            transcendentals=2 * tokens * hidden,
        ),
        name="feedforward",
    )
    slope = pltpu.VMEM((block, hidden), F32)
    if place is None:
        in_specs += [
            whole((width, width)),
            whole((width, hidden)),
            whole((hidden, width)),
            whole((8, width)),
            whole((1, hidden)),
        ]
        return pl.pallas_call(
            functools.partial(feedforward_rows, length, chunk),
            grid=grid,
            in_specs=in_specs,
            out_specs=out_specs,
            out_shape=out_shape,
            scratch_shapes=[slope],
            **settings,
        )(x, ctx, seg, pooled_grad, *weights)
    spec = pltpu.PrefetchScalarGridSpec(
        num_scalar_prefetch=1,
        grid=grid,
        in_specs=in_specs + [pl.BlockSpec(memory_space=pl.ANY)] * 16,
        out_specs=out_specs,
        scratch_shapes=[
            slope,
            pltpu.VMEM((width, width), BF16),
            pltpu.VMEM((width, hidden), BF16),
            pltpu.VMEM((hidden, width), BF16),
            pltpu.VMEM((8, width), F32),
            pltpu.VMEM((1, hidden), F32),
            pltpu.VMEM((16, SMALL, BLOCK), BF16),
            pltpu.SemaphoreType.DMA((32 * (hidden // width + 2) + 16,)),
        ],
    )
    return pl.pallas_call(
        functools.partial(feedforward_gathered_kernel, length, chunk),
        grid_spec=spec,
        out_shape=out_shape,
        **settings,
    )(place, x, ctx, seg, pooled_grad, *weights)


def resident(shape):
    return pl.BlockSpec(shape, lambda i, *_: (0,) * len(shape), pipeline_mode=pl.Buffered(1))


def attention_back_kernel(length, width, first, qkv_ref, grad_ref, seg_ref, *rest):
    out_ref, small_ref = rest[-2:]
    tokens = grad_ref.shape[0]
    step = pl.program_id(0) + first

    @pl.when(pl.program_id(0) == 0)
    def _():
        small_ref[...] = rest[1][...] if first else jnp.zeros_like(small_ref)

    low_half, high_half = lane_halves()
    scale = BF16(HEAD**-0.5)
    masks = []
    for local in range(tokens // length):
        along_lanes, along_rows = segment_grid(seg_ref, step * (tokens // length) + local, length)
        same = along_lanes == along_rows
        masks.append(jnp.concatenate([same, same], axis=1))

    def load(ref, local, part, pair):
        return ref[pl.ds(local * length, length), pl.ds(part * width + pair * PAIR, PAIR)]

    def split(block):
        return split_heads(block, low_half, high_half)

    def score(local, pair):
        q = split(load(qkv_ref, local, 0, pair) * scale)
        ctx_grad = split(load(grad_ref, local, 0, pair))
        k, v = load(qkv_ref, local, 1, pair), load(qkv_ref, local, 2, pair)
        return times_transpose(k, q), times_transpose(v, ctx_grad)

    def weigh(local, pair, products):
        scores, probs_grad = products
        scores = jnp.where(masks[local], scores, -1e30)
        weights = jnp.exp(scores - jnp.max(scores, axis=0, keepdims=True))
        weights = weights * (1.0 / jnp.sum(weights, axis=0, keepdims=True))
        inner = jnp.sum(weights * probs_grad, axis=0, keepdims=True)
        scores_grad = (weights * (probs_grad - inner)).astype(BF16)
        turned = jnp.concatenate([scores_grad[:, :length].T, scores_grad[:, length:].T], axis=1)
        return weights.astype(BF16), scores_grad, turned

    def mix(local, pair, found):
        weights, scores_grad, turned = found
        values_grad = product(weights, split(load(grad_ref, local, 0, pair))).astype(BF16)
        keys_grad = product(scores_grad, split(load(qkv_ref, local, 0, pair) * scale)).astype(BF16)
        queries_grad = product(turned, split(load(qkv_ref, local, 1, pair) * scale)).astype(BF16)
        rows = pl.ds(local * length, length)
        for part, grad in enumerate((queries_grad, keys_grad, values_grad)):
            out_ref[rows, pl.ds(part * width + pair * PAIR, PAIR)] = grad
        small_ref[:, pl.ds(pair * PAIR, PAIR)] += fold(queries_grad.astype(F32))
        small_ref[:, pl.ds(width + pair * PAIR, PAIR)] += fold(values_grad.astype(F32))

    interleave([(local, pair) for local in range(tokens // length) for pair in range(width // PAIR)], score, weigh, mix)


def attention_backward(qkv, ctx_grad, seg, part=(0, 1), earlier=(), rows_per_step=2):
    row_count, length = seg.shape
    tokens, width = ctx_grad.shape
    block = rows_per_step * length
    steps = row_count // rows_per_step // part[1]
    first = part[0] * steps
    sums_spec = pl.BlockSpec((8, 2 * width), lambda i: (0, 0))
    return pl.pallas_call(
        functools.partial(attention_back_kernel, length, width, first),
        grid=(steps,),
        in_specs=[
            pl.BlockSpec((block, 3 * width), lambda i: (i + first, 0)),
            pl.BlockSpec((block, width), lambda i: (i + first, 0)),
            pl.BlockSpec((row_count, length), lambda i: (0, 0)),
        ]
        + [pl.BlockSpec(memory_space=pl.ANY), sums_spec][: len(earlier)],
        out_specs=[pl.BlockSpec((block, 3 * width), lambda i: (i + first, 0)), sums_spec],
        out_shape=[
            jax.ShapeDtypeStruct((tokens, 3 * width), BF16),
            jax.ShapeDtypeStruct((8, 2 * width), F32),
        ],
        input_output_aliases={3: 0} if earlier else {},
        compiler_params=pltpu.CompilerParams(vmem_limit_bytes=VMEM_LIMIT),
        cost_estimate=pl.CostEstimate(
            flops=20 * tokens * length * width // part[1],
            bytes_accessed=tokens * width * 14 // part[1],
            transcendentals=tokens * length * (width // HEAD) // part[1],
        ),
        name="attention_backward",
    )(qkv, ctx_grad, seg, *earlier)


def cut_columns(half_index, shard, out_ref, row_at, blocks):
    rows = shard.shape[0]
    for half in range(2):

        @pl.when(half_index == half)
        def _():
            for block in range(blocks):
                cols = pl.ds((half * blocks + block) * BLOCK, BLOCK)
                out_ref[pl.ds(row_at + block * rows, rows), :] = shard[:, cols]


def pack_attention_kernel(place_ref, qkv_ref, small_ref, out_ref):
    unit = qkv_ref.shape[0]
    cut_columns(place_ref[0], qkv_ref, out_ref, 0, 3)
    out_ref[pl.ds(3 * unit, SMALL), :] = small_ref[...]


def pack_feedforward_kernel(place_ref, up_ref, down_ref, out_w_ref, small_ref, out_ref):
    unit = up_ref.shape[0]
    ratio = down_ref.shape[0] // unit
    cut_columns(place_ref[0], up_ref, out_ref, 0, ratio)
    cut_columns(place_ref[0], down_ref, out_ref, ratio * unit, 1)
    cut_columns(place_ref[0], out_w_ref, out_ref, 2 * ratio * unit, 1)
    out_ref[pl.ds((2 * ratio + 1) * unit, SMALL), :] = small_ref[...]


def pack(kernel, name, place, rows, *shards):
    spec = pltpu.PrefetchScalarGridSpec(
        num_scalar_prefetch=1,
        grid=(1,),
        in_specs=[pl.BlockSpec(s.shape, lambda i, *_: (0, 0)) for s in shards],
        out_specs=pl.BlockSpec((rows, BLOCK), lambda i, *_: (0, 0)),
    )
    return pl.pallas_call(
        kernel, grid_spec=spec, out_shape=jax.ShapeDtypeStruct((rows, BLOCK), BF16), name=name
    )(place, *shards)


def store_shards(place_ref, keep_ref, send_ref, plane_z, half, row_at, rows, values):
    y, z, x, core = place_of(place_ref)
    turn = (z - plane_z) & 3
    first = core == 0
    for plane_x in range(2):
        even = values(plane_z * 4 + plane_x * 2)
        odd = values(plane_z * 4 + plane_x * 2 + 1)
        at = (half ^ y, plane_x ^ x, turn, pl.ds(row_at, rows))
        keep_ref[at] = jnp.where(first, even, odd)
        send_ref[at] = jnp.where(first, odd, even)


def down_gradient_kernel(place_ref, active_ref, branch_ref, keep_ref, send_ref):
    grad = transpose_times(active_ref[...], branch_ref[...]).astype(BF16)
    rows = grad.shape[0] // 4
    for half in range(2):

        def values(s):
            return grad[(s % 4) * rows : (s % 4 + 1) * rows, half * BLOCK : (half + 1) * BLOCK]

        y, z, x, core = place_of(place_ref)
        turn = (z - pl.program_id(0)) & 3
        first = core == 0
        for plane_x in range(2):
            even, odd = values(plane_x * 2), values(plane_x * 2 + 1)
            at = (half ^ y, plane_x ^ x, turn)
            keep_ref[at] = jnp.where(first, even, odd)
            send_ref[at] = jnp.where(first, odd, even)


def store_columns(place_ref, keep_ref, send_ref, grad, first_block, blocks):
    unit = grad.shape[0] // 16
    for part in range(2):
        number = first_block + part
        half = number // blocks
        row_at = (number - half * blocks) * unit
        if not isinstance(row_at, int):
            row_at = pl.multiple_of(row_at, unit)

        def values(s):
            return grad[s * unit : (s + 1) * unit, part * BLOCK : (part + 1) * BLOCK]

        for plane_z in range(4):
            store_shards(place_ref, keep_ref, send_ref, plane_z, half, row_at, unit, values)


def store_small(place_ref, keep_ref, send_ref, row_at, values):
    for half in range(2):
        for plane_z in range(4):
            store_shards(place_ref, keep_ref, send_ref, plane_z, half, row_at, SMALL, values)


def up_gradient_kernel(
    place_ref, normed_ref, hidden_ref, ctx_ref, attended_ref, sums_ref, up_sums_ref, keep_ref, send_ref, turned_ref
):
    step = pl.program_id(0)
    last = pl.num_programs(0) - 1
    width = normed_ref.shape[1]
    unit = width // 16
    blocks = last

    @pl.when(step == 0)
    def _():
        turned_ref[...] = normed_ref[...].T

    @pl.when(step < last)
    def _():
        grad = product(turned_ref[...], hidden_ref[...]).astype(BF16)
        store_columns(place_ref, keep_ref, send_ref, grad, 2 * step, blocks)

    @pl.when(step == last)
    def _():
        grad = transpose_times(ctx_ref[...], attended_ref[...]).astype(BF16)
        steps = up_sums_ref.shape[1] // width
        for part in range(2):

            def values(s):
                return grad[s * unit : (s + 1) * unit, part * BLOCK : (part + 1) * BLOCK]

            for plane_z in range(4):
                store_shards(place_ref, keep_ref, send_ref, plane_z, part, steps * unit, unit, values)
        row = lax.broadcasted_iota(jnp.int32, (SMALL, width), 0)
        vectors = jnp.zeros((SMALL, width), F32)
        for number in range(6):
            total = jnp.sum(sums_ref[pl.ds(8 * number, 8), :], axis=0, keepdims=True)
            vectors = jnp.where(row == number, total, vectors)
        up_total = jnp.sum(up_sums_ref[...], axis=0, keepdims=True)
        row = row[:, :BLOCK]

        def small(s):
            rolled = pltpu.roll(vectors, width - s * unit, 1) if s else vectors
            up = jnp.broadcast_to(up_total[:, (s // 2) * BLOCK : (s // 2 + 1) * BLOCK], (SMALL, BLOCK))
            up = pltpu.roll(up, BLOCK // 2, 1) if s % 2 else up
            return jnp.where(row == 6, up, rolled[:, :BLOCK]).astype(BF16)

        store_small(place_ref, keep_ref, send_ref, (steps + 1) * unit, small)


def qkv_gradient_kernel(place_ref, x_ref, grad_ref, sums_ref, keep_ref, send_ref, turned_ref):
    step = pl.program_id(0)
    width = x_ref.shape[1]
    unit = width // 16

    @pl.when(step == 0)
    def _():
        turned_ref[...] = x_ref[...].T
        total = jnp.sum(sums_ref[...], axis=0, keepdims=True)

        def small(s):
            part = total[:, (s // 8) * width : (s // 8 + 1) * width]
            part = jnp.broadcast_to(part, (SMALL, width))
            shift = (s % 8) * 2 * unit
            part = pltpu.roll(part, width - shift, 1) if shift else part
            return part[:, :BLOCK].astype(BF16)

        store_small(place_ref, keep_ref, send_ref, 3 * unit, small)

    grad = product(turned_ref[...], grad_ref[...]).astype(BF16)
    store_columns(place_ref, keep_ref, send_ref, grad, 2 * step, 3)


def weight_gradient(kernel, name, place, rows, steps, arrays, specs, flops, turned=None):
    shape = (2, 2, 4, rows, BLOCK)
    whole = pl.BlockSpec(shape, lambda i, *_: (0,) * 5)
    spec = pltpu.PrefetchScalarGridSpec(
        num_scalar_prefetch=1,
        grid=(steps,),
        in_specs=specs,
        out_specs=[whole, whole],
        scratch_shapes=[] if turned is None else [pltpu.VMEM(turned, BF16)],
    )
    return pl.pallas_call(
        kernel,
        grid_spec=spec,
        out_shape=[jax.ShapeDtypeStruct(shape, BF16)] * 2,
        compiler_params=pltpu.CompilerParams(vmem_limit_bytes=VMEM_LIMIT),
        cost_estimate=pl.CostEstimate(
            flops=flops, bytes_accessed=sum(2 * a.size for a in arrays), transcendentals=0
        ),
        name=name,
    )(place, *arrays)


def input_gradient_kernel(first_ref, grad_ref, w_ref, *outs):
    outs[-1][...] = first_ref[...] + times_transpose(grad_ref[...], w_ref[...])


def input_gradient(first_grad, qkv_grad, matrix, part=(0, 1, 1), earlier=(), rows=256):
    tokens, width = first_grad.shape
    first = tokens // rows * part[0] // part[2]
    steps = tokens // rows * part[1] // part[2] - first
    return pl.pallas_call(
        input_gradient_kernel,
        grid=(steps,),
        in_specs=[
            pl.BlockSpec((rows, width), lambda i: (i + first, 0)),
            pl.BlockSpec((rows, 3 * width), lambda i: (i + first, 0)),
            resident(matrix.shape),
        ]
        + [pl.BlockSpec(memory_space=pl.ANY)] * len(earlier),
        out_specs=pl.BlockSpec((rows, width), lambda i: (i + first, 0)),
        out_shape=jax.ShapeDtypeStruct((tokens, width), F32),
        input_output_aliases={3: 0} if earlier else {},
        compiler_params=pltpu.CompilerParams(vmem_limit_bytes=VMEM_LIMIT),
        cost_estimate=pl.CostEstimate(
            flops=6 * steps * rows * width * width,
            bytes_accessed=14 * steps * rows * width,
            transcendentals=0,
        ),
        name="input_gradient",
    )(first_grad, qkv_grad, matrix, *earlier)


AXES = ("dp", "fsdp")
DEVICES = 32
CORE, X, Y = 1, 2, 16


def across(value, mask):
    return lax.ppermute(value, AXES, [(i, i ^ mask) for i in range(DEVICES)])


def along_z(value, distance):
    def target(i):
        return i - i % 16 + (i % 16 + 4 * distance) % 16

    return lax.ppermute(value, AXES, [(i, target(i)) for i in range(DEVICES)])


def together(*values):
    return lax.optimization_barrier(values)


def shifts(own):
    return tuple(along_z(own, d) for d in (1, 2, 3))


class Reduction:
    def __init__(self, keep, got):
        self.keep, self.got = keep, got

    def pair(self, *at):
        return self.keep[at].astype(F32) + self.got[at].astype(F32)

    def first(self):
        low_x = self.pair(slice(None), 1, slice(0, 2)).astype(BF16)
        high_y = self.pair(1, slice(None), slice(2, 4)).astype(BF16)
        return low_x, high_y

    @staticmethod
    def send_first(values):
        return across(values[0], X), across(values[1], Y)

    def second(self, received):
        low_x, high_y = self.received = received
        low_y = (self.pair(1, 0, slice(0, 2)) + low_x[1].astype(F32)).astype(BF16)
        high_x = (self.pair(0, 1, slice(2, 4)) + high_y[1].astype(F32)).astype(BF16)
        return low_y, high_x

    @staticmethod
    def send_second(values):
        return across(values[0], Y), across(values[1], X)

    def third(self, received):
        low = self.pair(0, 0, slice(0, 2)) + self.received[0][0].astype(F32) + received[0].astype(F32)
        high = self.pair(0, 0, slice(2, 4)) + self.received[1][0].astype(F32) + received[1].astype(F32)
        self.total = low[0]
        return low[1].astype(BF16), high[0].astype(BF16), high[1].astype(BF16)

    @staticmethod
    def send_third(values):
        return tuple(along_z(value, 3 - n) for n, value in enumerate(values))

    def finish(self, received):
        total = self.total
        for part in received:
            total = total + part.astype(F32)
        return total


def both_halves(mine, theirs, y):
    theirs = theirs.astype(F32)
    swap = y == 0
    return jnp.where(swap, mine, theirs), jnp.where(swap, theirs, mine)


def join_columns(halves, unit, blocks):
    parts = []
    for half in halves:
        cols = half.reshape(blocks, unit, BLOCK)
        parts += [cols[b] for b in range(blocks)]
    return jnp.concatenate(parts, axis=1)


def rows_of(vectors, rows):
    padded = [jnp.pad(v, (0, BLOCK - v.shape[0])) for v in vectors]
    padded += [jnp.zeros((BLOCK,), BF16)] * (rows - len(padded))
    return jnp.stack(padded)


def body_by_permutes(
    hidden_in,
    segment_ids,
    pooled_grad,
    qkv_weight,
    qv_bias,
    out_weight,
    out_bias,
    first_gain,
    first_shift,
    up_weight,
    up_bias,
    down_weight,
    down_bias,
    second_gain,
    second_shift,
):
    row_count, length, width = hidden_in.shape
    tokens = row_count * length
    x = hidden_in.reshape(tokens, width)
    unit = qkv_weight.shape[0]
    hidden = up_weight.shape[1]
    ratio = hidden // width
    y, shard = lax.axis_index("dp"), lax.axis_index("fsdp")
    place = jnp.stack([y, shard // 4, shard // 2 % 2, shard % 2]).astype(jnp.int32)

    own_attention = pack(
        pack_attention_kernel,
        "pack_attention",
        place,
        3 * unit + SMALL,
        qkv_weight,
        jnp.pad(qv_bias[None], ((0, SMALL - 1), (0, BLOCK - 2 * unit))),
    )
    vectors = [out_bias, first_gain, first_shift, down_bias, second_gain, second_shift, up_bias]
    own_attention, *vectors = together(own_attention, *vectors)
    own_feedforward = pack(
        pack_feedforward_kernel,
        "pack_feedforward",
        place,
        (2 * ratio + 1) * unit + SMALL,
        up_weight,
        down_weight,
        out_weight,
        rows_of(vectors, SMALL),
    )
    turned = shifts(own_attention)
    own_attention, own_feedforward, *turned = together(own_attention, own_feedforward, *turned)
    here_a = jnp.stack([own_attention, *turned])
    x_a, y_a = across(here_a, X), across(here_a, Y)
    here_a_core = across(here_a, CORE)
    turn_f = along_z(own_feedforward, 1)
    x_a, y_a, own_feedforward, turn_f = together(x_a, y_a, own_feedforward, turn_f)
    low_a, high_a = across(x_a[:2], Y), across(y_a[2:], X)
    x_a_core, y_a_core = across(x_a, CORE), across(y_a, CORE)
    here_low = jnp.stack([own_feedforward, turn_f])
    low_a, high_a, here_low, own_feedforward = together(low_a, high_a, here_low, own_feedforward)
    turn_two, turn_three = along_z(own_feedforward, 2), along_z(own_feedforward, 3)
    attention_pieces = (here_a, x_a, y_a, low_a, high_a)
    attention_pieces += (here_a_core, x_a_core, y_a_core, across(low_a, CORE), across(high_a, CORE))
    here_low, turn_three, *attention_pieces = together(here_low, turn_three, *attention_pieces)
    x_low, y_low = across(here_low, X), across(here_low, Y)
    here_low_core = across(here_low, CORE)
    qkv, ctx, qkv_matrix, qkv_bias = attention_forward(x, segment_ids, attention_pieces, place, (0, 2))
    x_low, y_low, turn_two, qkv, ctx = together(x_low, y_low, turn_two, qkv, ctx)
    here_high, qkv, ctx = together(jnp.stack([turn_two, turn_three]), qkv, ctx)
    x_high, y_high = across(here_high, X), across(here_high, Y)
    x_low_core, y_low_core, here_high_core = across(x_low, CORE), across(y_low, CORE), across(here_high, CORE)
    qkv, ctx = attention_forward(x, segment_ids, (qkv_matrix, qkv_bias), None, (1, 2), (qkv, ctx))
    x_high, y_high, qkv, ctx = together(x_high, y_high, qkv, ctx)
    both_low, both_high = across(x_low, Y), across(y_high, X)
    x_high_core, y_high_core = across(x_high, CORE), across(y_high, CORE)
    feedforward_pieces = (here_low, here_high, x_low, x_high, y_low, y_high, both_low, both_high)
    feedforward_pieces += (here_low_core, here_high_core, x_low_core, x_high_core, y_low_core, y_high_core)
    feedforward_pieces += (across(both_low, CORE), across(both_high, CORE))
    pooled, active, hidden_grad, normed, branch, first_grad, attended, ctx_grad, sums, up_sums = feedforward(
        x, ctx, segment_ids, pooled_grad, feedforward_pieces, hidden, place
    )

    up_keep, up_send = weight_gradient(
        up_gradient_kernel,
        "up_gradient",
        place,
        (ratio + 1) * unit + SMALL,
        ratio + 1,
        (normed, hidden_grad, ctx, attended, sums, up_sums),
        [
            resident((tokens, width)),
            pl.BlockSpec((tokens, width), lambda i, *_: (0, jnp.minimum(i, ratio - 1))),
            resident((tokens, width)),
            resident((tokens, width)),
            resident(sums.shape),
            resident(up_sums.shape),
        ],
        2 * tokens * width * (hidden + width),
        (width, tokens),
    )
    up_keep, up_send, active = together(up_keep, up_send, active)
    up_got = across(up_send, CORE)
    down_keep, down_send = weight_gradient(
        down_gradient_kernel,
        "down_gradient",
        place,
        ratio * unit,
        4,
        (active, branch),
        [pl.BlockSpec((tokens, hidden // 4), lambda i, *_: (0, i)), resident((tokens, width))],
        2 * tokens * hidden * width,
    )
    up_got, down_keep, down_send = together(up_got, down_keep, down_send)
    up = Reduction(up_keep, up_got)
    low_u, high_u, down_send, ctx_grad = together(*up.first(), down_send, ctx_grad)
    up_first = up.send_first((low_u, high_u))
    down_got = across(down_send, CORE)
    qkv_grad, qv_sums = attention_backward(qkv, ctx_grad, segment_ids)
    low_u, high_u, down_got, qkv_grad, qv_sums = together(*up_first, down_got, qkv_grad, qv_sums)
    down = Reduction(down_keep, down_got)
    low_u, high_u, low_d, high_d, qv_sums = together(*up.second((low_u, high_u)), *down.first(), qv_sums)
    up_second = up.send_second((low_u, high_u))
    down_first = down.send_first((low_d, high_d))
    qkv_keep, qkv_send = weight_gradient(
        qkv_gradient_kernel,
        "qkv_gradient",
        place,
        3 * unit + SMALL,
        3,
        (x, qkv_grad, qv_sums),
        [
            resident((tokens, width)),
            pl.BlockSpec((tokens, width), lambda i, *_: (0, i)),
            resident(qv_sums.shape),
        ],
        6 * tokens * width * width,
        (width, tokens),
    )
    low_u, high_u, qkv_keep, qkv_send = together(*up_second, qkv_keep, qkv_send)
    u1, u2, u3, qkv_send, qkv_grad = together(*up.third((low_u, high_u)), qkv_send, qkv_grad)
    up_third = up.send_third((u1, u2, u3))
    qkv_got = across(qkv_send, CORE)
    grad_input = input_gradient(first_grad, qkv_grad, qkv_matrix, (0, 1, 4))
    low_d, high_d, qkv_got, grad_input = together(*down_first, qkv_got, grad_input)
    qkv_sum = Reduction(qkv_keep, qkv_got)
    low_d, high_d, low_q, high_q, grad_input = together(*down.second((low_d, high_d)), *qkv_sum.first(), grad_input)
    down_second = down.send_second((low_d, high_d))
    qkv_first = qkv_sum.send_first((low_q, high_q))
    grad_input = input_gradient(first_grad, qkv_grad, qkv_matrix, (1, 3, 4), (grad_input,))
    low_d, high_d, low_q, high_q, *up_third, grad_input = together(*down_second, *qkv_first, *up_third, grad_input)
    d1, d2, d3, low_q, high_q, grad_input = together(
        *down.third((low_d, high_d)), *qkv_sum.second((low_q, high_q)), grad_input
    )
    qkv_second = qkv_sum.send_second((low_q, high_q))
    down_third = down.send_third((d1, d2, d3))
    up_total = up.finish(up_third)
    up_part, up_small = up_total[: (ratio + 1) * unit], up_total[(ratio + 1) * unit :]
    grad_input = input_gradient(first_grad, qkv_grad, qkv_matrix, (3, 4, 4), (grad_input,))
    low_q, high_q, grad_input = together(*qkv_second, grad_input)
    qkv_third = together(*qkv_sum.third((low_q, high_q)), up_part)
    up_part = qkv_third[-1]
    qkv_third = qkv_sum.send_third(qkv_third[:-1])
    up_theirs = across(up_part.astype(BF16), Y)
    up_low, up_high = both_halves(up_part, up_theirs, y)
    grad_up = join_columns((up_low[: ratio * unit], up_high[: ratio * unit]), unit, ratio)
    grad_out = join_columns((up_low[ratio * unit :], up_high[ratio * unit :]), unit, 1)
    down_total = down.finish(down_third)
    *qkv_third, down_total, grad_up, grad_out = together(*qkv_third, down_total, grad_up, grad_out)
    qkv_total = qkv_sum.finish(qkv_third)
    qkv_part, qkv_small = qkv_total[: 3 * unit], qkv_total[3 * unit :]
    theirs = across(jnp.concatenate([qkv_part, down_total], axis=0).astype(BF16), Y)
    qkv_theirs, down_theirs = theirs[: 3 * unit], theirs[3 * unit :]
    grad_down = jnp.concatenate(both_halves(down_total, down_theirs, y), axis=1)
    grad_qkv = join_columns(both_halves(qkv_part, qkv_theirs, y), unit, 3)
    return (
        pooled,
        grad_input.reshape(row_count, length, width),
        grad_qkv,
        qkv_small[0, : 2 * unit],
        grad_out,
        up_small[0, :unit],
        up_small[1, :unit],
        up_small[2, :unit],
        grad_up,
        up_small[6, : ratio * unit],
        grad_down,
        up_small[3, :unit],
        up_small[4, :unit],
        up_small[5, :unit],
    )


def body_by_collectives(
    hidden_in,
    segment_ids,
    pooled_grad,
    qkv_weight,
    qv_bias,
    out_weight,
    out_bias,
    first_gain,
    first_shift,
    up_weight,
    up_bias,
    down_weight,
    down_bias,
    second_gain,
    second_shift,
):
    row_count, length, width = hidden_in.shape
    x = hidden_in.reshape(row_count * length, width)

    def gather(shard):
        return lax.all_gather(shard, "fsdp", axis=0, tiled=True)

    small = jnp.concatenate(
        [qv_bias, out_bias, first_gain, first_shift, up_bias, down_bias, second_gain, second_shift]
    ).astype(BF16)
    small = lax.all_gather(small, "fsdp", axis=0, tiled=False).astype(F32)
    unit = out_bias.shape[0]
    ends = [0]
    for part in (qv_bias, out_bias, first_gain, first_shift, up_bias, down_bias, second_gain, second_shift):
        ends.append(ends[-1] + part.shape[0])
    qv, ob, g1, s1, ub, db, g2, s2 = (small[:, a:b].reshape(1, -1) for a, b in zip(ends[:-1], ends[1:]))
    zeros = jnp.zeros((1, width), F32)
    vectors = jnp.concatenate([ob, g1, s1, db, g2, s2, zeros, zeros], axis=0)
    qkv_bias = jnp.concatenate([qv[:, :width], zeros, qv[:, width:]], axis=1)
    qkv_matrix = gather(qkv_weight)
    out_matrix = gather(out_weight)
    up_matrix = gather(up_weight)
    down_matrix = gather(down_weight)
    qkv, ctx = attention_forward(x, segment_ids, (qkv_matrix, qkv_bias))
    pooled, active, hidden_grad, normed, branch, first_grad, attended, ctx_grad, sums, up_sums = feedforward(
        x, ctx, segment_ids, pooled_grad, (out_matrix, up_matrix, down_matrix, vectors, ub), up_matrix.shape[1]
    )

    def scatter(grad):
        return lax.psum_scatter(grad.astype(BF16), "fsdp", scatter_dimension=0, tiled=True)

    grad_down = scatter(transpose_times(active, branch))
    grad_up = scatter(transpose_times(normed, hidden_grad))
    grad_out = scatter(transpose_times(ctx, attended))
    qkv_grad, qv_sums = attention_backward(qkv, ctx_grad, segment_ids)
    grad_qkv = scatter(transpose_times(x, qkv_grad))
    grad_input = first_grad + times_transpose(qkv_grad, qkv_matrix)
    grad_qkv, grad_out, grad_up, grad_down = lax.psum(
        tuple(g.astype(F32) for g in (grad_qkv, grad_out, grad_up, grad_down)), "dp"
    )
    sums = jnp.sum(sums.reshape(6, 8, width), axis=1)
    vector_sums = jnp.concatenate(
        [jnp.sum(qv_sums, axis=0), sums.reshape(-1), jnp.sum(up_sums, axis=0)]
    )
    vector_sums = lax.psum(vector_sums, ("dp", "fsdp"))
    me = lax.axis_index("fsdp")

    def mine(start, size):
        return lax.dynamic_slice(vector_sums, (start + me * size,), (size,))

    at = 2 * width
    return (
        pooled,
        grad_input.reshape(row_count, length, width),
        grad_qkv,
        mine(0, 2 * unit),
        grad_out,
        mine(at, unit),
        mine(at + width, unit),
        mine(at + 2 * width, unit),
        grad_up,
        mine(at + 6 * width, up_bias.shape[0]),
        grad_down,
        mine(at + 3 * width, unit),
        mine(at + 4 * width, unit),
        mine(at + 5 * width, unit),
    )


def solution(mesh):
    rows = ("dp", "fsdp")
    in_specs = (P(rows, None, None), P(rows, None), P(rows, None, None)) + (
        P("fsdp", None),
        P("fsdp"),
        P("fsdp", None),
        P("fsdp"),
        P("fsdp"),
        P("fsdp"),
        P("fsdp", None),
        P("fsdp"),
        P("fsdp", None),
        P("fsdp"),
        P("fsdp"),
        P("fsdp"),
    )
    out_specs = (
        P(rows, None, None),
        P(rows, None, None),
        P("fsdp", None),
        P("fsdp"),
        P("fsdp", None),
        P("fsdp"),
        P("fsdp"),
        P("fsdp"),
        P("fsdp", None),
        P("fsdp"),
        P("fsdp", None),
        P("fsdp"),
        P("fsdp"),
        P("fsdp"),
    )
    body = body_by_permutes if dict(mesh.shape) == {"dp": 2, "fsdp": 16} else body_by_collectives
    return jax.shard_map(body, mesh=mesh, in_specs=in_specs, out_specs=out_specs, check_vma=False)
```

```python
import functools
import math

import jax
import jax.numpy as jnp
from jax import lax
from jax.experimental import pallas as pl
from jax.experimental.pallas import tpu as pltpu
from jax.sharding import PartitionSpec as P

HEAD = 64
PAIR = 2 * HEAD
EPSILON = 1e-12
F32 = jnp.float32
BF16 = jnp.bfloat16
VMEM_LIMIT = 60000 * 1024
FF_ROWS = 2


def product(left, right):
    return jnp.dot(left, right, preferred_element_type=F32)


def times_transpose(left, right):
    return lax.dot_general(left, right, (((1,), (1,)), ((), ())), preferred_element_type=F32)


def transpose_times(left, right):
    return lax.dot_general(left, right, (((0,), (0,)), ((), ())), preferred_element_type=F32)


def normal_parts(u):
    cumulative = 0.5 + 0.5 * lax.erf(u * math.sqrt(0.5))
    return cumulative, u * (jnp.exp(-0.5 * u * u) * (1.0 / math.sqrt(2.0 * math.pi)))


def normalise(rows):
    average = jnp.mean(rows, axis=-1, keepdims=True)
    centred = rows - average
    variance = jnp.mean(centred * centred, axis=-1, keepdims=True)
    rstd = lax.rsqrt(variance + EPSILON)
    return centred * rstd, rstd


def normalise_back(grad, gain, xhat, rstd):
    e = grad * gain
    mean_e = jnp.mean(e, axis=-1, keepdims=True)
    mean_ex = jnp.mean(e * xhat, axis=-1, keepdims=True)
    return rstd * (e - mean_e - xhat * mean_ex)


def fold(values):
    rows, width = values.shape
    return jnp.sum(values.reshape(rows // 8, 8, width), axis=0)


def interleave(work, first, second, third):
    begun, done = {}, {}
    for number in range(len(work) + 2):
        if number < len(work):
            begun[number] = first(*work[number])
        if 0 <= number - 1 < len(work):
            done[number - 1] = second(*work[number - 1], begun.pop(number - 1))
        if number >= 2:
            third(*work[number - 2], done.pop(number - 2))


def lane_halves():
    lane = lax.broadcasted_iota(jnp.int32, (1, PAIR), 1)
    return (lane < HEAD).astype(BF16), (lane >= HEAD).astype(BF16)


def split_heads(block, low_half, high_half):
    return jnp.concatenate([block * low_half, block * high_half], axis=0)


def segment_grid(seg_ref, row, length):
    ids = seg_ref[pl.ds(row, 1), :].astype(F32)
    along_lanes = jnp.broadcast_to(ids, (length, length))
    return along_lanes, along_lanes.T


BLOCK = 384
SMALL = 16


def place_of(place_ref):
    return place_ref[0], place_ref[1], place_ref[2], place_ref[3]


def shard_slots(place_ref, whole_planes):
    y, z, x, core = place_of(place_ref)
    for other in range(2):
        for plane in range(4):
            for turn in range(4):
                if plane < whole_planes:
                    buffer, at = plane, turn
                else:
                    buffer, at = 2 * plane - whole_planes + turn // 2, turn % 2
                owner = ((z - turn) & 3) * 4 + (x ^ (plane & 1)) * 2 + (core ^ other)
                yield (8 - whole_planes) * other + buffer, at, owner, y ^ (plane >> 1), plane < 2


def run_copies(copies, sems):
    started = []
    for number, (source, target) in enumerate(copies):
        copy = pltpu.make_async_copy(source, target, sems.at[number])
        copy.start()
        started.append(copy)
    for copy in started:
        copy.wait()


def aligned(index, unit):
    return pl.multiple_of(index * unit, unit)


def attention_rows(length, width, first, x_ref, seg_ref, w_ref, bias_ref, qkv_ref, ctx_ref):
    tokens = x_ref.shape[0]
    step = pl.program_id(0) + first
    x = x_ref[...]
    for part in range(3):
        cols = pl.ds(part * width, width)
        qkv_ref[:, cols] = (product(x, w_ref[:, cols]) + bias_ref[0:1, cols]).astype(BF16)
    low_half, high_half = lane_halves()
    ones = jnp.concatenate(
        [jnp.broadcast_to(low_half, (length, PAIR)), jnp.broadcast_to(high_half, (length, PAIR))], axis=0
    )
    scale = HEAD**-0.5
    masks = []
    for local in range(tokens // length):
        along_lanes, along_rows = segment_grid(seg_ref, step * (tokens // length) + local, length)
        masks.append(along_lanes == along_rows)

    def score(local, pair):
        rows = pl.ds(local * length, length)
        q = qkv_ref[rows, pl.ds(pair * PAIR, PAIR)] * BF16(scale)
        k = qkv_ref[rows, pl.ds(width + pair * PAIR, PAIR)]
        return times_transpose(q, split_heads(k, low_half, high_half))

    def weigh(local, pair, scores):
        parts = []
        for half in range(2):
            masked = jnp.where(masks[local], scores[:, half * length : (half + 1) * length], -1e30)
            parts.append(jnp.exp(masked - jnp.max(masked, axis=-1, keepdims=True)).astype(BF16))
        return jnp.concatenate(parts, axis=1)

    def mix(local, pair, weights):
        rows = pl.ds(local * length, length)
        v = qkv_ref[rows, pl.ds(2 * width + pair * PAIR, PAIR)]
        values = jnp.concatenate([split_heads(v, low_half, high_half), ones], axis=1)
        both = product(weights, values)
        ctx_ref[rows, pl.ds(pair * PAIR, PAIR)] = (both[:, :PAIR] / both[:, PAIR:]).astype(BF16)

    interleave([(local, pair) for local in range(tokens // length) for pair in range(width // PAIR)], score, weigh, mix)


def attention_gathered_kernel(length, width, place_ref, x_ref, seg_ref, *rest):
    buffers, (qkv_ref, ctx_ref, w_ref, bias_ref, small_ref, sems) = rest[:10], rest[10:]
    unit = width // 16

    @pl.when(pl.program_id(0) == 0)
    def _():
        copies = []
        for buffer, at, owner, half, first in shard_slots(place_ref, 3):
            source = buffers[buffer].at[at]
            for block in range(3):
                target = w_ref.at[
                    pl.ds(aligned(owner, unit), unit), pl.ds(aligned(half * 3 + block, BLOCK), BLOCK)
                ]
                copies.append((source.at[pl.ds(block * unit, unit)], target))
            if first:
                copies.append((source.at[pl.ds(3 * unit, SMALL)], small_ref.at[owner]))
        run_copies(copies, sems)
        piece = 2 * unit
        lane = lax.broadcasted_iota(jnp.int32, (8, width), 1)
        for part, first in ((0, 0), (2, 8)):
            total = jnp.zeros((8, width), F32)
            for s in range(8):
                row = small_ref[first + s].astype(F32)[:8]
                row = jnp.where(lane < piece, jnp.concatenate([row, row], axis=1), 0.0)
                total = total + (pltpu.roll(row, s * piece, 1) if s else row)
            bias_ref[:, pl.ds(part * width, width)] = total
        bias_ref[:, pl.ds(width, width)] = jnp.zeros((8, width), F32)

    attention_rows(length, width, 0, x_ref, seg_ref, w_ref, bias_ref, qkv_ref, ctx_ref)


def attention_whole_kernel(length, width, first, x_ref, seg_ref, w_ref, bias_ref, *outs):
    attention_rows(length, width, first, x_ref, seg_ref, w_ref, bias_ref, *outs[-2:])


def attention_forward(x, seg, weights, place=None, part=(0, 1), earlier=(), rows_per_step=2):
    row_count, length = seg.shape
    tokens, width = x.shape
    block = rows_per_step * length
    steps = row_count // rows_per_step // part[1]
    first = part[0] * steps
    in_specs = [
        pl.BlockSpec((block, width), lambda i, *_: (i + first, 0)),
        pl.BlockSpec((row_count, length), lambda i, *_: (0, 0)),
    ]
    out_specs = [
        pl.BlockSpec((block, 3 * width), lambda i, *_: (i + first, 0)),
        pl.BlockSpec((block, width), lambda i, *_: (i + first, 0)),
    ]
    out_shape = [
        jax.ShapeDtypeStruct((tokens, 3 * width), BF16),
        jax.ShapeDtypeStruct((tokens, width), BF16),
    ]
    settings = dict(
        compiler_params=pltpu.CompilerParams(vmem_limit_bytes=VMEM_LIMIT),
        cost_estimate=pl.CostEstimate(
            flops=(2 * tokens * width * 3 * width + 8 * tokens * length * width) // part[1],
            bytes_accessed=tokens * width * 10 // part[1] + 6 * width * width,
            transcendentals=tokens * length * (width // HEAD) // part[1],
        ),
        name="attention_forward",
    )
    if place is None:
        in_specs += [
            pl.BlockSpec((width, 3 * width), lambda i: (0, 0), pipeline_mode=pl.Buffered(1)),
            pl.BlockSpec(weights[1].shape, lambda i: (0, 0)),
        ]
        in_specs += [pl.BlockSpec(memory_space=pl.ANY)] * len(earlier)
        return pl.pallas_call(
            functools.partial(attention_whole_kernel, length, width, first),
            grid=(steps,),
            in_specs=in_specs,
            out_specs=out_specs,
            out_shape=out_shape,
            input_output_aliases={4 + n: n for n in range(len(earlier))},
            **settings,
        )(x, seg, *weights, *earlier)
    spec = pltpu.PrefetchScalarGridSpec(
        num_scalar_prefetch=1,
        grid=(steps,),
        in_specs=in_specs + [pl.BlockSpec(memory_space=pl.ANY)] * 10,
        out_specs=out_specs
        + [
            pl.BlockSpec((width, 3 * width), lambda i, *_: (0, 0)),
            pl.BlockSpec((8, 3 * width), lambda i, *_: (0, 0)),
        ],
        scratch_shapes=[
            pltpu.VMEM((16, SMALL, BLOCK), BF16),
            pltpu.SemaphoreType.DMA((112,)),
        ],
    )
    return pl.pallas_call(
        functools.partial(attention_gathered_kernel, length, width),
        grid_spec=spec,
        out_shape=out_shape
        + [
            jax.ShapeDtypeStruct((width, 3 * width), BF16),
            jax.ShapeDtypeStruct((8, 3 * width), F32),
        ],
        **settings,
    )(place, x, seg, *weights)


def feedforward_rows(
    length,
    chunk,
    x_ref,
    ctx_ref,
    seg_ref,
    pooled_grad_ref,
    out_w_ref,
    up_w_ref,
    down_w_ref,
    vec_ref,
    up_bias_ref,
    pooled_ref,
    active_ref,
    hidden_ref,
    normed_ref,
    branch_ref,
    first_ref,
    attended_ref,
    context_ref,
    small_ref,
    up_small_ref,
    slope_ref,
):
    step = pl.program_id(0)
    tokens, width = x_ref.shape
    hidden = up_w_ref.shape[1]
    segments = pooled_grad_ref.shape[1]
    out_bias, gain_one, shift_one = vec_ref[0:1, :], vec_ref[1:2, :], vec_ref[2:3, :]
    down_bias, gain_two, shift_two = vec_ref[3:4, :], vec_ref[4:5, :], vec_ref[5:6, :]

    @pl.when(step == 0)
    def _():
        small_ref[...] = jnp.zeros_like(small_ref)
        up_small_ref[...] = jnp.zeros_like(up_small_ref)

    first_sum = x_ref[...].astype(F32) + product(ctx_ref[...], out_w_ref[...]) + out_bias
    xhat_one, rstd_one = normalise(first_sum)
    normed_one = xhat_one * gain_one + shift_one
    normed_low = normed_one.astype(BF16)
    normed_ref[...] = normed_low
    second_sum = normed_one + down_bias
    for start in range(0, hidden, chunk):
        cols = pl.ds(start, chunk)
        pre = product(normed_low, up_w_ref[:, cols]) + up_bias_ref[:, cols]
        cumulative, tilt = normal_parts(pre)
        active = (pre * cumulative).astype(BF16)
        slope_ref[:, cols] = cumulative + tilt
        active_ref[:, cols] = active
        second_sum = second_sum + product(active, down_w_ref[cols, :])
    xhat_two, rstd_two = normalise(second_sum)
    final = xhat_two * gain_two + shift_two
    final_high = final.astype(BF16)
    final_low = (final - final_high.astype(F32)).astype(BF16)
    token_parts = []
    for local in range(tokens // length):
        rows = slice(local * length, (local + 1) * length)
        along_lanes, along_rows = segment_grid(seg_ref, step * (tokens // length) + local, length)
        index = lax.broadcasted_iota(jnp.int32, (8, length), 0).astype(F32)
        member = (along_lanes[:8, :] == index).astype(F32)
        population = jnp.sum(member, axis=1, keepdims=True)
        member_low = member.astype(BF16)
        sums = product(member_low, final_high[rows]) + product(member_low, final_low[rows])
        pooled_ref[local] = sums[:segments] / population[:segments]
        share = pooled_grad_ref[local] / population[:segments]
        wide = jnp.concatenate([along_rows] * (width // length), axis=1)
        token = jnp.broadcast_to(share[segments - 1 : segments], (length, width))
        for s in range(segments - 2, -1, -1):
            token = jnp.where(wide == float(s), share[s : s + 1], token)
        token_parts.append(token)
    token_grad = jnp.concatenate(token_parts, axis=0)
    second_grad = normalise_back(token_grad, gain_two, xhat_two, rstd_two)
    branch = second_grad.astype(BF16)
    branch_ref[...] = branch
    small_ref[24:32, :] += fold(branch.astype(F32))
    small_ref[32:40, :] += fold(token_grad * xhat_two)
    small_ref[40:48, :] += fold(token_grad)
    normed_grad = second_grad
    for start in range(0, hidden, chunk):
        cols = pl.ds(start, chunk)
        grad = (times_transpose(branch, down_w_ref[cols, :]) * slope_ref[:, cols]).astype(BF16)
        hidden_ref[:, cols] = grad
        up_small_ref[:, cols] += fold(grad.astype(F32))
        normed_grad = normed_grad + times_transpose(grad, up_w_ref[:, cols])
    first_grad = normalise_back(normed_grad, gain_one, xhat_one, rstd_one)
    first_ref[...] = first_grad
    attended = first_grad.astype(BF16)
    attended_ref[...] = attended
    context_ref[...] = times_transpose(attended, out_w_ref[...]).astype(BF16)
    small_ref[0:8, :] += fold(attended.astype(F32))
    small_ref[8:16, :] += fold(normed_grad * xhat_one)
    small_ref[16:24, :] += fold(normed_grad)


def feedforward_gathered_kernel(length, chunk, place_ref, x_ref, ctx_ref, seg_ref, pooled_grad_ref, *rest):
    buffers, outs = rest[:16], rest[16:26]
    slope_ref, out_w_ref, up_w_ref, down_w_ref, vec_ref, up_bias_ref, gathered_ref, sems = rest[26:]
    width, hidden = up_w_ref.shape
    unit = width // 16
    ratio = hidden // width

    @pl.when(pl.program_id(0) == 0)
    def _():
        copies = []
        for buffer, at, owner, half, first in shard_slots(place_ref, 0):
            source = buffers[buffer].at[at]
            rows = pl.ds(aligned(owner, unit), unit)
            for block in range(ratio):
                cols = pl.ds(aligned(half * ratio + block, BLOCK), BLOCK)
                copies.append((source.at[pl.ds(block * unit, unit)], up_w_ref.at[rows, cols]))
            cols = pl.ds(aligned(half, BLOCK), BLOCK)
            down_rows = pl.ds(aligned(owner, ratio * unit), ratio * unit)
            copies.append((source.at[pl.ds(ratio * unit, ratio * unit)], down_w_ref.at[down_rows, cols]))
            copies.append((source.at[pl.ds(2 * ratio * unit, unit)], out_w_ref.at[rows, cols]))
            if first:
                at_small = (2 * ratio + 1) * unit
                copies.append((source.at[pl.ds(at_small, SMALL)], gathered_ref.at[owner]))
        run_copies(copies, sems)
        lane = lax.broadcasted_iota(jnp.int32, (8, width), 1)
        total = jnp.zeros((8, width), F32)
        for s in range(16):
            row = gathered_ref[s].astype(F32)[:8]
            row = jnp.where(lane < unit, jnp.concatenate([row, row], axis=1), 0.0)
            total = total + (pltpu.roll(row, s * unit, 1) if s else row)
        vec_ref[...] = total
        lane = lax.broadcasted_iota(jnp.int32, (8, BLOCK), 1)
        for s in range(0, 16, 2):
            low = gathered_ref[s].astype(F32)[:8]
            high = gathered_ref[s + 1].astype(F32)[:8]
            high = pltpu.roll(high, BLOCK // 2, 1)
            both = jnp.where(lane < BLOCK // 2, low, high)
            up_bias_ref[:, pl.ds((s // 2) * BLOCK, BLOCK)] = both[6:7, :]

    feedforward_rows(
        length, chunk, x_ref, ctx_ref, seg_ref, pooled_grad_ref,
        out_w_ref, up_w_ref, down_w_ref, vec_ref, up_bias_ref, *outs, slope_ref,
    )


def feedforward(x, ctx, seg, pooled_grad, weights, hidden, place=None, rows_per_step=FF_ROWS, chunk=768):
    row_count, length = seg.shape
    tokens, width = x.shape
    segments = pooled_grad.shape[1]
    block = rows_per_step * length

    def tiled(columns):
        return pl.BlockSpec((block, columns), lambda i, *_: (i, 0))

    def whole(shape):
        return pl.BlockSpec(shape, lambda i, *_: (0,) * len(shape), pipeline_mode=pl.Buffered(1))

    def kept(shape):
        return pl.BlockSpec(shape, lambda i, *_: (0,) * len(shape))

    def rows(columns, dtype):
        return jax.ShapeDtypeStruct((tokens, columns), dtype)

    grid = (row_count // rows_per_step,)
    in_specs = [
        tiled(width),
        tiled(width),
        whole((row_count, length)),
        pl.BlockSpec((rows_per_step, segments, width), lambda i, *_: (i, 0, 0)),
    ]
    out_specs = [
        pl.BlockSpec((rows_per_step, segments, width), lambda i, *_: (i, 0, 0)),
        tiled(hidden),
        tiled(hidden),
        tiled(width),
        tiled(width),
        tiled(width),
        tiled(width),
        tiled(width),
        kept((48, width)),
        kept((8, hidden)),
    ]
    out_shape = [
        jax.ShapeDtypeStruct((row_count, segments, width), F32),
        rows(hidden, BF16),
        rows(hidden, BF16),
        rows(width, BF16),
        rows(width, BF16),
        rows(width, F32),
        rows(width, BF16),
        rows(width, BF16),
        jax.ShapeDtypeStruct((48, width), F32),
        jax.ShapeDtypeStruct((8, hidden), F32),
    ]
    settings = dict(
        compiler_params=pltpu.CompilerParams(vmem_limit_bytes=VMEM_LIMIT),
        cost_estimate=pl.CostEstimate(
            flops=tokens * width * (4 * width + 8 * hidden),
            bytes_accessed=tokens * (width * 18 + hidden * 4) + 4 * width * hidden,
            transcendentals=2 * tokens * hidden,
        ),
        name="feedforward",
    )
    slope = pltpu.VMEM((block, hidden), F32)
    if place is None:
        in_specs += [
            whole((width, width)),
            whole((width, hidden)),
            whole((hidden, width)),
            whole((8, width)),
            whole((1, hidden)),
        ]
        return pl.pallas_call(
            functools.partial(feedforward_rows, length, chunk),
            grid=grid,
            in_specs=in_specs,
            out_specs=out_specs,
            out_shape=out_shape,
            scratch_shapes=[slope],
            **settings,
        )(x, ctx, seg, pooled_grad, *weights)
    spec = pltpu.PrefetchScalarGridSpec(
        num_scalar_prefetch=1,
        grid=grid,
        in_specs=in_specs + [pl.BlockSpec(memory_space=pl.ANY)] * 16,
        out_specs=out_specs,
        scratch_shapes=[
            slope,
            pltpu.VMEM((width, width), BF16),
            pltpu.VMEM((width, hidden), BF16),
            pltpu.VMEM((hidden, width), BF16),
            pltpu.VMEM((8, width), F32),
            pltpu.VMEM((1, hidden), F32),
            pltpu.VMEM((16, SMALL, BLOCK), BF16),
            pltpu.SemaphoreType.DMA((32 * (hidden // width + 2) + 16,)),
        ],
    )
    return pl.pallas_call(
        functools.partial(feedforward_gathered_kernel, length, chunk),
        grid_spec=spec,
        out_shape=out_shape,
        **settings,
    )(place, x, ctx, seg, pooled_grad, *weights)


def tiled(block, columns):
    return pl.BlockSpec((block, columns), lambda i, *_: (i, 0))


def resident(shape):
    return pl.BlockSpec(shape, lambda i, *_: (0,) * len(shape), pipeline_mode=pl.Buffered(1))


def attention_back_kernel(length, width, first, qkv_ref, grad_ref, seg_ref, *rest):
    out_ref, small_ref = rest[-2:]
    tokens = grad_ref.shape[0]
    step = pl.program_id(0) + first

    @pl.when(pl.program_id(0) == 0)
    def _():
        small_ref[...] = rest[1][...] if first else jnp.zeros_like(small_ref)

    low_half, high_half = lane_halves()
    scale = BF16(HEAD**-0.5)
    masks = []
    for local in range(tokens // length):
        along_lanes, along_rows = segment_grid(seg_ref, step * (tokens // length) + local, length)
        same = along_lanes == along_rows
        masks.append(jnp.concatenate([same, same], axis=1))

    def load(ref, local, part, pair):
        return ref[pl.ds(local * length, length), pl.ds(part * width + pair * PAIR, PAIR)]

    def split(block):
        return split_heads(block, low_half, high_half)

    def score(local, pair):
        q = split(load(qkv_ref, local, 0, pair) * scale)
        ctx_grad = split(load(grad_ref, local, 0, pair))
        k, v = load(qkv_ref, local, 1, pair), load(qkv_ref, local, 2, pair)
        return times_transpose(k, q), times_transpose(v, ctx_grad)

    def weigh(local, pair, products):
        scores, probs_grad = products
        scores = jnp.where(masks[local], scores, -1e30)
        weights = jnp.exp(scores - jnp.max(scores, axis=0, keepdims=True))
        weights = weights * (1.0 / jnp.sum(weights, axis=0, keepdims=True))
        inner = jnp.sum(weights * probs_grad, axis=0, keepdims=True)
        scores_grad = (weights * (probs_grad - inner)).astype(BF16)
        turned = jnp.concatenate([scores_grad[:, :length].T, scores_grad[:, length:].T], axis=1)
        return weights.astype(BF16), scores_grad, turned

    def mix(local, pair, found):
        weights, scores_grad, turned = found
        values_grad = product(weights, split(load(grad_ref, local, 0, pair))).astype(BF16)
        keys_grad = product(scores_grad, split(load(qkv_ref, local, 0, pair) * scale)).astype(BF16)
        queries_grad = product(turned, split(load(qkv_ref, local, 1, pair) * scale)).astype(BF16)
        rows = pl.ds(local * length, length)
        for part, grad in enumerate((queries_grad, keys_grad, values_grad)):
            out_ref[rows, pl.ds(part * width + pair * PAIR, PAIR)] = grad
        small_ref[:, pl.ds(pair * PAIR, PAIR)] += fold(queries_grad.astype(F32))
        small_ref[:, pl.ds(width + pair * PAIR, PAIR)] += fold(values_grad.astype(F32))

    interleave([(local, pair) for local in range(tokens // length) for pair in range(width // PAIR)], score, weigh, mix)


def attention_backward(qkv, ctx_grad, seg, part=(0, 1), earlier=(), rows_per_step=2):
    row_count, length = seg.shape
    tokens, width = ctx_grad.shape
    block = rows_per_step * length
    steps = row_count // rows_per_step // part[1]
    first = part[0] * steps
    sums_spec = pl.BlockSpec((8, 2 * width), lambda i: (0, 0))
    return pl.pallas_call(
        functools.partial(attention_back_kernel, length, width, first),
        grid=(steps,),
        in_specs=[
            pl.BlockSpec((block, 3 * width), lambda i: (i + first, 0)),
            pl.BlockSpec((block, width), lambda i: (i + first, 0)),
            pl.BlockSpec((row_count, length), lambda i: (0, 0)),
        ]
        + [pl.BlockSpec(memory_space=pl.ANY), sums_spec][: len(earlier)],
        out_specs=[pl.BlockSpec((block, 3 * width), lambda i: (i + first, 0)), sums_spec],
        out_shape=[
            jax.ShapeDtypeStruct((tokens, 3 * width), BF16),
            jax.ShapeDtypeStruct((8, 2 * width), F32),
        ],
        input_output_aliases={3: 0} if earlier else {},
        compiler_params=pltpu.CompilerParams(vmem_limit_bytes=VMEM_LIMIT),
        cost_estimate=pl.CostEstimate(
            flops=20 * tokens * length * width // part[1],
            bytes_accessed=tokens * width * 14 // part[1],
            transcendentals=tokens * length * (width // HEAD) // part[1],
        ),
        name="attention_backward",
    )(qkv, ctx_grad, seg, *earlier)


def cut_columns(half_index, shard, out_ref, row_at, blocks):
    rows = shard.shape[0]
    for half in range(2):

        @pl.when(half_index == half)
        def _():
            for block in range(blocks):
                cols = pl.ds((half * blocks + block) * BLOCK, BLOCK)
                out_ref[pl.ds(row_at + block * rows, rows), :] = shard[:, cols]


def pack_attention_kernel(place_ref, qkv_ref, bias_ref, out_ref):
    unit = qkv_ref.shape[0]
    cut_columns(place_ref[0], qkv_ref, out_ref, 0, 3)
    out_ref[pl.ds(3 * unit, SMALL), :] = jnp.zeros((SMALL, BLOCK), BF16)
    out_ref[pl.ds(3 * unit, 1), pl.ds(0, 2 * unit)] = bias_ref[...]


def pack_feedforward_kernel(place_ref, up_ref, down_ref, out_w_ref, small_ref, out_ref):
    unit = up_ref.shape[0]
    ratio = down_ref.shape[0] // unit
    cut_columns(place_ref[0], up_ref, out_ref, 0, ratio)
    cut_columns(place_ref[0], down_ref, out_ref, ratio * unit, 1)
    cut_columns(place_ref[0], out_w_ref, out_ref, 2 * ratio * unit, 1)
    out_ref[pl.ds((2 * ratio + 1) * unit, SMALL), :] = small_ref[...]


def pack(kernel, name, place, rows, *shards):
    spec = pltpu.PrefetchScalarGridSpec(
        num_scalar_prefetch=1,
        grid=(1,),
        in_specs=[pl.BlockSpec(s.shape, lambda i, *_: (0, 0)) for s in shards],
        out_specs=pl.BlockSpec((rows, BLOCK), lambda i, *_: (0, 0)),
    )
    return pl.pallas_call(
        kernel, grid_spec=spec, out_shape=jax.ShapeDtypeStruct((rows, BLOCK), BF16), name=name
    )(place, *shards)


def store_shards(place_ref, keep_ref, send_ref, plane_z, half, row_at, rows, values):
    y, z, x, core = place_of(place_ref)
    turn = (z - plane_z) & 3
    first = core == 0
    for plane_x in range(2):
        even = values(plane_z * 4 + plane_x * 2)
        odd = values(plane_z * 4 + plane_x * 2 + 1)
        at = (half ^ y, plane_x ^ x, turn, pl.ds(row_at, rows))
        keep_ref[at] = jnp.where(first, even, odd)
        send_ref[at] = jnp.where(first, odd, even)


def write_back(regions, steps, pairs, sems):
    step = pl.program_id(0)

    def copies(at_step):
        for number, region in enumerate(regions(at_step)):
            for side, (stored, result) in enumerate(pairs):
                sem = sems.at[at_step, number, side]
                yield pltpu.make_async_copy(stored.at[region], result.at[region], sem)

    for copy in copies(step):
        copy.start()

    @pl.when(step == steps - 1)
    def _():
        for at_step in range(steps):
            for copy in copies(at_step):
                copy.wait()


def down_gradient_kernel(place_ref, active_ref, branch_ref, keep_out, send_out, keep_ref, send_ref, sems):
    grad = transpose_times(active_ref[...], branch_ref[...]).astype(BF16)
    rows = grad.shape[0] // 4
    y, z, x, core = place_of(place_ref)
    first = core == 0
    turn = (z - pl.program_id(0)) & 3
    for half in range(2):
        cols = slice(half * BLOCK, (half + 1) * BLOCK)
        for plane_x in range(2):
            even = grad[2 * plane_x * rows : (2 * plane_x + 1) * rows, cols]
            odd = grad[(2 * plane_x + 1) * rows : (2 * plane_x + 2) * rows, cols]
            at = (half ^ y, plane_x ^ x, turn)
            keep_ref[at] = jnp.where(first, even, odd)
            send_ref[at] = jnp.where(first, odd, even)
    every = slice(None)

    def regions(step):
        return [(every, every, (z - step) & 3)]

    write_back(regions, 4, ((keep_ref, keep_out), (send_ref, send_out)), sems)


def block_place(number, blocks, unit):
    half = number // blocks
    row = (number - half * blocks) * unit
    return half, row if isinstance(row, int) else pl.multiple_of(row, unit)


def store_columns(place_ref, keep_ref, send_ref, grad, first_block, blocks):
    unit = grad.shape[0] // 16
    for part in range(2):
        half, row_at = block_place(first_block + part, blocks, unit)

        def values(s):
            return grad[s * unit : (s + 1) * unit, part * BLOCK : (part + 1) * BLOCK]

        for plane_z in range(4):
            store_shards(place_ref, keep_ref, send_ref, plane_z, half, row_at, unit, values)


def column_regions(place_ref, first_block, blocks, unit):
    every = slice(None)
    for part in range(2):
        half, row_at = block_place(first_block + part, blocks, unit)
        yield half ^ place_ref[0], every, every, pl.ds(row_at, unit)


def store_small(place_ref, keep_ref, send_ref, row_at, values):
    for half in range(2):
        for plane_z in range(4):
            store_shards(place_ref, keep_ref, send_ref, plane_z, half, row_at, SMALL, values)


def up_gradient_kernel(
    place_ref, normed_ref, hidden_ref, ctx_ref, attended_ref, sums_ref, up_sums_ref,
    keep_out, send_out, keep_ref, send_ref, sems, turned_ref, total_ref,
):
    step = pl.program_id(0)
    steps = up_sums_ref.shape[1] // normed_ref.shape[1]
    width = normed_ref.shape[1]
    unit = width // 16

    @pl.when(step == 0)
    def _():
        turned_ref[...] = normed_ref[...].T
        total_ref[...] = jnp.zeros_like(total_ref)

    grad = product(turned_ref[...], hidden_ref[...]).astype(BF16)
    store_columns(place_ref, keep_ref, send_ref, grad, 2 * step, steps)
    total_ref[...] += transpose_times(ctx_ref[...], attended_ref[...])

    @pl.when(step == steps - 1)
    def _():
        for part in range(2):

            def values(s):
                cols = pl.ds(part * BLOCK, BLOCK)
                return total_ref[pl.ds(s * unit, unit), cols].astype(BF16)

            for plane_z in range(4):
                store_shards(place_ref, keep_ref, send_ref, plane_z, part, steps * unit, unit, values)
        row = lax.broadcasted_iota(jnp.int32, (SMALL, width), 0)
        vectors = jnp.zeros((SMALL, width), F32)
        for number in range(6):
            total = jnp.sum(sums_ref[pl.ds(8 * number, 8), :], axis=0, keepdims=True)
            vectors = jnp.where(row == number, total, vectors)
        up_total = jnp.sum(up_sums_ref[...], axis=0, keepdims=True)
        row = row[:, :BLOCK]

        def small(s):
            rolled = pltpu.roll(vectors, width - s * unit, 1) if s else vectors
            up = jnp.broadcast_to(up_total[:, (s // 2) * BLOCK : (s // 2 + 1) * BLOCK], (SMALL, BLOCK))
            up = pltpu.roll(up, BLOCK // 2, 1) if s % 2 else up
            return jnp.where(row == 6, up, rolled[:, :BLOCK]).astype(BF16)

        store_small(place_ref, keep_ref, send_ref, (steps + 1) * unit, small)

    every = slice(None)

    def regions(at_step):
        yield from column_regions(place_ref, 2 * at_step, steps, unit)
        if isinstance(at_step, int) and at_step == steps - 1:
            yield every, every, every, pl.ds(steps * unit, unit + SMALL)

    @pl.when(step == steps - 1)
    def _():
        region = (every, every, every, pl.ds(steps * unit, unit + SMALL))
        for side, (stored, result) in enumerate(((keep_ref, keep_out), (send_ref, send_out))):
            pltpu.make_async_copy(stored.at[region], result.at[region], sems.at[steps - 1, 2, side]).start()

    write_back(regions, steps, ((keep_ref, keep_out), (send_ref, send_out)), sems)


def qkv_gradient_kernel(
    place_ref, x_ref, grad_ref, sums_ref, keep_out, send_out, keep_ref, send_ref, sems, turned_ref
):
    step = pl.program_id(0)
    width = x_ref.shape[1]
    unit = width // 16
    every = slice(None)
    pairs = ((keep_ref, keep_out), (send_ref, send_out))

    @pl.when(step == 0)
    def _():
        turned_ref[...] = x_ref[...].T
        total = jnp.sum(sums_ref[...], axis=0, keepdims=True)

        def small(s):
            part = total[:, (s // 8) * width : (s // 8 + 1) * width]
            part = jnp.broadcast_to(part, (SMALL, width))
            shift = (s % 8) * 2 * unit
            part = pltpu.roll(part, width - shift, 1) if shift else part
            return part[:, :BLOCK].astype(BF16)

        store_small(place_ref, keep_ref, send_ref, 3 * unit, small)
        region = (every, every, every, pl.ds(3 * unit, SMALL))
        for side, (stored, result) in enumerate(pairs):
            pltpu.make_async_copy(stored.at[region], result.at[region], sems.at[0, 2, side]).start()

    grad = product(turned_ref[...], grad_ref[...]).astype(BF16)
    store_columns(place_ref, keep_ref, send_ref, grad, 2 * step, 3)

    def regions(at_step):
        yield from column_regions(place_ref, 2 * at_step, 3, unit)
        if isinstance(at_step, int) and at_step == 0:
            yield every, every, every, pl.ds(3 * unit, SMALL)

    write_back(regions, 3, pairs, sems)


def weight_gradient(kernel, name, place, rows, steps, arrays, specs, flops, scratch=()):
    shape = (2, 2, 4, rows, BLOCK)
    spec = pltpu.PrefetchScalarGridSpec(
        num_scalar_prefetch=1,
        grid=(steps,),
        in_specs=specs,
        out_specs=[pl.BlockSpec(memory_space=pl.ANY)] * 2,
        scratch_shapes=[
            pltpu.VMEM(shape, BF16),
            pltpu.VMEM(shape, BF16),
            pltpu.SemaphoreType.DMA((steps, 3, 2)),
            *scratch,
        ],
    )
    return pl.pallas_call(
        kernel,
        grid_spec=spec,
        out_shape=[jax.ShapeDtypeStruct(shape, BF16)] * 2,
        compiler_params=pltpu.CompilerParams(vmem_limit_bytes=VMEM_LIMIT),
        cost_estimate=pl.CostEstimate(
            flops=flops, bytes_accessed=sum(2 * a.size for a in arrays), transcendentals=0
        ),
        name=name,
    )(place, *arrays)


def input_gradient_kernel(first_ref, grad_ref, w_ref, *outs):
    outs[-1][...] = first_ref[...] + times_transpose(grad_ref[...], w_ref[...])


def input_gradient(first_grad, qkv_grad, matrix, part=(0, 1, 1), earlier=(), rows=256):
    tokens, width = first_grad.shape
    first = tokens // rows * part[0] // part[2]
    steps = tokens // rows * part[1] // part[2] - first
    return pl.pallas_call(
        input_gradient_kernel,
        grid=(steps,),
        in_specs=[
            pl.BlockSpec((rows, width), lambda i: (i + first, 0)),
            pl.BlockSpec((rows, 3 * width), lambda i: (i + first, 0)),
            resident(matrix.shape),
        ]
        + [pl.BlockSpec(memory_space=pl.ANY)] * len(earlier),
        out_specs=pl.BlockSpec((rows, width), lambda i: (i + first, 0)),
        out_shape=jax.ShapeDtypeStruct((tokens, width), F32),
        input_output_aliases={3: 0} if earlier else {},
        compiler_params=pltpu.CompilerParams(vmem_limit_bytes=VMEM_LIMIT),
        cost_estimate=pl.CostEstimate(
            flops=6 * steps * rows * width * width,
            bytes_accessed=14 * steps * rows * width,
            transcendentals=0,
        ),
        name="input_gradient",
    )(first_grad, qkv_grad, matrix, *earlier)


AXES = ("dp", "fsdp")
DEVICES = 32
CORE, X, Y = 1, 2, 16


def across(value, mask):
    return lax.ppermute(value, AXES, [(i, i ^ mask) for i in range(DEVICES)])


def along_z(value, distance):
    def target(i):
        return i - i % 16 + (i % 16 + 4 * distance) % 16

    return lax.ppermute(value, AXES, [(i, target(i)) for i in range(DEVICES)])


def together(*values):
    return lax.optimization_barrier(values)


def shifts(own):
    return tuple(along_z(own, d) for d in (1, 2, 3))


class Reduction:
    def __init__(self, keep, got):
        self.keep, self.got = keep, got

    def pair(self, *at):
        return self.keep[at].astype(F32) + self.got[at].astype(F32)

    def first(self):
        low_x = self.pair(slice(None), 1, slice(0, 2)).astype(BF16)
        high_y = self.pair(1, slice(None), slice(2, 4)).astype(BF16)
        return low_x, high_y

    @staticmethod
    def send_first(values):
        return across(values[0], X), across(values[1], Y)

    def second(self, received):
        low_x, high_y = self.received = received
        low_y = (self.pair(1, 0, slice(0, 2)) + low_x[1].astype(F32)).astype(BF16)
        high_x = (self.pair(0, 1, slice(2, 4)) + high_y[1].astype(F32)).astype(BF16)
        return low_y, high_x

    @staticmethod
    def send_second(values):
        return across(values[0], Y), across(values[1], X)

    def third(self, received):
        low = self.pair(0, 0, slice(0, 2)) + self.received[0][0].astype(F32) + received[0].astype(F32)
        high = self.pair(0, 0, slice(2, 4)) + self.received[1][0].astype(F32) + received[1].astype(F32)
        self.total = low[0]
        return low[1].astype(BF16), high[0].astype(BF16), high[1].astype(BF16)

    @staticmethod
    def send_third(values):
        return tuple(along_z(value, 3 - n) for n, value in enumerate(values))

    def finish(self, received):
        total = self.total
        for part in received:
            total = total + part.astype(F32)
        return total


def both_halves(mine, theirs, y):
    theirs = theirs.astype(F32)
    swap = y == 0
    return jnp.where(swap, mine, theirs), jnp.where(swap, theirs, mine)


def join_columns(halves, unit, blocks):
    parts = []
    for half in halves:
        cols = half.reshape(blocks, unit, BLOCK)
        parts += [cols[b] for b in range(blocks)]
    return jnp.concatenate(parts, axis=1)


def rows_of(vectors, rows):
    padded = [jnp.pad(v, (0, BLOCK - v.shape[0])) for v in vectors]
    padded += [jnp.zeros((BLOCK,), BF16)] * (rows - len(padded))
    return jnp.stack(padded)


def body_by_permutes(
    hidden_in,
    segment_ids,
    pooled_grad,
    qkv_weight,
    qv_bias,
    out_weight,
    out_bias,
    first_gain,
    first_shift,
    up_weight,
    up_bias,
    down_weight,
    down_bias,
    second_gain,
    second_shift,
):
    row_count, length, width = hidden_in.shape
    tokens = row_count * length
    x = hidden_in.reshape(tokens, width)
    unit = qkv_weight.shape[0]
    hidden = up_weight.shape[1]
    ratio = hidden // width
    y, shard = lax.axis_index("dp"), lax.axis_index("fsdp")
    place = jnp.stack([y, shard // 4, shard // 2 % 2, shard % 2]).astype(jnp.int32)

    own_attention = pack(
        pack_attention_kernel,
        "pack_attention",
        place,
        3 * unit + SMALL,
        qkv_weight,
        qv_bias[None],
    )
    vectors = [out_bias, first_gain, first_shift, down_bias, second_gain, second_shift, up_bias]
    own_attention, *vectors = together(own_attention, *vectors)
    own_feedforward = pack(
        pack_feedforward_kernel,
        "pack_feedforward",
        place,
        (2 * ratio + 1) * unit + SMALL,
        up_weight,
        down_weight,
        out_weight,
        rows_of(vectors, SMALL),
    )
    turned = shifts(own_attention)
    own_attention, own_feedforward, *turned = together(own_attention, own_feedforward, *turned)
    here_a = jnp.stack([own_attention, *turned])
    x_a, y_a = across(here_a, X), across(here_a, Y)
    here_a_core = across(here_a, CORE)
    turn_f = along_z(own_feedforward, 1)
    x_a, y_a, own_feedforward, turn_f = together(x_a, y_a, own_feedforward, turn_f)
    low_a, high_a = across(x_a[:2], Y), across(y_a[2:], X)
    x_a_core, y_a_core = across(x_a, CORE), across(y_a, CORE)
    here_low = jnp.stack([own_feedforward, turn_f])
    low_a, high_a, here_low, own_feedforward = together(low_a, high_a, here_low, own_feedforward)
    turn_two, turn_three = along_z(own_feedforward, 2), along_z(own_feedforward, 3)
    attention_pieces = (here_a, x_a, y_a, low_a, high_a)
    attention_pieces += (here_a_core, x_a_core, y_a_core, across(low_a, CORE), across(high_a, CORE))
    here_low, turn_three, *attention_pieces = together(here_low, turn_three, *attention_pieces)
    x_low, y_low = across(here_low, X), across(here_low, Y)
    here_low_core = across(here_low, CORE)
    qkv, ctx, qkv_matrix, qkv_bias = attention_forward(x, segment_ids, attention_pieces, place, (0, 2))
    x_low, y_low, turn_two, qkv, ctx = together(x_low, y_low, turn_two, qkv, ctx)
    here_high, qkv, ctx = together(jnp.stack([turn_two, turn_three]), qkv, ctx)
    x_high, y_high = across(here_high, X), across(here_high, Y)
    x_low_core, y_low_core, here_high_core = across(x_low, CORE), across(y_low, CORE), across(here_high, CORE)
    qkv, ctx = attention_forward(x, segment_ids, (qkv_matrix, qkv_bias), None, (1, 2), (qkv, ctx))
    x_high, y_high, qkv, ctx = together(x_high, y_high, qkv, ctx)
    both_low, both_high = across(x_low, Y), across(y_high, X)
    x_high_core, y_high_core = across(x_high, CORE), across(y_high, CORE)
    feedforward_pieces = (here_low, here_high, x_low, x_high, y_low, y_high, both_low, both_high)
    feedforward_pieces += (here_low_core, here_high_core, x_low_core, x_high_core, y_low_core, y_high_core)
    feedforward_pieces += (across(both_low, CORE), across(both_high, CORE))
    pooled, active, hidden_grad, normed, branch, first_grad, attended, ctx_grad, sums, up_sums = feedforward(
        x, ctx, segment_ids, pooled_grad, feedforward_pieces, hidden, place
    )

    up_keep, up_send = weight_gradient(
        up_gradient_kernel,
        "up_gradient",
        place,
        (ratio + 1) * unit + SMALL,
        ratio,
        (normed, hidden_grad, ctx, attended, sums, up_sums),
        [
            resident((tokens, width)),
            pl.BlockSpec((tokens, width), lambda i, *_: (0, i)),
            tiled(tokens // ratio, width),
            tiled(tokens // ratio, width),
            resident(sums.shape),
            resident(up_sums.shape),
        ],
        2 * tokens * width * (hidden + width),
        (pltpu.VMEM((width, tokens), BF16), pltpu.VMEM((width, width), F32)),
    )
    up_keep, up_send, active = together(up_keep, up_send, active)
    up_got = across(up_send, CORE)
    down_keep, down_send = weight_gradient(
        down_gradient_kernel,
        "down_gradient",
        place,
        ratio * unit,
        4,
        (active, branch),
        [pl.BlockSpec((tokens, hidden // 4), lambda i, *_: (0, i)), resident((tokens, width))],
        2 * tokens * hidden * width,
    )
    up_got, down_keep, down_send = together(up_got, down_keep, down_send)
    up = Reduction(up_keep, up_got)
    low_u, high_u, down_send, ctx_grad = together(*up.first(), down_send, ctx_grad)
    up_first = up.send_first((low_u, high_u))
    down_got = across(down_send, CORE)
    qkv_grad, qv_sums = attention_backward(qkv, ctx_grad, segment_ids)
    low_u, high_u, down_got, qkv_grad, qv_sums = together(*up_first, down_got, qkv_grad, qv_sums)
    down = Reduction(down_keep, down_got)
    low_u, high_u, low_d, high_d, qv_sums = together(*up.second((low_u, high_u)), *down.first(), qv_sums)
    up_second = up.send_second((low_u, high_u))
    down_first = down.send_first((low_d, high_d))
    qkv_keep, qkv_send = weight_gradient(
        qkv_gradient_kernel,
        "qkv_gradient",
        place,
        3 * unit + SMALL,
        3,
        (x, qkv_grad, qv_sums),
        [
            resident((tokens, width)),
            pl.BlockSpec((tokens, width), lambda i, *_: (0, i)),
            resident(qv_sums.shape),
        ],
        6 * tokens * width * width,
        (pltpu.VMEM((width, tokens), BF16),),
    )
    low_u, high_u, low_d, high_d, qkv_keep, qkv_send = together(*up_second, *down_first, qkv_keep, qkv_send)
    u1, u2, u3, low_d, high_d, qkv_send, qkv_grad = together(
        *up.third((low_u, high_u)), *down.second((low_d, high_d)), qkv_send, qkv_grad
    )
    up_third = up.send_third((u1, u2, u3))
    down_second = down.send_second((low_d, high_d))
    qkv_got = across(qkv_send, CORE)
    grad_input = input_gradient(first_grad, qkv_grad, qkv_matrix, (0, 1, 4))
    low_d, high_d, u1, u3, qkv_got, grad_input = together(
        *down_second, up_third[0], up_third[2], qkv_got, grad_input
    )
    qkv_sum = Reduction(qkv_keep, qkv_got)
    d1, d2, d3, low_q, high_q, grad_input = together(*down.third((low_d, high_d)), *qkv_sum.first(), grad_input)
    qkv_first = qkv_sum.send_first((low_q, high_q))
    grad_input = input_gradient(first_grad, qkv_grad, qkv_matrix, (1, 3, 4), (grad_input,))
    low_q, high_q, u2, grad_input = together(*qkv_first, up_third[1], grad_input)
    low_q, high_q, d1, d2, d3, grad_input = together(*qkv_sum.second((low_q, high_q)), d1, d2, d3, grad_input)
    qkv_second = qkv_sum.send_second((low_q, high_q))
    down_third = down.send_third((d1, d2, d3))
    up_total = up.finish((u1, u2, u3))
    up_part, up_small = up_total[: (ratio + 1) * unit], up_total[(ratio + 1) * unit :]
    grad_input = input_gradient(first_grad, qkv_grad, qkv_matrix, (3, 4, 4), (grad_input,))
    low_q, high_q, grad_input = together(*qkv_second, grad_input)
    qkv_third = together(*qkv_sum.third((low_q, high_q)), up_part)
    up_part = qkv_third[-1]
    qkv_third = qkv_sum.send_third(qkv_third[:-1])
    up_theirs = across(up_part.astype(BF16), Y)
    up_low, up_high = both_halves(up_part, up_theirs, y)
    grad_up = join_columns((up_low[: ratio * unit], up_high[: ratio * unit]), unit, ratio)
    grad_out = join_columns((up_low[ratio * unit :], up_high[ratio * unit :]), unit, 1)
    down_total = down.finish(down_third)
    *qkv_third, down_total, grad_up, grad_out = together(*qkv_third, down_total, grad_up, grad_out)
    qkv_total = qkv_sum.finish(qkv_third)
    qkv_part, qkv_small = qkv_total[: 3 * unit], qkv_total[3 * unit :]
    theirs = across(jnp.concatenate([qkv_part, down_total], axis=0).astype(BF16), Y)
    qkv_theirs, down_theirs = theirs[: 3 * unit], theirs[3 * unit :]
    grad_down = jnp.concatenate(both_halves(down_total, down_theirs, y), axis=1)
    grad_qkv = join_columns(both_halves(qkv_part, qkv_theirs, y), unit, 3)
    return (
        pooled,
        grad_input.reshape(row_count, length, width),
        grad_qkv,
        qkv_small[0, : 2 * unit],
        grad_out,
        up_small[0, :unit],
        up_small[1, :unit],
        up_small[2, :unit],
        grad_up,
        up_small[6, : ratio * unit],
        grad_down,
        up_small[3, :unit],
        up_small[4, :unit],
        up_small[5, :unit],
    )


def body_by_collectives(
    hidden_in,
    segment_ids,
    pooled_grad,
    qkv_weight,
    qv_bias,
    out_weight,
    out_bias,
    first_gain,
    first_shift,
    up_weight,
    up_bias,
    down_weight,
    down_bias,
    second_gain,
    second_shift,
):
    row_count, length, width = hidden_in.shape
    x = hidden_in.reshape(row_count * length, width)

    def gather(shard):
        return lax.all_gather(shard, "fsdp", axis=0, tiled=True)

    small = jnp.concatenate(
        [qv_bias, out_bias, first_gain, first_shift, up_bias, down_bias, second_gain, second_shift]
    ).astype(BF16)
    small = lax.all_gather(small, "fsdp", axis=0, tiled=False).astype(F32)
    unit = out_bias.shape[0]
    ends = [0]
    for part in (qv_bias, out_bias, first_gain, first_shift, up_bias, down_bias, second_gain, second_shift):
        ends.append(ends[-1] + part.shape[0])
    qv, ob, g1, s1, ub, db, g2, s2 = (small[:, a:b].reshape(1, -1) for a, b in zip(ends[:-1], ends[1:]))
    zeros = jnp.zeros((1, width), F32)
    vectors = jnp.concatenate([ob, g1, s1, db, g2, s2, zeros, zeros], axis=0)
    qkv_bias = jnp.concatenate([qv[:, :width], zeros, qv[:, width:]], axis=1)
    qkv_matrix = gather(qkv_weight)
    out_matrix = gather(out_weight)
    up_matrix = gather(up_weight)
    down_matrix = gather(down_weight)
    qkv, ctx = attention_forward(x, segment_ids, (qkv_matrix, qkv_bias))
    pooled, active, hidden_grad, normed, branch, first_grad, attended, ctx_grad, sums, up_sums = feedforward(
        x, ctx, segment_ids, pooled_grad, (out_matrix, up_matrix, down_matrix, vectors, ub), up_matrix.shape[1]
    )

    def scatter(grad):
        return lax.psum_scatter(grad.astype(BF16), "fsdp", scatter_dimension=0, tiled=True)

    grad_down = scatter(transpose_times(active, branch))
    grad_up = scatter(transpose_times(normed, hidden_grad))
    grad_out = scatter(transpose_times(ctx, attended))
    qkv_grad, qv_sums = attention_backward(qkv, ctx_grad, segment_ids)
    grad_qkv = scatter(transpose_times(x, qkv_grad))
    grad_input = first_grad + times_transpose(qkv_grad, qkv_matrix)
    grad_qkv, grad_out, grad_up, grad_down = lax.psum(
        tuple(g.astype(F32) for g in (grad_qkv, grad_out, grad_up, grad_down)), "dp"
    )
    sums = jnp.sum(sums.reshape(6, 8, width), axis=1)
    vector_sums = jnp.concatenate(
        [jnp.sum(qv_sums, axis=0), sums.reshape(-1), jnp.sum(up_sums, axis=0)]
    )
    vector_sums = lax.psum(vector_sums, ("dp", "fsdp"))
    me = lax.axis_index("fsdp")

    def mine(start, size):
        return lax.dynamic_slice(vector_sums, (start + me * size,), (size,))

    at = 2 * width
    return (
        pooled,
        grad_input.reshape(row_count, length, width),
        grad_qkv,
        mine(0, 2 * unit),
        grad_out,
        mine(at, unit),
        mine(at + width, unit),
        mine(at + 2 * width, unit),
        grad_up,
        mine(at + 6 * width, up_bias.shape[0]),
        grad_down,
        mine(at + 3 * width, unit),
        mine(at + 4 * width, unit),
        mine(at + 5 * width, unit),
    )


def solution(mesh):
    rows = ("dp", "fsdp")
    in_specs = (P(rows, None, None), P(rows, None), P(rows, None, None)) + (
        P("fsdp", None),
        P("fsdp"),
        P("fsdp", None),
        P("fsdp"),
        P("fsdp"),
        P("fsdp"),
        P("fsdp", None),
        P("fsdp"),
        P("fsdp", None),
        P("fsdp"),
        P("fsdp"),
        P("fsdp"),
    )
    out_specs = (
        P(rows, None, None),
        P(rows, None, None),
        P("fsdp", None),
        P("fsdp"),
        P("fsdp", None),
        P("fsdp"),
        P("fsdp"),
        P("fsdp"),
        P("fsdp", None),
        P("fsdp"),
        P("fsdp", None),
        P("fsdp"),
        P("fsdp"),
        P("fsdp"),
    )
    body = body_by_permutes if dict(mesh.shape) == {"dp": 2, "fsdp": 16} else body_by_collectives
    return jax.shard_map(body, mesh=mesh, in_specs=in_specs, out_specs=out_specs, check_vma=False)
```
